256 devices in a mesh: dp: 64 (over z, y, core), mp: 4 (over x).
Axes of the slice: x: 4, y: 4, z: 8, core: 2. Of those that a mesh axis runs over, the one named last changes fastest.
Arguments:
- weights: bfloat16 [14336, 8, 128], P('mp'), may hold values from -0.1875 to 0.1875
- hidden: bfloat16 [16384, 14336], P('dp', 'mp'), may hold values from -6 to 6
- cotangent: bfloat16 [16384, 8192], P('dp', 'mp'), may hold values from -6 to 6
- sketch: float32 [128, 8192], P(None, ('dp', 'mp')), may hold values from -0.046875 to 0.046875
- projection: float32 [128, 4, 3584], P(None, 'mp', 'dp'), may hold values from -0.046875 to 0.046875
- pattern: int32 [112, 8], P('mp'), may hold values from 0 to 63, as said below
Outputs:
- input_grad: bfloat16 [16384, 14336], P('dp', 'mp')
- direction: float32 [4, 3584, 8, 128], P('mp', 'dp')
The draws below stay inside these ranges and needn't reach their ends.
Inputs may be any that keep to these rules, and one draw needn't show every extreme that they name: `pattern`: each block row names 8 different column blocks.
All inputs are finite; a program needn't handle non-finite values.
Results may differ from the reference program's by a relative error of at most 0.001.
Values may be sent and summed in bfloat16 or wider, within the bound.
A program may use at most 192 MiB of HBM per device.

```python
import math
import jax
import jax.numpy as jnp
from jax import lax

D = 8192
FFW = 14336
BLK = 128
KB = 8
RANK = 128
NS_STEPS = 5
TOKENS = 16384
HBLK = 112
N_MP = 4


def draw_pattern(key, part):
    row_keys = jax.random.split(key, HBLK)

    def one_row(row_key):
        return jax.random.permutation(row_key, D // BLK)[:KB]
    return jax.vmap(one_row)(row_keys).astype(jnp.int32)


def steps_of(key, dims, cuts, smallest, high):
    def one(position, parts):
        draws = jax.random.uniform(jax.random.fold_in(jax.random.fold_in(key, 6), position), (parts,), jnp.float32, smallest / len(cuts), high / len(cuts))
        return jnp.repeat(jnp.exp(draws), dims[position] // parts).reshape((-1,) + (1,) * (len(dims) - position - 1))

    loudness = one(*cuts[0])
    for cut in cuts[1:]:
        loudness = loudness * one(*cut)
    return loudness


def bell_draw(key, shape, width, bound, cuts=(), kind=jnp.bfloat16):
    level = steps_of(key, shape, cuts, -0.22, 0.18) if cuts else 1.0
    entries = jax.random.normal(key, shape, jnp.float32) * width * level
    return jnp.minimum(jnp.maximum(entries, -bound), bound).astype(kind)


def setup_inputs(seed: int = 0) -> dict:
    seeds = jax.random.split(jax.random.key(seed), 7)
    return {
        "weights": bell_draw(seeds[0], (FFW, KB, BLK), (KB * BLK) ** -0.5, 0.1875, ((0, 4),)),
        "hidden": bell_draw(seeds[1], (TOKENS, FFW), 1.0, 6.0, ((0, 64), (1, 4))),
        "cotangent": bell_draw(seeds[2], (TOKENS, D), 1.0, 6.0, ((0, 64), (1, 4))),
        "sketch": bell_draw(seeds[3], (RANK, D), 0.003, 0.046875, ((1, 256),), jnp.float32),
        "projection": bell_draw(seeds[4], (RANK, N_MP, FFW // N_MP), FFW ** -0.5, 0.046875, ((1, 4), (2, 64)), jnp.float32),
        "pattern": draw_pattern(jax.random.fold_in(seeds[6], 71), 0),
    }


shift_eps = 0.0001

def matmul(operand_a, operand_b):
    return jnp.dot(operand_a.astype(jnp.float32), operand_b.astype(jnp.float32), precision=lax.Precision.HIGHEST, preferred_element_type=jnp.float32)

def root_factor(gram):
    identity = jnp.eye(gram.shape[0], dtype=jnp.float32)
    shifted = gram + shift_eps * identity
    frobenius = jnp.sqrt(jnp.sum(shifted * shifted))
    root_iter = shifted / frobenius
    inverse_iter = identity
    for iteration in range(NS_STEPS):
        middle = 0.5 * (3.0 * identity - matmul(inverse_iter, root_iter))
        root_iter = matmul(root_iter, middle)
        inverse_iter = matmul(middle, inverse_iter)
    shifted_root = 0.5 * jnp.sqrt(frobenius) * (root_iter + root_iter.T) + math.sqrt(shift_eps) * identity
    factor = jnp.linalg.cholesky(shifted_root)
    solved = jax.scipy.linalg.cho_solve((factor, True), inverse_iter.T)
    return -solved.T / (math.sqrt(shift_eps) * jnp.sqrt(frobenius))

def reference(weights, hidden, cotangent, sketch, projection, pattern):
    all_tokens = hidden.shape[0]
    cot_blocks = cotangent.reshape(all_tokens, D // BLK, BLK)
    proj_full = projection.reshape(RANK, FFW)
    highest = lax.Precision.HIGHEST

    def grad_row(carry, index):
        cols_row = pattern[index]
        chosen = jnp.take(cot_blocks, cols_row, axis=1).astype(jnp.float32)
        hid_row = lax.dynamic_slice_in_dim(hidden, index * BLK, BLK, 1).astype(jnp.float32)
        weight_row = lax.dynamic_slice_in_dim(weights, index * BLK, BLK, 0).astype(jnp.float32)
        grad_block = jnp.einsum('ti,tkn->ikn', hid_row, chosen, precision=highest) / all_tokens
        back_row = jnp.einsum('tkn,ikn->ti', chosen, weight_row, precision=highest).astype(jnp.bfloat16)
        proj_row = lax.dynamic_slice_in_dim(proj_full, index * BLK, BLK, 1)
        contrib = jnp.einsum('mi,ikn->mkn', proj_row, grad_block, precision=highest)
        carry = carry.at[:, cols_row, :].add(contrib)
        return (carry, (grad_block, back_row))
    start = jnp.zeros((RANK, D // BLK, BLK), jnp.float32)
    compressed, (grads, backs) = lax.scan(grad_row, start, jnp.arange(HBLK, dtype=jnp.int32))
    input_grad = jnp.transpose(backs, (1, 0, 2)).reshape(all_tokens, FFW)
    stacked = jnp.concatenate([sketch, compressed.reshape(RANK, D)], axis=0)
    gram = matmul(stacked, stacked.T)
    mixing = root_factor(gram)
    stacked_blocks = stacked.reshape(2 * RANK, D // BLK, BLK)

    def direction_row(index):
        grad_block = grads[index]
        selected = jnp.take(stacked_blocks, pattern[index], axis=1)
        projected = jnp.einsum('ikn,mkn->im', grad_block, selected, precision=highest)
        mixed = matmul(projected, mixing)
        return grad_block / math.sqrt(shift_eps) + jnp.einsum('im,mkn->ikn', mixed, selected, precision=highest)
    direction = lax.map(direction_row, jnp.arange(HBLK, dtype=jnp.int32))
    return (input_grad, direction.reshape(N_MP, FFW // N_MP, KB, BLK))
```

```python
import functools
import math

import jax
import jax.numpy as jnp
from jax import lax
from jax.experimental import pallas as pl
from jax.experimental.pallas import tpu as pltpu
from jax.sharding import PartitionSpec as P

NS_STEPS = 5
EPS = 0.0001
F32 = jnp.float32
BF16 = jnp.bfloat16
MIB = 1 << 20


def split_bf16(value):
    high = value.astype(BF16)
    low = (value - high.astype(F32)).astype(BF16)
    return high, low


def exact_dot(left, right, dims):
    return lax.dot_general(
        left, right, (dims, ((), ())), precision=lax.Precision.HIGHEST, preferred_element_type=F32
    )


def local_kernel(inv_tokens, pat_ref, cot_ref, hid_ref, wgt_ref, proj_ref, back_ref, grad_ref, comp_ref, z_ref):
    step = pl.program_id(0)
    slots = wgt_ref.shape[0]
    blk = hid_ref.shape[1]
    per_part = cot_ref.shape[2] // blk
    col_blocks = cot_ref.shape[0] * per_part

    def cot_block(col):
        lane = pl.multiple_of(lax.rem(col, per_part) * blk, blk)
        return cot_ref[lax.div(col, per_part), :, pl.ds(lane, blk)]

    @pl.when(step == 0)
    def _():
        @pl.loop(0, col_blocks)
        def _(col):
            z_ref[col] = jnp.zeros(z_ref.shape[1:], F32)

    cols = [pat_ref[step, k] for k in range(slots)]
    chosen = jnp.concatenate([cot_block(col) for col in cols], axis=1)
    weight = jnp.concatenate([wgt_ref[k] for k in range(slots)], axis=1)
    back = lax.dot_general(chosen, weight, (((1,), (1,)), ((), ())), preferred_element_type=F32)
    back_ref[...] = back.astype(BF16)
    hid = hid_ref[...]
    grad = lax.dot_general(hid, chosen, (((0,), (0,)), ((), ())), preferred_element_type=F32)
    grad = grad * inv_tokens
    for k in range(slots):
        grad_ref[k] = grad[:, k * blk : (k + 1) * blk]
    high, low = split_bf16(proj_ref[...])
    both = jnp.dot(hid, jnp.concatenate([high, low], axis=1), preferred_element_type=F32)
    rank = proj_ref.shape[1]
    y = both[:, :rank] + both[:, rank:]
    for col in cols:
        z_ref[col] += y

    @pl.when(step == pl.num_programs(0) - 1)
    def _():
        @pl.loop(0, col_blocks)
        def _(col):
            zh, zl = split_bf16(z_ref[col])
            out = lax.dot_general(
                cot_block(col),
                jnp.concatenate([zh, zl], axis=1),
                (((0,), (0,)), ((), ())),
                preferred_element_type=F32,
            )
            comp_ref[col] = (out[:, :rank] + out[:, rank:]) * inv_tokens


def local_step(pattern, cot, hidden, weights, proj, all_tokens):
    parts, tokens, part_cols = cot.shape
    block_rows, slots = pattern.shape
    blk = weights.shape[2]
    rows = hidden.shape[1]
    rank = proj.shape[1]
    col_blocks = parts * part_cols // blk
    grid_spec = pltpu.PrefetchScalarGridSpec(
        num_scalar_prefetch=1,
        grid=(block_rows,),
        in_specs=[
            pl.BlockSpec((parts, tokens, part_cols), lambda r, pat: (0, 0, 0), pipeline_mode=pl.Buffered(1)),
            pl.BlockSpec((tokens, blk), lambda r, pat: (0, r)),
            pl.BlockSpec((slots, blk, blk), lambda r, pat: (0, r, 0)),
            pl.BlockSpec((blk, rank), lambda r, pat: (r, 0)),
        ],
        out_specs=[
            pl.BlockSpec((tokens, blk), lambda r, pat: (0, r)),
            pl.BlockSpec((slots, blk, blk), lambda r, pat: (0, r, 0)),
            pl.BlockSpec((col_blocks, blk, rank), lambda r, pat: (0, 0, 0), pipeline_mode=pl.Buffered(1)),
        ],
        scratch_shapes=[pltpu.VMEM((col_blocks, tokens, rank), F32)],
    )
    return pl.pallas_call(
        functools.partial(local_kernel, 1.0 / all_tokens),
        grid_spec=grid_spec,
        out_shape=(
            jax.ShapeDtypeStruct((tokens, rows), BF16),
            jax.ShapeDtypeStruct((slots, rows, blk), F32),
            jax.ShapeDtypeStruct((col_blocks, blk, rank), F32),
        ),
        compiler_params=pltpu.CompilerParams(vmem_limit_bytes=48 * MIB),
        cost_estimate=pl.CostEstimate(flops=6_000_000_000, bytes_accessed=36_000_000, transcendentals=0),
        name="local_step",
    )(pattern, cot, hidden, weights, proj)


def identity(n):
    rows = lax.broadcasted_iota(jnp.int32, (n, n), 0)
    cols = lax.broadcasted_iota(jnp.int32, (n, n), 1)
    return jnp.where(rows == cols, 1.0, 0.0).astype(F32)


def mul(left, right):
    return exact_dot(left, right, ((1,), (0,)))


def spd_inverse(mat, eye):
    n = mat.shape[0]
    bound = jnp.max(jnp.sum(jnp.abs(mat), axis=1, keepdims=True))
    start = eye * (2.0 / (bound + math.sqrt(EPS)))

    def unfinished(state):
        count, previous, residual, _ = state
        return (count < 100) & (residual > 2e-6) & ((residual < 0.5 * previous) | (residual > 0.1))

    def body(state):
        count, _, residual, guess = state
        gap = eye - mul(mat, guess)
        guess = guess + mul(guess, gap)
        return count + 1, residual, jnp.max(jnp.abs(gap)), guess

    state = lax.while_loop(unfinished, body, (0, jnp.float32(4.0), jnp.float32(2.0), start))
    return state[3]


def mixing_of(gram):
    n = gram.shape[0]
    eye = identity(n)
    shifted = gram + EPS * eye
    total = jnp.sum(jnp.sum(shifted * shifted, axis=1, keepdims=True), axis=0, keepdims=True)
    frob = jnp.sqrt(total)
    root = shifted / frob
    middle = 1.5 * eye - 0.5 * root
    root = mul(root, middle)
    inverse = middle
    for _ in range(NS_STEPS - 1):
        middle = 1.5 * eye - 0.5 * mul(inverse, root)
        root = mul(root, middle)
        inverse = mul(middle, inverse)
    half = 0.5 * jnp.sqrt(frob) * (root + root.T) + math.sqrt(EPS) * eye
    half_inv = spd_inverse(half, eye)
    return -mul(inverse, half_inv) / (math.sqrt(EPS) * jnp.sqrt(frob))


def finish_kernel(row_ref, pat_ref, grad_ref, sketch_ref, comp_ref, out_ref, gram_ref, sel_ref):
    slots, rows, blk = grad_ref.shape
    rank = comp_ref.shape[1]
    width = comp_ref.shape[0]
    chunk = 1024
    gram_ref[...] = jnp.zeros_like(gram_ref)

    @pl.loop(0, width // chunk)
    def _(i):
        at = pl.ds(pl.multiple_of(i * chunk, chunk), chunk)
        st = jnp.concatenate([sketch_ref[at, :], comp_ref[at, :]], axis=1)
        high, low = split_bf16(st)
        dims = (((0,), (0,)), ((), ()))
        gram_ref[0] += lax.dot_general(high, high, dims, preferred_element_type=F32)
        gram_ref[1] += lax.dot_general(high, low, dims, preferred_element_type=F32)

    cross = gram_ref[1]
    mixing = mixing_of(gram_ref[0] + (cross + cross.T))
    start = row_ref[0]
    first = lax.div(start, blk)
    last = pat_ref.shape[0] - 1
    grad = jnp.concatenate([grad_ref[k] for k in range(slots)], axis=1)
    block_of = lax.div(start + lax.broadcasted_iota(jnp.int32, (rows, 1), 0), blk)
    projected = None
    for g in range(2):
        brow = jnp.minimum(first + g, last)
        for k in range(slots):
            col = pl.multiple_of(pat_ref[brow, k] * blk, blk)
            here = pl.ds(k * blk, blk)
            sel_ref[g, here, :rank] = sketch_ref[pl.ds(col, blk), :]
            sel_ref[g, here, rank:] = comp_ref[pl.ds(col, blk), :]
        part = mul(grad, sel_ref[g])
        projected = part if projected is None else jnp.where(block_of == first + g, part, projected)
    mixed = mul(projected, mixing)
    corr = exact_dot(mixed, sel_ref[0], ((1,), (1,)))
    corr1 = exact_dot(mixed, sel_ref[1], ((1,), (1,)))
    corr = jnp.where(block_of == first + 1, corr1, corr)
    result = grad * (1.0 / math.sqrt(EPS)) + corr
    for k in range(slots):
        out_ref[:, k, :] = result[:, k * blk : (k + 1) * blk]


def finish(start_row, pattern, grad, sketch_t, comp_t):
    slots, rows, blk = grad.shape
    rank = comp_t.shape[1]
    smem = pl.BlockSpec(memory_space=pltpu.SMEM)
    vmem = pl.BlockSpec(memory_space=pltpu.VMEM)
    return pl.pallas_call(
        finish_kernel,
        in_specs=[smem, smem, vmem, vmem, vmem],
        out_specs=vmem,
        out_shape=jax.ShapeDtypeStruct((rows, slots, blk), F32),
        scratch_shapes=[
            pltpu.VMEM((2, 2 * rank, 2 * rank), F32),
            pltpu.VMEM((2, slots * blk, 2 * rank), F32),
        ],
        compiler_params=pltpu.CompilerParams(vmem_limit_bytes=40 * MIB),
        cost_estimate=pl.CostEstimate(flops=5_000_000_000, bytes_accessed=9_000_000, transcendentals=0),
        name="finish",
    )(start_row, pattern, grad, sketch_t, comp_t)


def per_device(weights, hidden, cotangent, sketch, projection, pattern):
    rank = sketch.shape[0]
    slots, blk = weights.shape[1:]
    dp_size = lax.axis_size("dp")
    dev_rows = weights.shape[0] // dp_size
    all_tokens = hidden.shape[0] * dp_size
    cot = lax.all_gather(cotangent, "mp")
    proj = lax.all_gather(projection.reshape(rank, dev_rows).T, "dp", tiled=True)
    sketch_t = lax.all_gather(sketch.T, ("dp", "mp"), tiled=True)
    weights_t = weights.transpose(1, 0, 2)
    input_grad, grad, comp = local_step(pattern, cot, hidden, weights_t, proj, all_tokens)
    comp = comp.reshape(-1, rank)
    comp_piece = lax.psum_scatter(comp, ("dp", "mp"), scatter_dimension=0, tiled=True)
    comp_t = lax.all_gather(comp_piece, ("dp", "mp"), tiled=True)
    grad = lax.psum_scatter(grad, "dp", scatter_dimension=1, tiled=True)
    start_row = (lax.axis_index("dp") * dev_rows).reshape(1).astype(jnp.int32)
    direction = finish(start_row, pattern, grad, sketch_t, comp_t)
    return input_grad, direction[None]


def solution(mesh):
    return jax.shard_map(
        per_device,
        mesh=mesh,
        in_specs=(
            P("mp", None, None),
            P("dp", "mp"),
            P("dp", "mp"),
            P(None, ("dp", "mp")),
            P(None, "mp", "dp"),
            P("mp", None),
        ),
        out_specs=(P("dp", "mp"), P("mp", "dp", None, None)),
        check_vma=False,
    )
```

```python
import functools
import math

import jax
import jax.numpy as jnp
from jax import lax
from jax.experimental import pallas as pl
from jax.experimental.pallas import tpu as pltpu
from jax.sharding import PartitionSpec as P

NS_STEPS = 5
EPS = 0.0001
F32 = jnp.float32
BF16 = jnp.bfloat16
MIB = 1 << 20


def split_bf16(value):
    high = value.astype(BF16)
    low = (value - high.astype(F32)).astype(BF16)
    return high, low


def exact_dot(left, right, dims):
    return lax.dot_general(
        left, right, (dims, ((), ())), precision=lax.Precision.HIGHEST, preferred_element_type=F32
    )


def local_kernel(inv_tokens, core_ref, pat_ref, cot_ref, hid_ref, wgt_ref, proj_ref, back_ref, grad_ref, comp_ref, z_ref):
    step = pl.program_id(0)
    core = core_ref[0]
    slots = wgt_ref.shape[0]
    mine = slots // 2
    blk = hid_ref.shape[1]
    rank = proj_ref.shape[1]
    tokens = back_ref.shape[0]
    per_part = cot_ref.shape[2] // blk
    half_blocks = z_ref.shape[0]
    own = pl.ds(pl.multiple_of(core * tokens, tokens), tokens)

    def cot_block(col, rows=slice(None)):
        lane = pl.multiple_of(lax.rem(col, per_part) * blk, blk)
        return cot_ref[lax.div(col, per_part), rows, pl.ds(lane, blk)]

    @pl.when(step == 0)
    def _():
        @pl.loop(0, half_blocks)
        def _(i):
            z_ref[i] = jnp.zeros(z_ref.shape[1:], F32)

    cols = [pat_ref[step, k] for k in range(slots)]
    chosen = jnp.concatenate([cot_block(col, own) for col in cols], axis=1)
    weight = jnp.concatenate([wgt_ref[k] for k in range(slots)], axis=1)
    back = lax.dot_general(chosen, weight, (((1,), (1,)), ((), ())), preferred_element_type=F32)
    back_ref[...] = back.astype(BF16)
    hid = hid_ref[...]
    wide = jnp.concatenate([cot_block(pat_ref[step, mine * core + j]) for j in range(mine)], axis=1)
    grad = lax.dot_general(hid, wide, (((0,), (0,)), ((), ())), preferred_element_type=F32)
    grad = grad * inv_tokens
    for j in range(mine):
        grad_ref[j] = grad[:, j * blk : (j + 1) * blk]
    high, low = split_bf16(proj_ref[...])
    both = jnp.dot(hid, jnp.concatenate([high, low], axis=1), preferred_element_type=F32)
    y = both[:, :rank] + both[:, rank:]
    for col in cols:

        @pl.when(lax.rem(col, 2) == core)
        def _(col=col):
            z_ref[lax.div(col, 2)] += y

    @pl.when(step == pl.num_programs(0) - 1)
    def _():
        @pl.loop(0, half_blocks)
        def _(i):
            zh, zl = split_bf16(z_ref[i])
            out = lax.dot_general(
                cot_block(2 * i + core),
                jnp.concatenate([zh, zl], axis=1),
                (((0,), (0,)), ((), ())),
                preferred_element_type=F32,
            )
            comp_ref[i] = (out[:, :rank] + out[:, rank:]) * inv_tokens


def local_step(core, pattern, cot, hidden, weights, proj, all_tokens):
    parts, wide_tokens, part_cols = cot.shape
    tokens = wide_tokens // 2
    block_rows, slots = pattern.shape
    blk = weights.shape[2]
    rows = hidden.shape[1]
    rank = proj.shape[1]
    half_blocks = parts * part_cols // blk // 2
    grid_spec = pltpu.PrefetchScalarGridSpec(
        num_scalar_prefetch=2,
        grid=(block_rows,),
        in_specs=[
            pl.BlockSpec((parts, wide_tokens, part_cols), lambda r, *_: (0, 0, 0), pipeline_mode=pl.Buffered(1)),
            pl.BlockSpec((wide_tokens, blk), lambda r, *_: (0, r)),
            pl.BlockSpec((slots, blk, blk), lambda r, *_: (0, r, 0)),
            pl.BlockSpec((blk, rank), lambda r, *_: (r, 0)),
        ],
        out_specs=[
            pl.BlockSpec((tokens, blk), lambda r, *_: (0, r)),
            pl.BlockSpec((slots // 2, blk, blk), lambda r, *_: (0, r, 0)),
            pl.BlockSpec((half_blocks, blk, rank), lambda r, *_: (0, 0, 0), pipeline_mode=pl.Buffered(1)),
        ],
        scratch_shapes=[pltpu.VMEM((half_blocks, wide_tokens, rank), F32)],
    )
    return pl.pallas_call(
        functools.partial(local_kernel, 1.0 / all_tokens),
        grid_spec=grid_spec,
        out_shape=(
            jax.ShapeDtypeStruct((tokens, rows), BF16),
            jax.ShapeDtypeStruct((slots // 2, rows, blk), F32),
            jax.ShapeDtypeStruct((half_blocks, blk, rank), F32),
        ),
        compiler_params=pltpu.CompilerParams(vmem_limit_bytes=48 * MIB),
        cost_estimate=pl.CostEstimate(flops=6_000_000_000, bytes_accessed=36_000_000, transcendentals=0),
        name="local_step",
    )(core, pattern, cot, hidden, weights, proj)


class Wires:
    def __init__(self, send_sems, recv_sems, local_sems):
        self.send_sems, self.recv_sems, self.local_sems = send_sems, recv_sems, local_sems
        self.used = 0
        self.locals = 0
        self.sent = []

    def send(self, source, target, device):
        copy = pltpu.make_async_remote_copy(
            src_ref=source,
            dst_ref=target,
            send_sem=self.send_sems.at[self.used],
            recv_sem=self.recv_sems.at[self.used],
            device_id=device,
            device_id_type=pl.DeviceIdType.MESH,
        )
        self.used += 1
        copy.start()
        self.sent.append(copy)
        return copy

    def keep(self, source, target):
        copy = pltpu.make_async_copy(source, target, self.local_sems.at[self.locals])
        self.locals += 1
        copy.start()
        return copy

    def drain(self):
        for copy in self.sent:
            copy.wait_send()


def received(*copies):
    for copy in copies:
        copy.wait_recv()


class Place:
    def __init__(self, ny, nz, nx):
        self.n = {"x": nx, "y": ny, "z": nz, "c": 2}
        d = lax.axis_index("dp")
        self.at = {
            "x": lax.axis_index("mp"),
            "c": lax.rem(d, 2),
            "y": lax.rem(lax.div(d, 2), ny),
            "z": lax.div(d, 2 * ny),
        }

    def shift(self, axis, by):
        n = self.n[axis]
        return lax.rem(self.at[axis] + (by % n), n)

    def device(self, axis, by):
        at = dict(self.at)
        at[axis] = self.shift(axis, by)
        return ((at["z"] * self.n["y"] + at["y"]) * 2 + at["c"], at["x"])


def meet(devices):
    barrier = pltpu.get_barrier_semaphore()
    for device in devices:
        pl.semaphore_signal(barrier, inc=1, device_id=device, device_id_type=pl.DeviceIdType.MESH)
    pl.semaphore_wait(barrier, len(devices))


def gather_kernel(ny, nz, nx, cot, hid, proj, sk, cot_o, hid_o, proj_o, sk_o, send_sems, recv_sems, local_sems):
    here = Place(ny, nz, nx)
    x, y, z, c = (here.at[name] for name in "xyzc")
    wires = Wires(send_sems, recv_sems, local_sems)
    partners = [here.device("x", j) for j in range(1, nx)] + [here.device("y", j) for j in range(1, ny)]
    partners += [here.device("z", 1), here.device("z", -1), here.device("c", 1)]
    sib = here.device("c", 1)
    keep_sk = wires.keep(sk, sk_o.at[z, y, c, x])
    keep_proj = wires.keep(proj, proj_o.at[z, y, c])
    keep_cot = wires.keep(cot, cot_o.at[x, c])
    keep_hid = wires.keep(hid, hid_o.at[c])
    meet(partners)
    rows = cot.shape[0] // 2
    top, bottom = pl.ds(0, rows), pl.ds(rows, rows)
    sk_x = [wires.send(sk, sk_o.at[z, y, c, x], here.device("x", j)) for j in range(1, nx)]
    proj_y = [wires.send(proj, proj_o.at[z, y, c], here.device("y", j)) for j in range(1, ny)]
    right, left = here.device("x", 1), here.device("x", -1)

    def cot_send(rows_at, device):
        return wires.send(cot.at[rows_at], cot_o.at[x, c, rows_at], device)

    def cot_pass(part, rows_at, device):
        return wires.send(cot_o.at[part, c, rows_at], cot_o.at[part, c, rows_at], device)

    r_top, l_bottom = cot_send(top, right), cot_send(bottom, left)
    r_bottom, l_top = cot_send(bottom, right), cot_send(top, left)
    from_sib = [wires.send(hid, hid_o.at[c], sib), wires.send(cot, cot_o.at[x, c], sib)]

    keep_sk.wait()
    received(*sk_x)
    sk_y = [
        wires.send(sk_o.at[z, y, c], sk_o.at[z, y, c], here.device("y", j)) for j in range(1, ny)
    ]
    keep_proj.wait()
    received(*proj_y)

    up, down = here.device("z", 1), here.device("z", -1)

    def z_pass(ref, layer, device, ys=slice(None)):
        view = ref.at[layer, ys, c]
        return wires.send(view, view, device)

    arrays = (proj_o, sk_o)
    low, high = pl.ds(0, ny // 2), pl.ds(ny // 2, ny // 2)
    going_up, going_down = [z_pass(proj_o, z, up)], [z_pass(proj_o, z, down)]
    from_sib.append(z_pass(proj_o, z, sib))
    received(*sk_y)
    going_up.append(z_pass(sk_o, z, up))
    going_down.append(z_pass(sk_o, z, down))
    from_sib.append(z_pass(sk_o, z, sib))

    def z_step(distance, going_up, going_down):
        below, above = here.shift("z", -distance), here.shift("z", distance)
        next_up, next_down = [], []
        last = distance == nz // 2
        for moved, layer, device, part, nexts in (
            (going_up, below, up, low, next_up),
            (going_down, above, down, high, next_down),
        ):
            for copy, ref in zip(moved, arrays):
                received(copy)
                if not last:
                    ys = part if distance + 1 == nz // 2 else slice(None)
                    nexts.append(z_pass(ref, layer, device, ys))
                from_sib.append(z_pass(ref, layer, sib, part if last else slice(None)))
        return next_up, next_down

    left_part, right_part, far_part = here.shift("x", -1), here.shift("x", 1), here.shift("x", 2)

    def cot_first():
        received(r_top)
        far_top = cot_pass(left_part, top, right)
        from_sib.append(cot_pass(left_part, top, sib))
        received(l_bottom)
        far_bottom = cot_pass(right_part, bottom, left)
        from_sib.append(cot_pass(right_part, bottom, sib))
        return far_top, far_bottom

    for distance in range(1, nz // 2 + 1):
        if distance == 2:
            far_top, far_bottom = cot_first()
        if distance == 3:
            received(r_bottom)
            from_sib.append(cot_pass(left_part, bottom, sib))
            received(l_top)
            from_sib.append(cot_pass(right_part, top, sib))
        going_up, going_down = z_step(distance, going_up, going_down)
    received(far_top)
    from_sib.append(cot_pass(far_part, top, sib))
    received(far_bottom)
    from_sib.append(cot_pass(far_part, bottom, sib))
    keep_cot.wait()
    keep_hid.wait()
    received(*from_sib)
    wires.drain()


def gather(ny, nz, nx, cot, hid, proj, sk):
    any_spec = pl.BlockSpec(memory_space=pl.ANY)
    copies = 80
    return pl.pallas_call(
        functools.partial(gather_kernel, ny, nz, nx),
        in_specs=[any_spec] * 4,
        out_specs=[any_spec] * 4,
        out_shape=(
            jax.ShapeDtypeStruct((nx, 2) + cot.shape, cot.dtype),
            jax.ShapeDtypeStruct((2,) + hid.shape, hid.dtype),
            jax.ShapeDtypeStruct((nz, ny, 2) + proj.shape, proj.dtype),
            jax.ShapeDtypeStruct((nz, ny, 2, nx) + sk.shape, sk.dtype),
        ),
        scratch_shapes=[
            pltpu.SemaphoreType.DMA((copies,)),
            pltpu.SemaphoreType.DMA((copies,)),
            pltpu.SemaphoreType.DMA((4,)),
        ],
        compiler_params=pltpu.CompilerParams(collective_id=1, has_side_effects=True),
        cost_estimate=pl.CostEstimate(flops=0, bytes_accessed=60_000_000, transcendentals=0),
        name="gather",
    )(cot, hid, proj, sk)


def add_into(target, index, source, loop):
    at = index.index(None)

    @pl.loop(0, loop)
    def _(i):
        place = tuple(index[:at]) + (i,) + tuple(index[at + 1 :])
        target[place] = target[place] + source[i]


def reduce_kernel(
    ny, nz, nx, grad, comp, grad_o, comp_o, xg, xc, ya, za, zb, yb, cx, cy, cz, send_sems, recv_sems, local_sems
):
    here = Place(ny, nz, nx)
    x, y, z, c = (here.at[name] for name in "xyzc")
    wires = Wires(send_sems, recv_sems, local_sems)
    keep_comp = wires.keep(comp, xc)
    keep_grad = wires.keep(grad, xg)
    sib = here.device("c", 1)
    partners = [here.device("x", j) for j in range(1, nx)] + [here.device("y", j) for j in range(1, ny)]
    partners += [here.device("z", j) for j in range(1, nz)] + [sib]
    meet(partners)
    xp, xm = here.device("x", 1), here.device("x", -1)
    yp, ym = here.device("y", 1), here.device("y", -1)
    zp, zm = here.device("z", 1), here.device("z", -1)
    x1, x2, x3 = (here.shift("x", j) for j in (1, 2, 3))
    y1, y2, y3 = (here.shift("y", j) for j in (1, 2, 3))
    send = wires.send
    zlow, zhigh = pl.ds(0, nz // 2), pl.ds(nz // 2, nz // 2)

    keep_comp.wait()
    c_far = (
        send(xc.at[zlow, :, x2], cx.at[0, zlow], xp),
        send(xc.at[zhigh, :, x2], cx.at[1, zhigh], xm),
    )
    c_near = [
        send(xc.at[zhigh, :, x1], cx.at[2, zhigh], xp),
        send(xc.at[zlow, :, x3], cx.at[3, zlow], xm),
    ]
    keep_grad.wait()
    a_far = (send(xg.at[0, :, y2], ya.at[0], yp), send(xg.at[1, :, y2], ya.at[1], ym))
    b_dist = nz // 2

    def b_send(slot_at, dist):
        first = slot_at == "far"
        plus = here.shift("z", dist)
        minus = here.shift("z", -dist)
        if first:
            return (
                [send(xg.at[2, plus], zb.at[0, dist - 1, 0], zp)],
                [send(xg.at[3, minus], zb.at[1, dist - 1, 1], zm)],
            )
        return (
            [send(xg.at[pl.ds(2, 2), plus], zb.at[0, dist - 1], zp)],
            [send(xg.at[pl.ds(2, 2), minus], zb.at[1, dist - 1], zm)],
        )

    b_moving = b_send("far", b_dist)
    a_near = [send(xg.at[1, :, y1], ya.at[2], yp), send(xg.at[0, :, y3], ya.at[3], ym)]

    def b_step(dist, moving):
        for side, slots in ((0, (0,) if dist == b_dist else (0, 1)), (1, (1,) if dist == b_dist else (0, 1))):
            received(*moving[side])
            layer = here.shift("z", (dist - 1) * (1 - 2 * side))
            for s in slots:
                add_into(xg, [2 + s, layer, None], zb.at[side, dist - 1, s], ny)
        return b_send("near", dist - 1) if dist > 1 else None

    b_moving = b_step(b_dist, b_moving)
    received(c_far[0])
    add_into(xc, [None, slice(None), x1], cx.at[0], nz // 2)
    c_near.append(send(xc.at[zlow, :, x1], cx.at[2, zlow], xp))
    received(c_far[1])

    @pl.loop(nz // 2, nz)
    def _(i):
        xc[i, :, x3] = xc[i, :, x3] + cx[1, i]

    c_near.append(send(xc.at[zhigh, :, x3], cx.at[3, zhigh], xm))
    received(a_far[0])
    add_into(xg, [0, None, y1], ya.at[0], nz)
    a_near.append(send(xg.at[0, :, y1], ya.at[4], yp))
    received(a_far[1])
    add_into(xg, [1, None, y3], ya.at[1], nz)
    a_near.append(send(xg.at[1, :, y3], ya.at[5], ym))
    b_moving = b_step(3, b_moving)

    received(*c_near)

    @pl.loop(0, nz)
    def _(i):
        xc[i, :, x] = xc[i, :, x] + cx[2, i] + cx[3, i]

    c_y = [send(xc.at[:, here.shift("y", j), x], cy.at[j - 1], here.device("y", j)) for j in range(1, ny)]
    received(*c_y)

    @pl.loop(0, nz)
    def _(i):
        xc[i, y, x] = xc[i, y, x] + (cy[0, i] + cy[1, i] + cy[2, i])

    c_z = [send(xc.at[here.shift("z", j), y, x], cz.at[j - 1], here.device("z", j)) for j in range(1, nz)]
    b_moving = b_step(2, b_moving)
    received(*c_z)
    total = xc[z, y, x]
    for j in range(nz - 1):
        total = total + cz[j]
    comp_o[z, y, c, x] = total
    mine = comp_o.at[z, y, c, x]
    g_z = [send(mine, mine, here.device("z", j)) for j in range(1, nz)]
    received(*a_near)

    @pl.loop(0, nz)
    def _(i):
        xg[0, i, y] = xg[0, i, y] + ya[2 + 2, i] + ya[3, i]
        xg[1, i, y] = xg[1, i, y] + ya[2, i] + ya[5, i]

    def a_send(dist):
        plus, minus = here.shift("z", dist), here.shift("z", -dist)
        if dist == b_dist:
            return (
                [send(xg.at[0, plus, y], za.at[0, dist - 1, 0], zp)],
                [send(xg.at[1, minus, y], za.at[1, dist - 1, 1], zm)],
            )
        return (
            [send(xg.at[pl.ds(0, 2), plus, y], za.at[0, dist - 1], zp)],
            [send(xg.at[pl.ds(0, 2), minus, y], za.at[1, dist - 1], zm)],
        )

    def a_step(dist, moving):
        for side, slots in ((0, (0,) if dist == b_dist else (0, 1)), (1, (1,) if dist == b_dist else (0, 1))):
            received(*moving[side])
            layer = here.shift("z", (dist - 1) * (1 - 2 * side))
            for s in slots:
                xg[s, layer, y] = xg[s, layer, y] + za[side, dist - 1, s]
        return a_send(dist - 1) if dist > 1 else None

    a_moving = a_send(b_dist)
    received(*g_z)
    column = comp_o.at[:, y, c, x]
    g_y = [send(column, column, here.device("y", j)) for j in range(1, ny)]
    b_step(1, b_moving)
    b2_far = (send(xg.at[2, z, y2], yb.at[0], yp), send(xg.at[3, z, y2], yb.at[1], ym))
    b2_near = [send(xg.at[3, z, y1], yb.at[2], yp), send(xg.at[2, z, y3], yb.at[3], ym)]
    received(*g_y)
    plane = comp_o.at[:, :, c, x]
    g_x = (send(plane, plane, xp), send(plane, plane, xm))
    from_sib = [send(plane, plane, sib)]
    a_moving = a_step(b_dist, a_moving)
    received(b2_far[0])
    xg[2, z, y1] = xg[2, z, y1] + yb[0]
    b2_near.append(send(xg.at[2, z, y1], yb.at[4], yp))
    received(b2_far[1])
    xg[3, z, y3] = xg[3, z, y3] + yb[1]
    b2_near.append(send(xg.at[3, z, y3], yb.at[5], ym))
    a_moving = a_step(3, a_moving)
    a_moving = a_step(2, a_moving)
    received(*b2_near)
    xg[2, z, y] = xg[2, z, y] + yb[4] + yb[3]
    xg[3, z, y] = xg[3, z, y] + yb[2] + yb[5]
    a_step(1, a_moving)
    units = grad_o.shape[1]
    theirs = pl.ds(pl.multiple_of((1 - c) * units, 8), units)
    swap = send(xg.at[:, z, y, theirs], grad_o.at[pl.ds(c * 4, 4)], sib)
    for s in range(4):
        grad_o[c * 4 + s] = xg[s, z, y, pl.ds(pl.multiple_of(c * units, 8), units)]
    received(g_x[0])
    part = comp_o.at[zlow, :, c, x3]
    far = [send(part, part, xp)]
    received(g_x[1])
    part = comp_o.at[zhigh, :, c, x1]
    far.append(send(part, part, xm))
    for at in (x3, x1):
        part = comp_o.at[:, :, c, at]
        from_sib.append(send(part, part, sib))
    received(far[0])
    part = comp_o.at[zlow, :, c, x2]
    from_sib.append(send(part, part, sib))
    received(far[1])
    part = comp_o.at[zhigh, :, c, x2]
    from_sib.append(send(part, part, sib))
    received(swap, *from_sib)
    wires.drain()


def reduce_all(ny, nz, nx, grad, comp):
    slots, _, _, units, blk = grad.shape
    piece = comp.shape[3:]
    any_spec = pl.BlockSpec(memory_space=pl.ANY)
    vmem = pl.BlockSpec(memory_space=pltpu.VMEM)
    copies = 96
    return pl.pallas_call(
        functools.partial(reduce_kernel, ny, nz, nx),
        in_specs=[any_spec] * 2,
        out_specs=[vmem, vmem],
        out_shape=(
            jax.ShapeDtypeStruct((2 * slots, units // 2, blk), F32),
            jax.ShapeDtypeStruct((nz, ny, 2, nx) + piece, F32),
        ),
        scratch_shapes=[
            pltpu.VMEM(grad.shape, F32),
            pltpu.VMEM(comp.shape, F32),
            pltpu.VMEM((6, nz, units, blk), F32),
            pltpu.VMEM((2, nz // 2, 2, units, blk), F32),
            pltpu.VMEM((2, nz // 2, 2, ny, units, blk), F32),
            pltpu.VMEM((6, units, blk), F32),
            pltpu.VMEM((4, nz, ny) + piece, F32),
            pltpu.VMEM((ny - 1, nz) + piece, F32),
            pltpu.VMEM((nz - 1,) + piece, F32),
            pltpu.SemaphoreType.DMA((copies,)),
            pltpu.SemaphoreType.DMA((copies,)),
            pltpu.SemaphoreType.DMA((2,)),
        ],
        compiler_params=pltpu.CompilerParams(
            collective_id=2, has_side_effects=True, vmem_limit_bytes=48 * MIB
        ),
        cost_estimate=pl.CostEstimate(flops=0, bytes_accessed=100_000_000, transcendentals=0),
        name="reduce",
    )(grad, comp)


def identity(n):
    rows = lax.broadcasted_iota(jnp.int32, (n, n), 0)
    cols = lax.broadcasted_iota(jnp.int32, (n, n), 1)
    return jnp.where(rows == cols, 1.0, 0.0).astype(F32)


def mul(left, right):
    return exact_dot(left, right, ((1,), (0,)))


def spd_inverse(mat, eye):
    n = mat.shape[0]
    bound = jnp.max(jnp.sum(jnp.abs(mat), axis=1, keepdims=True))
    start = eye * (2.0 / (bound + math.sqrt(EPS)))

    def unfinished(state):
        count, previous, residual, _ = state
        return (count < 100) & (residual > 2e-6) & ((residual < 0.5 * previous) | (residual > 0.1))

    def body(state):
        count, _, residual, guess = state
        gap = eye - mul(mat, guess)
        guess = guess + mul(guess, gap)
        return count + 1, residual, jnp.max(jnp.abs(gap)), guess

    state = lax.while_loop(unfinished, body, (0, jnp.float32(4.0), jnp.float32(2.0), start))
    return state[3]


def mixing_of(gram):
    n = gram.shape[0]
    eye = identity(n)
    shifted = gram + EPS * eye
    total = jnp.sum(jnp.sum(shifted * shifted, axis=1, keepdims=True), axis=0, keepdims=True)
    frob = jnp.sqrt(total)
    root = shifted / frob
    middle = 1.5 * eye - 0.5 * root
    root = mul(root, middle)
    inverse = middle
    for _ in range(NS_STEPS - 1):
        middle = 1.5 * eye - 0.5 * mul(inverse, root)
        root = mul(root, middle)
        inverse = mul(middle, inverse)
    half = 0.5 * jnp.sqrt(frob) * (root + root.T) + math.sqrt(EPS) * eye
    half_inv = spd_inverse(half, eye)
    return -mul(inverse, half_inv) / (math.sqrt(EPS) * jnp.sqrt(frob))


def finish_kernel(row_ref, pat_ref, grad_ref, sketch_ref, comp_ref, out_ref, gram_ref, sel_ref):
    slots, rows, blk = grad_ref.shape
    rank = comp_ref.shape[1]
    width = comp_ref.shape[0]
    chunk = 1024
    gram_ref[...] = jnp.zeros_like(gram_ref)

    @pl.loop(0, width // chunk)
    def _(i):
        at = pl.ds(pl.multiple_of(i * chunk, chunk), chunk)
        st = jnp.concatenate([sketch_ref[at, :], comp_ref[at, :]], axis=1)
        high, low = split_bf16(st)
        dims = (((0,), (0,)), ((), ()))
        gram_ref[0] += lax.dot_general(high, high, dims, preferred_element_type=F32)
        gram_ref[1] += lax.dot_general(high, low, dims, preferred_element_type=F32)

    cross = gram_ref[1]
    mixing = mixing_of(gram_ref[0] + (cross + cross.T))
    start = row_ref[0]
    first = lax.div(start, blk)
    last = pat_ref.shape[0] - 1
    grad = jnp.concatenate([grad_ref[k] for k in range(slots)], axis=1)
    block_of = lax.div(start + lax.broadcasted_iota(jnp.int32, (rows, 1), 0), blk)
    projected = None
    for g in range(2):
        brow = jnp.minimum(first + g, last)
        for k in range(slots):
            col = pl.multiple_of(pat_ref[brow, k] * blk, blk)
            here = pl.ds(k * blk, blk)
            sel_ref[g, here, :rank] = sketch_ref[pl.ds(col, blk), :]
            sel_ref[g, here, rank:] = comp_ref[pl.ds(col, blk), :]
        part = mul(grad, sel_ref[g])
        projected = part if projected is None else jnp.where(block_of == first + g, part, projected)
    mixed = mul(projected, mixing)
    corr = exact_dot(mixed, sel_ref[0], ((1,), (1,)))
    corr1 = exact_dot(mixed, sel_ref[1], ((1,), (1,)))
    corr = jnp.where(block_of == first + 1, corr1, corr)
    result = grad * (1.0 / math.sqrt(EPS)) + corr
    for k in range(slots):
        out_ref[:, k, :] = result[:, k * blk : (k + 1) * blk]


def finish(start_row, pattern, grad, sketch_t, comp_t):
    slots, rows, blk = grad.shape
    rank = comp_t.shape[1]
    smem = pl.BlockSpec(memory_space=pltpu.SMEM)
    vmem = pl.BlockSpec(memory_space=pltpu.VMEM)
    return pl.pallas_call(
        finish_kernel,
        in_specs=[smem, smem, vmem, vmem, vmem],
        out_specs=vmem,
        out_shape=jax.ShapeDtypeStruct((rows, slots, blk), F32),
        scratch_shapes=[
            pltpu.VMEM((2, 2 * rank, 2 * rank), F32),
            pltpu.VMEM((2, slots * blk, 2 * rank), F32),
        ],
        compiler_params=pltpu.CompilerParams(vmem_limit_bytes=40 * MIB),
        cost_estimate=pl.CostEstimate(flops=5_000_000_000, bytes_accessed=9_000_000, transcendentals=0),
        name="finish",
    )(start_row, pattern, grad, sketch_t, comp_t)


def per_device(weights, hidden, cotangent, sketch, projection, pattern):
    rank = sketch.shape[0]
    slots, blk = weights.shape[1:]
    dp_size = lax.axis_size("dp")
    nx = lax.axis_size("mp")
    ny = 4
    nz = dp_size // (2 * ny)
    dev_rows = weights.shape[0] // dp_size
    all_tokens = hidden.shape[0] * dp_size
    dp = lax.axis_index("dp")
    core = lax.rem(dp, 2).reshape(1).astype(jnp.int32)
    cot, hid, proj, sketch_t = gather(
        ny, nz, nx, cotangent, hidden, projection.reshape(rank, dev_rows).T, sketch.T
    )
    cot = cot.reshape(nx, -1, cotangent.shape[1])
    hid = hid.reshape(-1, hidden.shape[1])
    input_grad, grad, comp = local_step(
        core, pattern, cot, hid, weights.transpose(1, 0, 2), proj.reshape(-1, rank), all_tokens
    )
    grad, comp = reduce_all(
        ny, nz, nx, grad.reshape(slots // 2, nz, ny, 2 * dev_rows, blk), comp.reshape(nz, ny, nx, -1, rank)
    )
    start_row = (dp * dev_rows).reshape(1).astype(jnp.int32)
    direction = finish(start_row, pattern, grad, sketch_t.reshape(-1, rank), comp.reshape(-1, rank))
    return input_grad, direction[None]


def solution(mesh):
    return jax.shard_map(
        per_device,
        mesh=mesh,
        in_specs=(
            P("mp", None, None),
            P("dp", "mp"),
            P("dp", "mp"),
            P(None, ("dp", "mp")),
            P(None, "mp", "dp"),
            P("mp", None),
        ),
        out_specs=(P("dp", "mp"), P("mp", "dp", None, None)),
        check_vma=False,
    )
```

```python
import functools
import math

import jax
import jax.numpy as jnp
from jax import lax
from jax.experimental import pallas as pl
from jax.experimental.pallas import tpu as pltpu
from jax.sharding import PartitionSpec as P

NS_STEPS = 5
EPS = 0.0001
F32 = jnp.float32
BF16 = jnp.bfloat16
MIB = 1 << 20


def split_bf16(value):
    high = value.astype(BF16)
    low = (value - high.astype(F32)).astype(BF16)
    return high, low


def exact_dot(left, right, dims):
    return lax.dot_general(
        left, right, (dims, ((), ())), precision=lax.Precision.HIGHEST, preferred_element_type=F32
    )


def local_kernel(inv_tokens, core_ref, pat_ref, cot_ref, hid_ref, wgt_ref, proj_ref, back_ref, grad_ref, comp_ref, z_ref):
    step = pl.program_id(0)
    core = core_ref[0]
    slots = wgt_ref.shape[0]
    mine = slots // 2
    blk = hid_ref.shape[1]
    rank = proj_ref.shape[1]
    tokens = back_ref.shape[0]
    per_part = cot_ref.shape[2] // blk
    half_blocks = z_ref.shape[0]
    own = pl.ds(pl.multiple_of(core * tokens, tokens), tokens)

    def cot_block(col, rows=slice(None)):
        lane = pl.multiple_of(lax.rem(col, per_part) * blk, blk)
        return cot_ref[lax.div(col, per_part), rows, pl.ds(lane, blk)]

    @pl.when(step == 0)
    def _():
        @pl.loop(0, half_blocks)
        def _(i):
            z_ref[i] = jnp.zeros(z_ref.shape[1:], F32)

    cols = [pat_ref[step, k] for k in range(slots)]
    chosen = jnp.concatenate([cot_block(col, own) for col in cols], axis=1)
    weight = jnp.concatenate([wgt_ref[k] for k in range(slots)], axis=1)
    back = lax.dot_general(chosen, weight, (((1,), (1,)), ((), ())), preferred_element_type=F32)
    back_ref[...] = back.astype(BF16)
    hid = hid_ref[...]
    wide = jnp.concatenate([cot_block(pat_ref[step, mine * core + j]) for j in range(mine)], axis=1)
    grad = lax.dot_general(hid, wide, (((0,), (0,)), ((), ())), preferred_element_type=F32)
    grad = grad * inv_tokens
    for j in range(mine):
        grad_ref[j] = grad[:, j * blk : (j + 1) * blk]
    high, low = split_bf16(proj_ref[...])
    both = jnp.dot(hid, jnp.concatenate([high, low], axis=1), preferred_element_type=F32)
    y = both[:, :rank] + both[:, rank:]
    for col in cols:

        @pl.when(lax.rem(col, 2) == core)
        def _(col=col):
            z_ref[lax.div(col, 2)] += y

    @pl.when(step == pl.num_programs(0) - 1)
    def _():
        @pl.loop(0, half_blocks)
        def _(i):
            zh, zl = split_bf16(z_ref[i])
            out = lax.dot_general(
                cot_block(2 * i + core),
                jnp.concatenate([zh, zl], axis=1),
                (((0,), (0,)), ((), ())),
                preferred_element_type=F32,
            )
            comp_ref[i] = (out[:, :rank] + out[:, rank:]) * inv_tokens


def local_step(core, pattern, cot, hidden, weights, proj, all_tokens):
    parts, wide_tokens, part_cols = cot.shape
    tokens = wide_tokens // 2
    block_rows, slots = pattern.shape
    blk = weights.shape[2]
    rows = hidden.shape[1]
    rank = proj.shape[1]
    half_blocks = parts * part_cols // blk // 2
    grid_spec = pltpu.PrefetchScalarGridSpec(
        num_scalar_prefetch=2,
        grid=(block_rows,),
        in_specs=[
            pl.BlockSpec((parts, wide_tokens, part_cols), lambda r, *_: (0, 0, 0), pipeline_mode=pl.Buffered(1)),
            pl.BlockSpec((wide_tokens, blk), lambda r, *_: (0, r)),
            pl.BlockSpec((slots, blk, blk), lambda r, *_: (0, r, 0)),
            pl.BlockSpec((blk, rank), lambda r, *_: (r, 0)),
        ],
        out_specs=[
            pl.BlockSpec((tokens, blk), lambda r, *_: (0, r)),
            pl.BlockSpec((slots // 2, blk, blk), lambda r, *_: (0, r, 0)),
            pl.BlockSpec((half_blocks, blk, rank), lambda r, *_: (0, 0, 0), pipeline_mode=pl.Buffered(1)),
        ],
        scratch_shapes=[pltpu.VMEM((half_blocks, wide_tokens, rank), F32)],
    )
    return pl.pallas_call(
        functools.partial(local_kernel, 1.0 / all_tokens),
        grid_spec=grid_spec,
        out_shape=(
            jax.ShapeDtypeStruct((tokens, rows), BF16),
            jax.ShapeDtypeStruct((slots // 2, rows, blk), F32),
            jax.ShapeDtypeStruct((half_blocks, blk, rank), F32),
        ),
        compiler_params=pltpu.CompilerParams(vmem_limit_bytes=48 * MIB),
        cost_estimate=pl.CostEstimate(flops=6_000_000_000, bytes_accessed=36_000_000, transcendentals=0),
        name="local_step",
    )(core, pattern, cot, hidden, weights, proj)


class Wires:
    def __init__(self, send_sems, recv_sems, local_sems):
        self.send_sems, self.recv_sems, self.local_sems = send_sems, recv_sems, local_sems
        self.used = 0
        self.locals = 0
        self.sent = []

    def send(self, source, target, device):
        copy = pltpu.make_async_remote_copy(
            src_ref=source,
            dst_ref=target,
            send_sem=self.send_sems.at[self.used],
            recv_sem=self.recv_sems.at[self.used],
            device_id=device,
            device_id_type=pl.DeviceIdType.MESH,
        )
        self.used += 1
        copy.start()
        self.sent.append(copy)
        return copy

    def keep(self, source, target):
        copy = pltpu.make_async_copy(source, target, self.local_sems.at[self.locals])
        self.locals += 1
        copy.start()
        return copy

    def drain(self):
        for copy in self.sent:
            copy.wait_send()


def received(*copies):
    for copy in copies:
        copy.wait_recv()


class Place:
    def __init__(self, ny, nz, nx):
        self.n = {"x": nx, "y": ny, "z": nz, "c": 2}
        d = lax.axis_index("dp")
        self.at = {
            "x": lax.axis_index("mp"),
            "c": lax.rem(d, 2),
            "y": lax.rem(lax.div(d, 2), ny),
            "z": lax.div(d, 2 * ny),
        }

    def shift(self, axis, by):
        n = self.n[axis]
        return lax.rem(self.at[axis] + (by % n), n)

    def device(self, axis, by):
        at = dict(self.at)
        at[axis] = self.shift(axis, by)
        return ((at["z"] * self.n["y"] + at["y"]) * 2 + at["c"], at["x"])


def meet(devices):
    barrier = pltpu.get_barrier_semaphore()
    for device in devices:
        pl.semaphore_signal(barrier, inc=1, device_id=device, device_id_type=pl.DeviceIdType.MESH)
    pl.semaphore_wait(barrier, len(devices))


def gather_kernel(ny, nz, nx, cot, hid, proj, sk, cot_o, hid_o, proj_o, sk_o, cot_v, hid_v, proj_v, sk_v, send_sems, recv_sems, local_sems):
    here = Place(ny, nz, nx)
    x, y, z, c = (here.at[name] for name in "xyzc")
    wires = Wires(send_sems, recv_sems, local_sems)
    partners = [here.device("x", j) for j in range(1, nx)] + [here.device("y", j) for j in range(1, ny)]
    partners += [here.device("z", 1), here.device("z", -1), here.device("c", 1)]
    sib = here.device("c", 1)
    loads = [wires.keep(a, b) for a, b in ((sk, sk_v), (proj, proj_v), (cot, cot_v), (hid, hid_v))]
    meet(partners)
    targets = (sk_o.at[z, y, c, x], proj_o.at[z, y, c], cot_o.at[x, c], hid_o.at[c])
    rows = cot.shape[0] // 2
    top, bottom = pl.ds(0, rows), pl.ds(rows, rows)
    sk_x = [wires.send(sk, sk_o.at[z, y, c, x], here.device("x", j)) for j in range(1, nx)]
    proj_y = [wires.send(proj, proj_o.at[z, y, c], here.device("y", j)) for j in range(1, ny)]
    right, left = here.device("x", 1), here.device("x", -1)

    def cot_send(rows_at, device):
        return wires.send(cot.at[rows_at], cot_o.at[x, c, rows_at], device)

    def cot_pass(part, rows_at, device):
        return wires.send(cot_o.at[part, c, rows_at], cot_o.at[part, c, rows_at], device)

    r_top, l_bottom = cot_send(top, right), cot_send(bottom, left)
    r_bottom, l_top = cot_send(bottom, right), cot_send(top, left)
    from_sib = [wires.send(hid, hid_o.at[c], sib), wires.send(cot, cot_o.at[x, c], sib)]

    keeps = []
    for load, value, target in zip(loads, (sk_v, proj_v, cot_v, hid_v), targets):
        load.wait()
        keeps.append(wires.keep(value, target))
    keep_sk, keep_proj, keep_cot, keep_hid = keeps
    keep_sk.wait()
    received(*sk_x)
    sk_y = [
        wires.send(sk_o.at[z, y, c], sk_o.at[z, y, c], here.device("y", j)) for j in range(1, ny)
    ]
    keep_proj.wait()
    received(*proj_y)

    up, down = here.device("z", 1), here.device("z", -1)

    def z_pass(ref, layer, device, ys=slice(None)):
        view = ref.at[layer, ys, c]
        return wires.send(view, view, device)

    arrays = (proj_o, sk_o)
    low, high = pl.ds(0, ny // 2), pl.ds(ny // 2, ny // 2)
    going_up, going_down = [z_pass(proj_o, z, up)], [z_pass(proj_o, z, down)]
    from_sib.append(z_pass(proj_o, z, sib))
    received(*sk_y)
    going_up.append(z_pass(sk_o, z, up))
    going_down.append(z_pass(sk_o, z, down))
    from_sib.append(z_pass(sk_o, z, sib))

    def z_step(distance, going_up, going_down):
        below, above = here.shift("z", -distance), here.shift("z", distance)
        next_up, next_down = [], []
        last = distance == nz // 2
        for moved, layer, device, part, nexts in (
            (going_up, below, up, low, next_up),
            (going_down, above, down, high, next_down),
        ):
            for copy, ref in zip(moved, arrays):
                received(copy)
                if not last:
                    ys = part if distance + 1 == nz // 2 else slice(None)
                    nexts.append(z_pass(ref, layer, device, ys))
                from_sib.append(z_pass(ref, layer, sib, part if last else slice(None)))
        return next_up, next_down

    left_part, right_part, far_part = here.shift("x", -1), here.shift("x", 1), here.shift("x", 2)

    def cot_first():
        received(r_top)
        far_top = cot_pass(left_part, top, right)
        from_sib.append(cot_pass(left_part, top, sib))
        received(l_bottom)
        far_bottom = cot_pass(right_part, bottom, left)
        from_sib.append(cot_pass(right_part, bottom, sib))
        return far_top, far_bottom

    for distance in range(1, nz // 2 + 1):
        if distance == 2:
            far_top, far_bottom = cot_first()
        if distance == 3:
            received(r_bottom)
            from_sib.append(cot_pass(left_part, bottom, sib))
            received(l_top)
            from_sib.append(cot_pass(right_part, top, sib))
        going_up, going_down = z_step(distance, going_up, going_down)
    received(far_top)
    from_sib.append(cot_pass(far_part, top, sib))
    received(far_bottom)
    from_sib.append(cot_pass(far_part, bottom, sib))
    keep_cot.wait()
    keep_hid.wait()
    received(*from_sib)
    wires.drain()


def gather(ny, nz, nx, cot, hid, proj, sk):
    any_spec = pl.BlockSpec(memory_space=pl.ANY)
    copies = 80
    return pl.pallas_call(
        functools.partial(gather_kernel, ny, nz, nx),
        in_specs=[any_spec] * 4,
        out_specs=[any_spec] * 4,
        out_shape=(
            jax.ShapeDtypeStruct((nx, 2) + cot.shape, cot.dtype),
            jax.ShapeDtypeStruct((2,) + hid.shape, hid.dtype),
            jax.ShapeDtypeStruct((nz, ny, 2) + proj.shape, proj.dtype),
            jax.ShapeDtypeStruct((nz, ny, 2, nx) + sk.shape, sk.dtype),
        ),
        scratch_shapes=[
            pltpu.VMEM(cot.shape, cot.dtype),
            pltpu.VMEM(hid.shape, hid.dtype),
            pltpu.VMEM(proj.shape, proj.dtype),
            pltpu.VMEM(sk.shape, sk.dtype),
            pltpu.SemaphoreType.DMA((copies,)),
            pltpu.SemaphoreType.DMA((copies,)),
            pltpu.SemaphoreType.DMA((8,)),
        ],
        compiler_params=pltpu.CompilerParams(collective_id=1, has_side_effects=True),
        cost_estimate=pl.CostEstimate(flops=0, bytes_accessed=60_000_000, transcendentals=0),
        name="gather",
    )(cot, hid, proj, sk)


def add_into(target, index, source, loop):
    at = index.index(None)

    @pl.loop(0, loop)
    def _(i):
        place = tuple(index[:at]) + (i,) + tuple(index[at + 1 :])
        target[place] = target[place] + source[i]


def reduce_kernel(
    ny, nz, nx, grad, comp, grad_o, comp_o, xg, xc, ya, za, zb, yb, cx, cy, cz, send_sems, recv_sems, local_sems
):
    here = Place(ny, nz, nx)
    x, y, z, c = (here.at[name] for name in "xyzc")
    wires = Wires(send_sems, recv_sems, local_sems)
    keep_comp = wires.keep(comp, xc)
    keep_grad = wires.keep(grad, xg)
    sib = here.device("c", 1)
    partners = [here.device("x", j) for j in range(1, nx)] + [here.device("y", j) for j in range(1, ny)]
    partners += [here.device("z", j) for j in range(1, nz)] + [sib]
    meet(partners)
    xp, xm = here.device("x", 1), here.device("x", -1)
    yp, ym = here.device("y", 1), here.device("y", -1)
    zp, zm = here.device("z", 1), here.device("z", -1)
    x1, x2, x3 = (here.shift("x", j) for j in (1, 2, 3))
    y1, y2, y3 = (here.shift("y", j) for j in (1, 2, 3))
    send = wires.send
    zlow, zhigh = pl.ds(0, nz // 2), pl.ds(nz // 2, nz // 2)

    keep_comp.wait()
    c_far = (
        send(xc.at[zlow, :, x2], cx.at[0, zlow], xp),
        send(xc.at[zhigh, :, x2], cx.at[1, zhigh], xm),
    )
    c_near = [
        send(xc.at[zhigh, :, x1], cx.at[2, zhigh], xp),
        send(xc.at[zlow, :, x3], cx.at[3, zlow], xm),
    ]
    keep_grad.wait()
    a_far = (send(xg.at[0, :, y2], ya.at[0], yp), send(xg.at[1, :, y2], ya.at[1], ym))
    b_dist = nz // 2

    def b_send(slot_at, dist):
        first = slot_at == "far"
        plus = here.shift("z", dist)
        minus = here.shift("z", -dist)
        if first:
            return (
                [send(xg.at[2, plus], zb.at[0, dist - 1, 0], zp)],
                [send(xg.at[3, minus], zb.at[1, dist - 1, 1], zm)],
            )
        return (
            [send(xg.at[pl.ds(2, 2), plus], zb.at[0, dist - 1], zp)],
            [send(xg.at[pl.ds(2, 2), minus], zb.at[1, dist - 1], zm)],
        )

    b_moving = b_send("far", b_dist)
    a_near = [send(xg.at[1, :, y1], ya.at[2], yp), send(xg.at[0, :, y3], ya.at[3], ym)]

    def b_step(dist, moving):
        for side, slots in ((0, (0,) if dist == b_dist else (0, 1)), (1, (1,) if dist == b_dist else (0, 1))):
            received(*moving[side])
            layer = here.shift("z", (dist - 1) * (1 - 2 * side))
            for s in slots:
                add_into(xg, [2 + s, layer, None], zb.at[side, dist - 1, s], ny)
        return b_send("near", dist - 1) if dist > 1 else None

    b_moving = b_step(b_dist, b_moving)
    received(c_far[0])
    add_into(xc, [None, slice(None), x1], cx.at[0], nz // 2)
    c_near.append(send(xc.at[zlow, :, x1], cx.at[2, zlow], xp))
    received(c_far[1])

    @pl.loop(nz // 2, nz)
    def _(i):
        xc[i, :, x3] = xc[i, :, x3] + cx[1, i]

    c_near.append(send(xc.at[zhigh, :, x3], cx.at[3, zhigh], xm))
    received(a_far[0])
    add_into(xg, [0, None, y1], ya.at[0], nz)
    a_near.append(send(xg.at[0, :, y1], ya.at[4], yp))
    received(a_far[1])
    add_into(xg, [1, None, y3], ya.at[1], nz)
    a_near.append(send(xg.at[1, :, y3], ya.at[5], ym))
    b_moving = b_step(3, b_moving)

    received(*c_near)

    @pl.loop(0, nz)
    def _(i):
        xc[i, :, x] = xc[i, :, x] + cx[2, i] + cx[3, i]

    c_y = [send(xc.at[:, here.shift("y", j), x], cy.at[j - 1], here.device("y", j)) for j in range(1, ny)]
    received(*c_y)

    @pl.loop(0, nz)
    def _(i):
        xc[i, y, x] = xc[i, y, x] + (cy[0, i] + cy[1, i] + cy[2, i])

    c_z = [send(xc.at[here.shift("z", j), y, x], cz.at[j - 1], here.device("z", j)) for j in range(1, nz)]
    b_moving = b_step(2, b_moving)
    received(*c_z)
    total = xc[z, y, x]
    for j in range(nz - 1):
        total = total + cz[j]
    comp_o[z, y, c, x] = total
    mine = comp_o.at[z, y, c, x]
    g_z = [send(mine, mine, here.device("z", j)) for j in range(1, nz)]
    received(*a_near)

    @pl.loop(0, nz)
    def _(i):
        xg[0, i, y] = xg[0, i, y] + ya[2 + 2, i] + ya[3, i]
        xg[1, i, y] = xg[1, i, y] + ya[2, i] + ya[5, i]

    def a_send(dist):
        plus, minus = here.shift("z", dist), here.shift("z", -dist)
        if dist == b_dist:
            return (
                [send(xg.at[0, plus, y], za.at[0, dist - 1, 0], zp)],
                [send(xg.at[1, minus, y], za.at[1, dist - 1, 1], zm)],
            )
        return (
            [send(xg.at[pl.ds(0, 2), plus, y], za.at[0, dist - 1], zp)],
            [send(xg.at[pl.ds(0, 2), minus, y], za.at[1, dist - 1], zm)],
        )

    def a_step(dist, moving):
        for side, slots in ((0, (0,) if dist == b_dist else (0, 1)), (1, (1,) if dist == b_dist else (0, 1))):
            received(*moving[side])
            layer = here.shift("z", (dist - 1) * (1 - 2 * side))
            for s in slots:
                xg[s, layer, y] = xg[s, layer, y] + za[side, dist - 1, s]
        return a_send(dist - 1) if dist > 1 else None

    a_moving = a_send(b_dist)
    received(*g_z)
    column = comp_o.at[:, y, c, x]
    g_y = [send(column, column, here.device("y", j)) for j in range(1, ny)]
    b_step(1, b_moving)
    b2_far = (send(xg.at[2, z, y2], yb.at[0], yp), send(xg.at[3, z, y2], yb.at[1], ym))
    b2_near = [send(xg.at[3, z, y1], yb.at[2], yp), send(xg.at[2, z, y3], yb.at[3], ym)]
    received(*g_y)
    plane = comp_o.at[:, :, c, x]
    g_x = (send(plane, plane, xp), send(plane, plane, xm))
    from_sib = [send(plane, plane, sib)]
    a_moving = a_step(b_dist, a_moving)
    received(b2_far[0])
    xg[2, z, y1] = xg[2, z, y1] + yb[0]
    b2_near.append(send(xg.at[2, z, y1], yb.at[4], yp))
    received(b2_far[1])
    xg[3, z, y3] = xg[3, z, y3] + yb[1]
    b2_near.append(send(xg.at[3, z, y3], yb.at[5], ym))
    a_moving = a_step(3, a_moving)
    a_moving = a_step(2, a_moving)
    received(*b2_near)
    xg[2, z, y] = xg[2, z, y] + yb[4] + yb[3]
    xg[3, z, y] = xg[3, z, y] + yb[2] + yb[5]
    a_step(1, a_moving)
    units = grad_o.shape[1]
    theirs = pl.ds(pl.multiple_of((1 - c) * units, 8), units)
    swap = send(xg.at[:, z, y, theirs], grad_o.at[pl.ds(c * 4, 4)], sib)
    for s in range(4):
        grad_o[c * 4 + s] = xg[s, z, y, pl.ds(pl.multiple_of(c * units, 8), units)]
    received(g_x[0])
    part = comp_o.at[zlow, :, c, x3]
    far = [send(part, part, xp)]
    received(g_x[1])
    part = comp_o.at[zhigh, :, c, x1]
    far.append(send(part, part, xm))
    for at in (x3, x1):
        part = comp_o.at[:, :, c, at]
        from_sib.append(send(part, part, sib))
    received(far[0])
    part = comp_o.at[zlow, :, c, x2]
    from_sib.append(send(part, part, sib))
    received(far[1])
    part = comp_o.at[zhigh, :, c, x2]
    from_sib.append(send(part, part, sib))
    received(swap, *from_sib)
    wires.drain()


def reduce_all(ny, nz, nx, grad, comp):
    slots, _, _, units, blk = grad.shape
    piece = comp.shape[3:]
    any_spec = pl.BlockSpec(memory_space=pl.ANY)
    vmem = pl.BlockSpec(memory_space=pltpu.VMEM)
    copies = 96
    return pl.pallas_call(
        functools.partial(reduce_kernel, ny, nz, nx),
        in_specs=[any_spec] * 2,
        out_specs=[vmem, vmem],
        out_shape=(
            jax.ShapeDtypeStruct((2 * slots, units // 2, blk), F32),
            jax.ShapeDtypeStruct((nz, ny, 2, nx) + piece, F32),
        ),
        scratch_shapes=[
            pltpu.VMEM(grad.shape, F32),
            pltpu.VMEM(comp.shape, F32),
            pltpu.VMEM((6, nz, units, blk), F32),
            pltpu.VMEM((2, nz // 2, 2, units, blk), F32),
            pltpu.VMEM((2, nz // 2, 2, ny, units, blk), F32),
            pltpu.VMEM((6, units, blk), F32),
            pltpu.VMEM((4, nz, ny) + piece, F32),
            pltpu.VMEM((ny - 1, nz) + piece, F32),
            pltpu.VMEM((nz - 1,) + piece, F32),
            pltpu.SemaphoreType.DMA((copies,)),
            pltpu.SemaphoreType.DMA((copies,)),
            pltpu.SemaphoreType.DMA((2,)),
        ],
        compiler_params=pltpu.CompilerParams(
            collective_id=2, has_side_effects=True, vmem_limit_bytes=48 * MIB
        ),
        cost_estimate=pl.CostEstimate(flops=0, bytes_accessed=100_000_000, transcendentals=0),
        name="reduce",
    )(grad, comp)


def identity(n):
    rows = lax.broadcasted_iota(jnp.int32, (n, n), 0)
    cols = lax.broadcasted_iota(jnp.int32, (n, n), 1)
    return jnp.where(rows == cols, 1.0, 0.0).astype(F32)


def mul(left, right):
    return exact_dot(left, right, ((1,), (0,)))


def spd_inverse(mat, eye):
    n = mat.shape[0]
    bound = jnp.max(jnp.sum(jnp.abs(mat), axis=1, keepdims=True))
    start = eye * (2.0 / (bound + math.sqrt(EPS)))

    def unfinished(state):
        count, previous, residual, _ = state
        return (count < 100) & (residual > 2e-6) & ((residual < 0.5 * previous) | (residual > 0.1))

    def body(state):
        count, _, residual, guess = state
        gap = eye - mul(mat, guess)
        guess = guess + mul(guess, gap)
        return count + 1, residual, jnp.max(jnp.abs(gap)), guess

    state = lax.while_loop(unfinished, body, (0, jnp.float32(4.0), jnp.float32(2.0), start))
    return state[3]


def mixing_of(gram):
    n = gram.shape[0]
    eye = identity(n)
    shifted = gram + EPS * eye
    total = jnp.sum(jnp.sum(shifted * shifted, axis=1, keepdims=True), axis=0, keepdims=True)
    frob = jnp.sqrt(total)
    root = shifted / frob
    middle = 1.5 * eye - 0.5 * root
    root = mul(root, middle)
    inverse = middle
    for _ in range(NS_STEPS - 1):
        middle = 1.5 * eye - 0.5 * mul(inverse, root)
        root = mul(root, middle)
        inverse = mul(middle, inverse)
    half = 0.5 * jnp.sqrt(frob) * (root + root.T) + math.sqrt(EPS) * eye
    half_inv = spd_inverse(half, eye)
    return -mul(inverse, half_inv) / (math.sqrt(EPS) * jnp.sqrt(frob))


def finish_kernel(row_ref, pat_ref, grad_ref, sketch_ref, comp_ref, out_ref, gram_ref, sel_ref):
    slots, rows, blk = grad_ref.shape
    rank = comp_ref.shape[1]
    width = comp_ref.shape[0]
    chunk = 1024
    gram_ref[...] = jnp.zeros_like(gram_ref)

    @pl.loop(0, width // chunk)
    def _(i):
        at = pl.ds(pl.multiple_of(i * chunk, chunk), chunk)
        st = jnp.concatenate([sketch_ref[at, :], comp_ref[at, :]], axis=1)
        high, low = split_bf16(st)
        dims = (((0,), (0,)), ((), ()))
        gram_ref[0] += lax.dot_general(high, high, dims, preferred_element_type=F32)
        gram_ref[1] += lax.dot_general(high, low, dims, preferred_element_type=F32)

    cross = gram_ref[1]
    mixing = mixing_of(gram_ref[0] + (cross + cross.T))
    start = row_ref[0]
    first = lax.div(start, blk)
    last = pat_ref.shape[0] - 1
    grad = jnp.concatenate([grad_ref[k] for k in range(slots)], axis=1)
    block_of = lax.div(start + lax.broadcasted_iota(jnp.int32, (rows, 1), 0), blk)
    projected = None
    for g in range(2):
        brow = jnp.minimum(first + g, last)
        for k in range(slots):
            col = pl.multiple_of(pat_ref[brow, k] * blk, blk)
            here = pl.ds(k * blk, blk)
            sel_ref[g, here, :rank] = sketch_ref[pl.ds(col, blk), :]
            sel_ref[g, here, rank:] = comp_ref[pl.ds(col, blk), :]
        part = mul(grad, sel_ref[g])
        projected = part if projected is None else jnp.where(block_of == first + g, part, projected)
    mixed = mul(projected, mixing)
    corr = exact_dot(mixed, sel_ref[0], ((1,), (1,)))
    corr1 = exact_dot(mixed, sel_ref[1], ((1,), (1,)))
    corr = jnp.where(block_of == first + 1, corr1, corr)
    result = grad * (1.0 / math.sqrt(EPS)) + corr
    for k in range(slots):
        out_ref[:, k, :] = result[:, k * blk : (k + 1) * blk]


def finish(start_row, pattern, grad, sketch_t, comp_t):
    slots, rows, blk = grad.shape
    rank = comp_t.shape[1]
    smem = pl.BlockSpec(memory_space=pltpu.SMEM)
    vmem = pl.BlockSpec(memory_space=pltpu.VMEM)
    return pl.pallas_call(
        finish_kernel,
        in_specs=[smem, smem, vmem, vmem, vmem],
        out_specs=vmem,
        out_shape=jax.ShapeDtypeStruct((rows, slots, blk), F32),
        scratch_shapes=[
            pltpu.VMEM((2, 2 * rank, 2 * rank), F32),
            pltpu.VMEM((2, slots * blk, 2 * rank), F32),
        ],
        compiler_params=pltpu.CompilerParams(vmem_limit_bytes=40 * MIB),
        cost_estimate=pl.CostEstimate(flops=5_000_000_000, bytes_accessed=9_000_000, transcendentals=0),
        name="finish",
    )(start_row, pattern, grad, sketch_t, comp_t)


def per_device(weights, hidden, cotangent, sketch, projection, pattern):
    rank = sketch.shape[0]
    slots, blk = weights.shape[1:]
    dp_size = lax.axis_size("dp")
    nx = lax.axis_size("mp")
    ny = 4
    nz = dp_size // (2 * ny)
    dev_rows = weights.shape[0] // dp_size
    all_tokens = hidden.shape[0] * dp_size
    dp = lax.axis_index("dp")
    core = lax.rem(dp, 2).reshape(1).astype(jnp.int32)
    cot, hid, proj, sketch_t = gather(
        ny, nz, nx, cotangent, hidden, projection.reshape(rank, dev_rows).T, sketch.T
    )
    cot = cot.reshape(nx, -1, cotangent.shape[1])
    hid = hid.reshape(-1, hidden.shape[1])
    input_grad, grad, comp = local_step(
        core, pattern, cot, hid, weights.transpose(1, 0, 2), proj.reshape(-1, rank), all_tokens
    )
    grad, comp = reduce_all(
        ny, nz, nx, grad.reshape(slots // 2, nz, ny, 2 * dev_rows, blk), comp.reshape(nz, ny, nx, -1, rank)
    )
    start_row = (dp * dev_rows).reshape(1).astype(jnp.int32)
    direction = finish(start_row, pattern, grad, sketch_t.reshape(-1, rank), comp.reshape(-1, rank))
    return input_grad, direction[None]


def solution(mesh):
    return jax.shard_map(
        per_device,
        mesh=mesh,
        in_specs=(
            P("mp", None, None),
            P("dp", "mp"),
            P("dp", "mp"),
            P(None, ("dp", "mp")),
            P(None, "mp", "dp"),
            P("mp", None),
        ),
        out_specs=(P("dp", "mp"), P("mp", "dp", None, None)),
        check_vma=False,
    )
```

```python
import functools
import math

import jax
import jax.numpy as jnp
from jax import lax
from jax.experimental import pallas as pl
from jax.experimental.pallas import tpu as pltpu
from jax.sharding import PartitionSpec as P

NS_STEPS = 5
EPS = 0.0001
F32 = jnp.float32
BF16 = jnp.bfloat16
MIB = 1 << 20
TOGETHER = 4
UNROLL = 8
CHUNKS = 2


def split_bf16(value):
    high = value.astype(BF16)
    low = (value - high.astype(F32)).astype(BF16)
    return high, low


def exact_dot(left, right, dims):
    return lax.dot_general(
        left, right, (dims, ((), ())), precision=lax.Precision.HIGHEST, preferred_element_type=F32
    )


def local_kernel(inv_tokens, core_ref, pat_ref, cot_ref, hid_ref, wgt_ref, proj_ref, back_ref, grad_ref, comp_ref, z_ref, w_ref):
    step = pl.program_id(0)
    core = core_ref[0]
    _, slots, blk = wgt_ref.shape
    mine = slots // 2
    together = hid_ref.shape[1] // blk
    rank = proj_ref.shape[1]
    tokens = back_ref.shape[0]
    per_part = cot_ref.shape[2] // blk
    half_blocks = z_ref.shape[0]
    own = pl.ds(pl.multiple_of(core * tokens, tokens), tokens)

    def cot_block(col, rows=slice(None)):
        lane = pl.multiple_of(lax.rem(col, per_part) * blk, blk)
        return cot_ref[lax.div(col, per_part), rows, pl.ds(lane, blk)]

    @pl.when(step == 0)
    def _():
        @pl.loop(0, half_blocks)
        def _(i):
            z_ref[i] = jnp.zeros(z_ref.shape[1:], F32)

    for b in range(together):
        row = step * together + b
        units = slice(b * blk, (b + 1) * blk)
        cols = [pat_ref[row, k] for k in range(slots)]
        chosen = jnp.concatenate([cot_block(col, own) for col in cols], axis=1)
        w_ref[...] = wgt_ref[units].astype(F32).reshape(blk * slots, blk)
        weight = jnp.concatenate(
            [w_ref[pl.ds(k, blk, stride=slots), :].astype(BF16) for k in range(slots)], axis=1
        )
        back = lax.dot_general(chosen, weight, (((1,), (1,)), ((), ())), preferred_element_type=F32)
        back_ref[:, units] = back.astype(BF16)
        hid = hid_ref[:, units]
        wide = jnp.concatenate([cot_block(pat_ref[row, mine * core + j]) for j in range(mine)], axis=1)
        grad = lax.dot_general(hid, wide, (((0,), (0,)), ((), ())), preferred_element_type=F32)
        grad = grad * inv_tokens
        for j in range(mine):
            grad_ref[j, units, :] = grad[:, j * blk : (j + 1) * blk]
        high, low = split_bf16(proj_ref[units, :])
        both = jnp.dot(hid, jnp.concatenate([high, low], axis=1), preferred_element_type=F32)
        y = both[:, :rank] + both[:, rank:]
        for col in cols:

            @pl.when(lax.rem(col, 2) == core)
            def _(col=col, y=y):
                z_ref[lax.div(col, 2)] += y

    @pl.when(step == pl.num_programs(0) - 1)
    def _():
        @pl.loop(0, half_blocks, unroll=UNROLL)
        def _(i):
            zh, zl = split_bf16(z_ref[i])
            out = lax.dot_general(
                cot_block(2 * i + core),
                jnp.concatenate([zh, zl], axis=1),
                (((0,), (0,)), ((), ())),
                preferred_element_type=F32,
            )
            comp_ref[i] = (out[:, :rank] + out[:, rank:]) * inv_tokens


def local_step(core, pattern, cot, hidden, weights, proj, all_tokens):
    parts, wide_tokens, part_cols = cot.shape
    tokens = wide_tokens // 2
    block_rows, slots = pattern.shape
    blk = weights.shape[2]
    rows = hidden.shape[1]
    rank = proj.shape[1]
    half_blocks = parts * part_cols // blk // 2
    wide = TOGETHER * blk
    grid_spec = pltpu.PrefetchScalarGridSpec(
        num_scalar_prefetch=2,
        grid=(block_rows // TOGETHER,),
        in_specs=[
            pl.BlockSpec((parts, wide_tokens, part_cols), lambda r, *_: (0, 0, 0), pipeline_mode=pl.Buffered(1)),
            pl.BlockSpec((wide_tokens, wide), lambda r, *_: (0, r)),
            pl.BlockSpec((wide, slots, blk), lambda r, *_: (r, 0, 0)),
            pl.BlockSpec((wide, rank), lambda r, *_: (r, 0)),
        ],
        out_specs=[
            pl.BlockSpec((tokens, wide), lambda r, *_: (0, r)),
            pl.BlockSpec((slots // 2, wide, blk), lambda r, *_: (0, r, 0)),
            pl.BlockSpec((half_blocks, blk, rank), lambda r, *_: (0, 0, 0), pipeline_mode=pl.Buffered(1)),
        ],
        scratch_shapes=[pltpu.VMEM((half_blocks, wide_tokens, rank), F32), pltpu.VMEM((blk * slots, blk), F32)],
    )
    return pl.pallas_call(
        functools.partial(local_kernel, 1.0 / all_tokens),
        grid_spec=grid_spec,
        out_shape=(
            jax.ShapeDtypeStruct((tokens, rows), BF16),
            jax.ShapeDtypeStruct((slots // 2, rows, blk), F32),
            jax.ShapeDtypeStruct((half_blocks, blk, rank), F32),
        ),
        compiler_params=pltpu.CompilerParams(vmem_limit_bytes=56 * MIB),
        cost_estimate=pl.CostEstimate(flops=6_000_000_000, bytes_accessed=36_000_000, transcendentals=0),
        name="local_step",
    )(core, pattern, cot, hidden, weights, proj)


class Wires:
    def __init__(self, send_sems, recv_sems, local_sems):
        self.send_sems, self.recv_sems, self.local_sems = send_sems, recv_sems, local_sems
        self.used = 0
        self.locals = 0
        self.sent = []

    def send(self, source, target, device):
        copy = pltpu.make_async_remote_copy(
            src_ref=source,
            dst_ref=target,
            send_sem=self.send_sems.at[self.used],
            recv_sem=self.recv_sems.at[self.used],
            device_id=device,
            device_id_type=pl.DeviceIdType.MESH,
        )
        self.used += 1
        copy.start()
        self.sent.append(copy)
        return copy

    def keep(self, source, target):
        copy = pltpu.make_async_copy(source, target, self.local_sems.at[self.locals])
        self.locals += 1
        copy.start()
        return copy

    def drain(self):
        for copy in self.sent:
            copy.wait_send()


def received(*copies):
    for copy in copies:
        copy.wait_recv()


class Place:
    def __init__(self, ny, nz, nx):
        self.n = {"x": nx, "y": ny, "z": nz, "c": 2}
        d = lax.axis_index("dp")
        self.at = {
            "x": lax.axis_index("mp"),
            "c": lax.rem(d, 2),
            "y": lax.rem(lax.div(d, 2), ny),
            "z": lax.div(d, 2 * ny),
        }

    def shift(self, axis, by):
        n = self.n[axis]
        return lax.rem(self.at[axis] + (by % n), n)

    def device(self, axis, by):
        at = dict(self.at)
        at[axis] = self.shift(axis, by)
        return ((at["z"] * self.n["y"] + at["y"]) * 2 + at["c"], at["x"])


def meet(devices):
    barrier = pltpu.get_barrier_semaphore()
    for device in devices:
        pl.semaphore_signal(barrier, inc=1, device_id=device, device_id_type=pl.DeviceIdType.MESH)
    pl.semaphore_wait(barrier, len(devices))


def gather_kernel(ny, nz, nx, cot, hid, proj, sk, cot_o, hid_o, proj_o, sk_o, cot_v, hid_v, proj_v, sk_v, send_sems, recv_sems, local_sems):
    here = Place(ny, nz, nx)
    x, y, z, c = (here.at[name] for name in "xyzc")
    wires = Wires(send_sems, recv_sems, local_sems)
    partners = [here.device("x", j) for j in range(1, nx)] + [here.device("y", j) for j in range(1, ny)]
    partners += [here.device("z", 1), here.device("z", -1), here.device("c", 1)]
    sib = here.device("c", 1)
    loads = [wires.keep(a, b) for a, b in ((sk, sk_v), (proj, proj_v), (cot, cot_v), (hid, hid_v))]
    meet(partners)
    targets = (sk_o.at[z, y, c, x], proj_o.at[z, y, c], cot_o.at[x, c], hid_o.at[c])
    rows = cot.shape[0] // 2
    top, bottom = pl.ds(0, rows), pl.ds(rows, rows)
    sk_x = [wires.send(sk, sk_o.at[z, y, c, x], here.device("x", j)) for j in range(1, nx)]
    proj_y = [wires.send(proj, proj_o.at[z, y, c], here.device("y", j)) for j in range(1, ny)]
    right, left = here.device("x", 1), here.device("x", -1)

    def cot_send(rows_at, device):
        return wires.send(cot.at[rows_at], cot_o.at[x, c, rows_at], device)

    def cot_pass(part, rows_at, device):
        return wires.send(cot_o.at[part, c, rows_at], cot_o.at[part, c, rows_at], device)

    r_top, l_bottom = cot_send(top, right), cot_send(bottom, left)
    r_bottom, l_top = cot_send(bottom, right), cot_send(top, left)
    from_sib = [wires.send(hid, hid_o.at[c], sib), wires.send(cot, cot_o.at[x, c], sib)]

    keeps = []
    for load, value, target in zip(loads, (sk_v, proj_v, cot_v, hid_v), targets):
        load.wait()
        keeps.append(wires.keep(value, target))
    keep_sk, keep_proj, keep_cot, keep_hid = keeps
    keep_sk.wait()
    received(*sk_x)
    sk_y = [
        wires.send(sk_o.at[z, y, c], sk_o.at[z, y, c], here.device("y", j)) for j in range(1, ny)
    ]
    keep_proj.wait()
    received(*proj_y)

    up, down = here.device("z", 1), here.device("z", -1)

    def z_pass(ref, layer, device, ys=slice(None)):
        view = ref.at[layer, ys, c]
        return wires.send(view, view, device)

    arrays = (proj_o, sk_o)
    low, high = pl.ds(0, ny // 2), pl.ds(ny // 2, ny // 2)
    going_up, going_down = [z_pass(proj_o, z, up)], [z_pass(proj_o, z, down)]
    from_sib.append(z_pass(proj_o, z, sib))
    received(*sk_y)
    going_up.append(z_pass(sk_o, z, up))
    going_down.append(z_pass(sk_o, z, down))
    from_sib.append(z_pass(sk_o, z, sib))

    def z_step(distance, going_up, going_down):
        below, above = here.shift("z", -distance), here.shift("z", distance)
        next_up, next_down = [], []
        last = distance == nz // 2
        for moved, layer, device, part, nexts in (
            (going_up, below, up, low, next_up),
            (going_down, above, down, high, next_down),
        ):
            for copy, ref in zip(moved, arrays):
                received(copy)
                if not last:
                    ys = part if distance + 1 == nz // 2 else slice(None)
                    nexts.append(z_pass(ref, layer, device, ys))
                from_sib.append(z_pass(ref, layer, sib, part if last else slice(None)))
        return next_up, next_down

    left_part, right_part, far_part = here.shift("x", -1), here.shift("x", 1), here.shift("x", 2)

    def cot_first():
        received(r_top)
        far_top = cot_pass(left_part, top, right)
        from_sib.append(cot_pass(left_part, top, sib))
        received(l_bottom)
        far_bottom = cot_pass(right_part, bottom, left)
        from_sib.append(cot_pass(right_part, bottom, sib))
        return far_top, far_bottom

    for distance in range(1, nz // 2 + 1):
        if distance == 2:
            far_top, far_bottom = cot_first()
        if distance == 3:
            received(r_bottom)
            from_sib.append(cot_pass(left_part, bottom, sib))
            received(l_top)
            from_sib.append(cot_pass(right_part, top, sib))
        going_up, going_down = z_step(distance, going_up, going_down)
    received(far_top)
    from_sib.append(cot_pass(far_part, top, sib))
    received(far_bottom)
    from_sib.append(cot_pass(far_part, bottom, sib))
    keep_cot.wait()
    keep_hid.wait()
    received(*from_sib)
    wires.drain()


def gather(ny, nz, nx, cot, hid, proj, sk):
    any_spec = pl.BlockSpec(memory_space=pl.ANY)
    copies = 80
    return pl.pallas_call(
        functools.partial(gather_kernel, ny, nz, nx),
        in_specs=[any_spec] * 4,
        out_specs=[any_spec] * 4,
        out_shape=(
            jax.ShapeDtypeStruct((nx, 2) + cot.shape, cot.dtype),
            jax.ShapeDtypeStruct((2,) + hid.shape, hid.dtype),
            jax.ShapeDtypeStruct((nz, ny, 2) + proj.shape, proj.dtype),
            jax.ShapeDtypeStruct((nz, ny, 2, nx) + sk.shape, sk.dtype),
        ),
        scratch_shapes=[
            pltpu.VMEM(cot.shape, cot.dtype),
            pltpu.VMEM(hid.shape, hid.dtype),
            pltpu.VMEM(proj.shape, proj.dtype),
            pltpu.VMEM(sk.shape, sk.dtype),
            pltpu.SemaphoreType.DMA((copies,)),
            pltpu.SemaphoreType.DMA((copies,)),
            pltpu.SemaphoreType.DMA((8,)),
        ],
        compiler_params=pltpu.CompilerParams(collective_id=1, has_side_effects=True),
        cost_estimate=pl.CostEstimate(flops=0, bytes_accessed=60_000_000, transcendentals=0),
        name="gather",
    )(cot, hid, proj, sk)


def add_into(target, index, source, loop):
    at = index.index(None)

    @pl.loop(0, loop)
    def _(i):
        place = tuple(index[:at]) + (i,) + tuple(index[at + 1 :])
        target[place] = target[place] + source[i]


def reduce_kernel(
    ny, nz, nx, grad, comp, grad_o, comp_o, xg, xc, ya, za, zb, yb, cx, cy, cz, send_sems, recv_sems, local_sems
):
    here = Place(ny, nz, nx)
    x, y, z, c = (here.at[name] for name in "xyzc")
    wires = Wires(send_sems, recv_sems, local_sems)
    keep_comp = wires.keep(comp, xc)
    keep_grad = wires.keep(grad, xg)
    sib = here.device("c", 1)
    partners = [here.device("x", j) for j in range(1, nx)] + [here.device("y", j) for j in range(1, ny)]
    partners += [here.device("z", j) for j in range(1, nz)] + [sib]
    meet(partners)
    xp, xm = here.device("x", 1), here.device("x", -1)
    yp, ym = here.device("y", 1), here.device("y", -1)
    zp, zm = here.device("z", 1), here.device("z", -1)
    x1, x2, x3 = (here.shift("x", j) for j in (1, 2, 3))
    y1, y2, y3 = (here.shift("y", j) for j in (1, 2, 3))
    send = wires.send
    zlow, zhigh = pl.ds(0, nz // 2), pl.ds(nz // 2, nz // 2)

    chunk_rows = comp.shape[3] // CHUNKS
    from_sib = []

    class Chunk:
        def __init__(self, index):
            self.rows = pl.ds(index * chunk_rows, chunk_rows)

        def start(self):
            r = self.rows
            self.far = (
                send(xc.at[zlow, :, x2, r], cx.at[0, zlow, :, r], xp),
                send(xc.at[zhigh, :, x2, r], cx.at[1, zhigh, :, r], xm),
            )
            self.near = [
                send(xc.at[zhigh, :, x1, r], cx.at[2, zhigh, :, r], xp),
                send(xc.at[zlow, :, x3, r], cx.at[3, zlow, :, r], xm),
            ]

        def middle(self):
            r = self.rows
            received(self.far[0])

            @pl.loop(0, nz // 2)
            def _(i):
                xc[i, :, x1, r] = xc[i, :, x1, r] + cx[0, i, :, r]

            self.near.append(send(xc.at[zlow, :, x1, r], cx.at[2, zlow, :, r], xp))
            received(self.far[1])

            @pl.loop(nz // 2, nz)
            def _(i):
                xc[i, :, x3, r] = xc[i, :, x3, r] + cx[1, i, :, r]

            self.near.append(send(xc.at[zhigh, :, x3, r], cx.at[3, zhigh, :, r], xm))

        def along_y(self):
            r = self.rows
            received(*self.near)

            @pl.loop(0, nz)
            def _(i):
                xc[i, :, x, r] = xc[i, :, x, r] + cx[2, i, :, r] + cx[3, i, :, r]

            self.moved = [
                send(xc.at[:, here.shift("y", j), x, r], cy.at[j - 1, :, r], here.device("y", j)) for j in range(1, ny)
            ]

        def along_z(self):
            r = self.rows
            received(*self.moved)

            @pl.loop(0, nz)
            def _(i):
                xc[i, y, x, r] = xc[i, y, x, r] + (cy[0, i, r] + cy[1, i, r] + cy[2, i, r])

            self.moved = [
                send(xc.at[here.shift("z", j), y, x, r], cz.at[j - 1, r], here.device("z", j)) for j in range(1, nz)
            ]

        def total(self):
            r = self.rows
            received(*self.moved)
            total = xc[z, y, x, r]
            for j in range(nz - 1):
                total = total + cz[j, r]
            comp_o[z, y, c, x, r] = total
            mine = comp_o.at[z, y, c, x, r]
            self.moved = [send(mine, mine, here.device("z", j)) for j in range(1, nz)]

        def back_y(self):
            received(*self.moved)
            column = comp_o.at[:, y, c, x, self.rows]
            self.moved = [send(column, column, here.device("y", j)) for j in range(1, ny)]

        def copy_to(self, layers, at, device):
            part = comp_o.at[layers, :, c, at, self.rows]
            return send(part, part, device)

        def back_x(self):
            received(*self.moved)
            every = slice(None)
            self.moved = [self.copy_to(every, x, xp), self.copy_to(every, x, xm)]
            from_sib.append(self.copy_to(every, x, sib))

        def back_far(self):
            every = slice(None)
            received(self.moved[0])
            far = [self.copy_to(zlow, x3, xp)]
            received(self.moved[1])
            far.append(self.copy_to(zhigh, x1, xm))
            self.moved = far
            for at in (x3, x1):
                from_sib.append(self.copy_to(every, at, sib))

        def finish(self):
            for copy, layers in zip(self.moved, (zlow, zhigh)):
                received(copy)
                from_sib.append(self.copy_to(layers, x2, sib))

    keep_comp.wait()
    first, second = Chunk(0), Chunk(1)
    first.start()
    keep_grad.wait()
    a_far = (send(xg.at[0, :, y2], ya.at[0], yp), send(xg.at[1, :, y2], ya.at[1], ym))
    b_dist = nz // 2

    def ring_send(source, arrived, slots, dist):
        plus, minus = here.shift("z", dist), here.shift("z", -dist)
        if dist == b_dist:
            return (
                send(source(slots[0], plus), arrived.at[0, dist - 1, 0], zp),
                send(source(slots[1], minus), arrived.at[1, dist - 1, 1], zm),
            )
        both = pl.ds(slots[0], 2)
        return (
            send(source(both, plus), arrived.at[0, dist - 1], zp),
            send(source(both, minus), arrived.at[1, dist - 1], zm),
        )

    def b_send(dist):
        return ring_send(lambda s, layer: xg.at[s, layer], zb, (2, 3), dist)

    def a_send(dist):
        return ring_send(lambda s, layer: xg.at[s, layer, y], za, (0, 1), dist)

    def arrived_slots(dist, side):
        return (side,) if dist == b_dist else (0, 1)

    def b_step(dist, moving):
        for side in (0, 1):
            received(moving[side])
            layer = here.shift("z", (dist - 1) * (1 - 2 * side))
            for s in arrived_slots(dist, side):
                add_into(xg, [2 + s, layer, None], zb.at[side, dist - 1, s], ny)
        return b_send(dist - 1) if dist > 1 else None

    def a_step(dist, moving):
        for side in (0, 1):
            received(moving[side])
            layer = here.shift("z", (dist - 1) * (1 - 2 * side))
            for s in arrived_slots(dist, side):
                xg[s, layer, y] = xg[s, layer, y] + za[side, dist - 1, s]
        return a_send(dist - 1) if dist > 1 else None

    b_moving = b_send(b_dist)
    a_near = [send(xg.at[1, :, y1], ya.at[2], yp), send(xg.at[0, :, y3], ya.at[3], ym)]
    first.middle()
    second.start()
    b_moving = b_step(b_dist, b_moving)
    second.middle()
    received(a_far[0])
    add_into(xg, [0, None, y1], ya.at[0], nz)
    a_near.append(send(xg.at[0, :, y1], ya.at[4], yp))
    received(a_far[1])
    add_into(xg, [1, None, y3], ya.at[1], nz)
    a_near.append(send(xg.at[1, :, y3], ya.at[5], ym))
    first.along_y()
    b_moving = b_step(3, b_moving)
    first.along_z()
    second.along_y()
    first.total()
    second.along_z()
    first.back_y()
    b_moving = b_step(2, b_moving)
    second.total()
    first.back_x()
    second.back_y()
    received(*a_near)

    @pl.loop(0, nz)
    def _(i):
        xg[0, i, y] = xg[0, i, y] + ya[4, i] + ya[3, i]
        xg[1, i, y] = xg[1, i, y] + ya[2, i] + ya[5, i]

    a_moving = a_send(b_dist)
    second.back_x()
    b_step(1, b_moving)
    b2_far = (send(xg.at[2, z, y2], yb.at[0], yp), send(xg.at[3, z, y2], yb.at[1], ym))
    b2_near = [send(xg.at[3, z, y1], yb.at[2], yp), send(xg.at[2, z, y3], yb.at[3], ym)]
    first.back_far()
    a_moving = a_step(b_dist, a_moving)
    received(b2_far[0])
    xg[2, z, y1] = xg[2, z, y1] + yb[0]
    b2_near.append(send(xg.at[2, z, y1], yb.at[4], yp))
    received(b2_far[1])
    xg[3, z, y3] = xg[3, z, y3] + yb[1]
    b2_near.append(send(xg.at[3, z, y3], yb.at[5], ym))
    a_moving = a_step(3, a_moving)
    second.back_far()
    a_moving = a_step(2, a_moving)
    first.finish()
    received(*b2_near)
    xg[2, z, y] = xg[2, z, y] + yb[4] + yb[3]
    xg[3, z, y] = xg[3, z, y] + yb[2] + yb[5]
    a_step(1, a_moving)
    units = grad_o.shape[1]
    theirs = pl.ds(pl.multiple_of((1 - c) * units, 8), units)
    swap = send(xg.at[:, z, y, theirs], grad_o.at[pl.ds(c * 4, 4)], sib)
    for s in range(4):
        grad_o[c * 4 + s] = xg[s, z, y, pl.ds(pl.multiple_of(c * units, 8), units)]
    second.finish()
    received(swap, *from_sib)
    wires.drain()


def reduce_all(ny, nz, nx, grad, comp):
    slots, _, _, units, blk = grad.shape
    piece = comp.shape[3:]
    any_spec = pl.BlockSpec(memory_space=pl.ANY)
    vmem = pl.BlockSpec(memory_space=pltpu.VMEM)
    copies = 112
    return pl.pallas_call(
        functools.partial(reduce_kernel, ny, nz, nx),
        in_specs=[any_spec] * 2,
        out_specs=[vmem, vmem],
        out_shape=(
            jax.ShapeDtypeStruct((2 * slots, units // 2, blk), F32),
            jax.ShapeDtypeStruct((nz, ny, 2, nx) + piece, F32),
        ),
        scratch_shapes=[
            pltpu.VMEM(grad.shape, F32),
            pltpu.VMEM(comp.shape, F32),
            pltpu.VMEM((6, nz, units, blk), F32),
            pltpu.VMEM((2, nz // 2, 2, units, blk), F32),
            pltpu.VMEM((2, nz // 2, 2, ny, units, blk), F32),
            pltpu.VMEM((6, units, blk), F32),
            pltpu.VMEM((4, nz, ny) + piece, F32),
            pltpu.VMEM((ny - 1, nz) + piece, F32),
            pltpu.VMEM((nz - 1,) + piece, F32),
            pltpu.SemaphoreType.DMA((copies,)),
            pltpu.SemaphoreType.DMA((copies,)),
            pltpu.SemaphoreType.DMA((2,)),
        ],
        compiler_params=pltpu.CompilerParams(
            collective_id=2, has_side_effects=True, vmem_limit_bytes=48 * MIB
        ),
        cost_estimate=pl.CostEstimate(flops=0, bytes_accessed=100_000_000, transcendentals=0),
        name="reduce",
    )(grad, comp)


def identity(n):
    rows = lax.broadcasted_iota(jnp.int32, (n, n), 0)
    cols = lax.broadcasted_iota(jnp.int32, (n, n), 1)
    return jnp.where(rows == cols, 1.0, 0.0).astype(F32)


def mul(left, right):
    return exact_dot(left, right, ((1,), (0,)))


def spd_inverse(mat, eye):
    n = mat.shape[0]
    bound = jnp.max(jnp.sum(jnp.abs(mat), axis=1, keepdims=True))
    start = eye * (2.0 / (bound + math.sqrt(EPS)))

    def unfinished(state):
        count, previous, residual, _ = state
        return (count < 100) & (residual > 2e-6) & ((residual < 0.5 * previous) | (residual > 0.1))

    def body(state):
        count, _, residual, guess = state
        gap = eye - mul(mat, guess)
        guess = guess + mul(guess, gap)
        return count + 1, residual, jnp.max(jnp.abs(gap)), guess

    state = lax.while_loop(unfinished, body, (0, jnp.float32(4.0), jnp.float32(2.0), start))
    return state[3]


def mixing_of(gram):
    n = gram.shape[0]
    eye = identity(n)
    shifted = gram + EPS * eye
    total = jnp.sum(jnp.sum(shifted * shifted, axis=1, keepdims=True), axis=0, keepdims=True)
    frob = jnp.sqrt(total)
    root = shifted / frob
    middle = 1.5 * eye - 0.5 * root
    root = mul(root, middle)
    inverse = middle
    for _ in range(NS_STEPS - 1):
        middle = 1.5 * eye - 0.5 * mul(inverse, root)
        root = mul(root, middle)
        inverse = mul(middle, inverse)
    half = 0.5 * jnp.sqrt(frob) * (root + root.T) + math.sqrt(EPS) * eye
    half_inv = spd_inverse(half, eye)
    return -mul(inverse, half_inv) / (math.sqrt(EPS) * jnp.sqrt(frob))


def finish_kernel(row_ref, pat_ref, grad_ref, sketch_ref, comp_ref, out_ref, gram_ref, sel_ref):
    slots, rows, blk = grad_ref.shape
    rank = comp_ref.shape[1]
    width = comp_ref.shape[0]
    chunk = 1024
    gram_ref[...] = jnp.zeros_like(gram_ref)

    @pl.loop(0, width // chunk)
    def _(i):
        at = pl.ds(pl.multiple_of(i * chunk, chunk), chunk)
        st = jnp.concatenate([sketch_ref[at, :], comp_ref[at, :]], axis=1)
        high, low = split_bf16(st)
        dims = (((0,), (0,)), ((), ()))
        gram_ref[0] += lax.dot_general(high, high, dims, preferred_element_type=F32)
        gram_ref[1] += lax.dot_general(high, low, dims, preferred_element_type=F32)

    cross = gram_ref[1]
    mixing = mixing_of(gram_ref[0] + (cross + cross.T))
    start = row_ref[0]
    first = lax.div(start, blk)
    last = pat_ref.shape[0] - 1
    grad = jnp.concatenate([grad_ref[k] for k in range(slots)], axis=1)
    block_of = lax.div(start + lax.broadcasted_iota(jnp.int32, (rows, 1), 0), blk)
    projected = None
    for g in range(2):
        brow = jnp.minimum(first + g, last)
        for k in range(slots):
            col = pl.multiple_of(pat_ref[brow, k] * blk, blk)
            here = pl.ds(k * blk, blk)
            sel_ref[g, here, :rank] = sketch_ref[pl.ds(col, blk), :]
            sel_ref[g, here, rank:] = comp_ref[pl.ds(col, blk), :]
        part = mul(grad, sel_ref[g])
        projected = part if projected is None else jnp.where(block_of == first + g, part, projected)
    mixed = mul(projected, mixing)
    corr = exact_dot(mixed, sel_ref[0], ((1,), (1,)))
    corr1 = exact_dot(mixed, sel_ref[1], ((1,), (1,)))
    corr = jnp.where(block_of == first + 1, corr1, corr)
    result = grad * (1.0 / math.sqrt(EPS)) + corr
    for k in range(slots):
        out_ref[:, k, :] = result[:, k * blk : (k + 1) * blk]


def finish(start_row, pattern, grad, sketch_t, comp_t):
    slots, rows, blk = grad.shape
    rank = comp_t.shape[1]
    smem = pl.BlockSpec(memory_space=pltpu.SMEM)
    vmem = pl.BlockSpec(memory_space=pltpu.VMEM)
    return pl.pallas_call(
        finish_kernel,
        in_specs=[smem, smem, vmem, vmem, vmem],
        out_specs=vmem,
        out_shape=jax.ShapeDtypeStruct((rows, slots, blk), F32),
        scratch_shapes=[
            pltpu.VMEM((2, 2 * rank, 2 * rank), F32),
            pltpu.VMEM((2, slots * blk, 2 * rank), F32),
        ],
        compiler_params=pltpu.CompilerParams(vmem_limit_bytes=40 * MIB),
        cost_estimate=pl.CostEstimate(flops=5_000_000_000, bytes_accessed=9_000_000, transcendentals=0),
        name="finish",
    )(start_row, pattern, grad, sketch_t, comp_t)


def per_device(weights, hidden, cotangent, sketch, projection, pattern):
    rank = sketch.shape[0]
    slots, blk = weights.shape[1:]
    dp_size = lax.axis_size("dp")
    nx = lax.axis_size("mp")
    ny = 4
    nz = dp_size // (2 * ny)
    dev_rows = weights.shape[0] // dp_size
    all_tokens = hidden.shape[0] * dp_size
    dp = lax.axis_index("dp")
    core = lax.rem(dp, 2).reshape(1).astype(jnp.int32)
    cot, hid, proj, sketch_t = gather(
        ny, nz, nx, cotangent, hidden, projection.reshape(rank, dev_rows).T, sketch.T
    )
    cot = cot.reshape(nx, -1, cotangent.shape[1])
    hid = hid.reshape(-1, hidden.shape[1])
    input_grad, grad, comp = local_step(
        core, pattern, cot, hid, weights, proj.reshape(-1, rank), all_tokens
    )
    grad, comp = reduce_all(
        ny, nz, nx, grad.reshape(slots // 2, nz, ny, 2 * dev_rows, blk), comp.reshape(nz, ny, nx, -1, rank)
    )
    start_row = (dp * dev_rows).reshape(1).astype(jnp.int32)
    direction = finish(start_row, pattern, grad, sketch_t.reshape(-1, rank), comp.reshape(-1, rank))
    return input_grad, direction[None]


def solution(mesh):
    return jax.shard_map(
        per_device,
        mesh=mesh,
        in_specs=(
            P("mp", None, None),
            P("dp", "mp"),
            P("dp", "mp"),
            P(None, ("dp", "mp")),
            P(None, "mp", "dp"),
            P("mp", None),
        ),
        out_specs=(P("dp", "mp"), P("mp", "dp", None, None)),
        check_vma=False,
    )
```

```python
import functools
import math

import jax
import jax.numpy as jnp
from jax import lax
from jax.experimental import pallas as pl
from jax.experimental.pallas import tpu as pltpu
from jax.sharding import PartitionSpec as P

NS_STEPS = 5
EPS = 0.0001
F32 = jnp.float32
BF16 = jnp.bfloat16
MIB = 1 << 20
TOGETHER = 4
UNROLL = 8
CHUNKS = 2


def split_bf16(value):
    high = value.astype(BF16)
    low = (value - high.astype(F32)).astype(BF16)
    return high, low


def exact_dot(left, right, dims):
    return lax.dot_general(
        left, right, (dims, ((), ())), precision=lax.Precision.HIGHEST, preferred_element_type=F32
    )


def local_kernel(inv_tokens, core_ref, pat_ref, cot_ref, hid_ref, wgt_ref, proj_ref, back_ref, grad_ref, comp_ref, z_ref, w_ref):
    step = pl.program_id(0)
    core = core_ref[0]
    _, slots, blk = wgt_ref.shape
    mine = slots // 2
    together = hid_ref.shape[1] // blk
    rank = proj_ref.shape[1]
    tokens = back_ref.shape[0]
    per_part = cot_ref.shape[2] // blk
    half_blocks = z_ref.shape[0]
    own = pl.ds(pl.multiple_of(core * tokens, tokens), tokens)

    def cot_block(col, rows=slice(None)):
        lane = pl.multiple_of(lax.rem(col, per_part) * blk, blk)
        return cot_ref[lax.div(col, per_part), rows, pl.ds(lane, blk)]

    @pl.when(step == 0)
    def _():
        @pl.loop(0, half_blocks)
        def _(i):
            z_ref[i] = jnp.zeros(z_ref.shape[1:], F32)

    for b in range(together):
        row = step * together + b
        units = slice(b * blk, (b + 1) * blk)
        cols = [pat_ref[row, k] for k in range(slots)]
        chosen = jnp.concatenate([cot_block(col, own) for col in cols], axis=1)
        w_ref[...] = wgt_ref[units].astype(F32).reshape(blk * slots, blk)
        weight = jnp.concatenate(
            [w_ref[pl.ds(k, blk, stride=slots), :].astype(BF16) for k in range(slots)], axis=1
        )
        back = lax.dot_general(chosen, weight, (((1,), (1,)), ((), ())), preferred_element_type=F32)
        back_ref[:, units] = back.astype(BF16)
        hid = hid_ref[:, units]
        wide = jnp.concatenate([cot_block(pat_ref[row, mine * core + j]) for j in range(mine)], axis=1)
        grad = lax.dot_general(hid, wide, (((0,), (0,)), ((), ())), preferred_element_type=F32)
        grad = grad * inv_tokens
        for j in range(mine):
            grad_ref[j, units, :] = grad[:, j * blk : (j + 1) * blk]
        high, low = split_bf16(proj_ref[units, :])
        both = jnp.dot(hid, jnp.concatenate([high, low], axis=1), preferred_element_type=F32)
        y = both[:, :rank] + both[:, rank:]
        for col in cols:

            @pl.when(lax.rem(col, 2) == core)
            def _(col=col, y=y):
                z_ref[lax.div(col, 2)] += y

    @pl.when(step == pl.num_programs(0) - 1)
    def _():
        @pl.loop(0, half_blocks, unroll=UNROLL)
        def _(i):
            zh, zl = split_bf16(z_ref[i])
            out = lax.dot_general(
                cot_block(2 * i + core),
                jnp.concatenate([zh, zl], axis=1),
                (((0,), (0,)), ((), ())),
                preferred_element_type=F32,
            )
            comp_ref[i] = (out[:, :rank] + out[:, rank:]) * inv_tokens


def local_step(core, pattern, cot, hidden, weights, proj, all_tokens):
    parts, wide_tokens, part_cols = cot.shape
    tokens = wide_tokens // 2
    block_rows, slots = pattern.shape
    blk = weights.shape[2]
    rows = hidden.shape[1]
    rank = proj.shape[1]
    half_blocks = parts * part_cols // blk // 2
    wide = TOGETHER * blk
    grid_spec = pltpu.PrefetchScalarGridSpec(
        num_scalar_prefetch=2,
        grid=(block_rows // TOGETHER,),
        in_specs=[
            pl.BlockSpec((parts, wide_tokens, part_cols), lambda r, *_: (0, 0, 0), pipeline_mode=pl.Buffered(1)),
            pl.BlockSpec((wide_tokens, wide), lambda r, *_: (0, r)),
            pl.BlockSpec((wide, slots, blk), lambda r, *_: (r, 0, 0)),
            pl.BlockSpec((wide, rank), lambda r, *_: (r, 0)),
        ],
        out_specs=[
            pl.BlockSpec((tokens, wide), lambda r, *_: (0, r)),
            pl.BlockSpec((slots // 2, wide, blk), lambda r, *_: (0, r, 0)),
            pl.BlockSpec((half_blocks, blk, rank), lambda r, *_: (0, 0, 0), pipeline_mode=pl.Buffered(1)),
        ],
        scratch_shapes=[pltpu.VMEM((half_blocks, wide_tokens, rank), F32), pltpu.VMEM((blk * slots, blk), F32)],
    )
    return pl.pallas_call(
        functools.partial(local_kernel, 1.0 / all_tokens),
        grid_spec=grid_spec,
        out_shape=(
            jax.ShapeDtypeStruct((tokens, rows), BF16),
            jax.ShapeDtypeStruct((slots // 2, rows, blk), F32),
            jax.ShapeDtypeStruct((half_blocks, blk, rank), F32),
        ),
        compiler_params=pltpu.CompilerParams(vmem_limit_bytes=56 * MIB),
        cost_estimate=pl.CostEstimate(flops=6_000_000_000, bytes_accessed=36_000_000, transcendentals=0),
        name="local_step",
    )(core, pattern, cot, hidden, weights, proj)


class Wires:
    def __init__(self, send_sems, recv_sems, local_sems):
        self.send_sems, self.recv_sems, self.local_sems = send_sems, recv_sems, local_sems
        self.used = 0
        self.locals = 0
        self.sent = []

    def send(self, source, target, device):
        copy = pltpu.make_async_remote_copy(
            src_ref=source,
            dst_ref=target,
            send_sem=self.send_sems.at[self.used],
            recv_sem=self.recv_sems.at[self.used],
            device_id=device,
            device_id_type=pl.DeviceIdType.MESH,
        )
        self.used += 1
        copy.start()
        self.sent.append(copy)
        return copy

    def keep(self, source, target):
        copy = pltpu.make_async_copy(source, target, self.local_sems.at[self.locals])
        self.locals += 1
        copy.start()
        return copy

    def drain(self):
        for copy in self.sent:
            copy.wait_send()


def received(*copies):
    for copy in copies:
        copy.wait_recv()


class Place:
    def __init__(self, ny, nz, nx):
        self.n = {"x": nx, "y": ny, "z": nz, "c": 2}
        d = lax.axis_index("dp")
        self.at = {
            "x": lax.axis_index("mp"),
            "c": lax.rem(d, 2),
            "y": lax.rem(lax.div(d, 2), ny),
            "z": lax.div(d, 2 * ny),
        }

    def shift(self, axis, by):
        n = self.n[axis]
        return lax.rem(self.at[axis] + (by % n), n)

    def device(self, axis, by):
        at = dict(self.at)
        at[axis] = self.shift(axis, by)
        return ((at["z"] * self.n["y"] + at["y"]) * 2 + at["c"], at["x"])


def meet(devices):
    barrier = pltpu.get_barrier_semaphore()
    for device in devices:
        pl.semaphore_signal(barrier, inc=1, device_id=device, device_id_type=pl.DeviceIdType.MESH)
    pl.semaphore_wait(barrier, len(devices))


def gather_kernel(ny, nz, nx, cot, hid, proj, sk, cot_o, hid_o, proj_o, sk_o, cot_v, hid_v, proj_v, sk_v, send_sems, recv_sems, local_sems):
    here = Place(ny, nz, nx)
    x, y, z, c = (here.at[name] for name in "xyzc")
    wires = Wires(send_sems, recv_sems, local_sems)
    partners = [here.device("x", j) for j in range(1, nx)] + [here.device("y", j) for j in range(1, ny)]
    partners += [here.device("z", 1), here.device("z", -1), here.device("c", 1)]
    sib = here.device("c", 1)
    loads = [wires.keep(a, b) for a, b in ((sk, sk_v), (proj, proj_v), (cot, cot_v), (hid, hid_v))]
    meet(partners)
    targets = (sk_o.at[z, y, c, x], proj_o.at[z, y, c], cot_o.at[x, c], hid_o.at[c])
    rows = cot.shape[0] // 2
    top, bottom = pl.ds(0, rows), pl.ds(rows, rows)
    sk_x = [wires.send(sk, sk_o.at[z, y, c, x], here.device("x", j)) for j in range(1, nx)]
    proj_y = [wires.send(proj, proj_o.at[z, y, c], here.device("y", j)) for j in range(1, ny)]
    right, left = here.device("x", 1), here.device("x", -1)

    def cot_send(rows_at, device):
        return wires.send(cot.at[rows_at], cot_o.at[x, c, rows_at], device)

    def cot_pass(part, rows_at, device):
        return wires.send(cot_o.at[part, c, rows_at], cot_o.at[part, c, rows_at], device)

    r_top, l_bottom = cot_send(top, right), cot_send(bottom, left)
    r_bottom, l_top = cot_send(bottom, right), cot_send(top, left)
    from_sib = [wires.send(hid, hid_o.at[c], sib), wires.send(cot, cot_o.at[x, c], sib)]

    keeps = []
    for load, value, target in zip(loads, (sk_v, proj_v, cot_v, hid_v), targets):
        load.wait()
        keeps.append(wires.keep(value, target))
    keep_sk, keep_proj, keep_cot, keep_hid = keeps
    keep_sk.wait()
    received(*sk_x)
    sk_y = [
        wires.send(sk_o.at[z, y, c], sk_o.at[z, y, c], here.device("y", j)) for j in range(1, ny)
    ]
    keep_proj.wait()
    received(*proj_y)

    up, down = here.device("z", 1), here.device("z", -1)

    def z_pass(ref, layer, device, ys=slice(None)):
        view = ref.at[layer, ys, c]
        return wires.send(view, view, device)

    arrays = (proj_o, sk_o)
    low, high = pl.ds(0, ny // 2), pl.ds(ny // 2, ny // 2)
    going_up, going_down = [z_pass(proj_o, z, up)], [z_pass(proj_o, z, down)]
    from_sib.append(z_pass(proj_o, z, sib))
    received(*sk_y)
    going_up.append(z_pass(sk_o, z, up))
    going_down.append(z_pass(sk_o, z, down))
    from_sib.append(z_pass(sk_o, z, sib))

    def z_step(distance, going_up, going_down):
        below, above = here.shift("z", -distance), here.shift("z", distance)
        next_up, next_down = [], []
        last = distance == nz // 2
        for moved, layer, device, part, nexts in (
            (going_up, below, up, low, next_up),
            (going_down, above, down, high, next_down),
        ):
            for copy, ref in zip(moved, arrays):
                received(copy)
                if not last:
                    ys = part if distance + 1 == nz // 2 else slice(None)
                    nexts.append(z_pass(ref, layer, device, ys))
                from_sib.append(z_pass(ref, layer, sib, part if last else slice(None)))
        return next_up, next_down

    left_part, right_part, far_part = here.shift("x", -1), here.shift("x", 1), here.shift("x", 2)

    def cot_first():
        received(r_top)
        far_top = cot_pass(left_part, top, right)
        from_sib.append(cot_pass(left_part, top, sib))
        received(l_bottom)
        far_bottom = cot_pass(right_part, bottom, left)
        from_sib.append(cot_pass(right_part, bottom, sib))
        return far_top, far_bottom

    for distance in range(1, nz // 2 + 1):
        if distance == 2:
            far_top, far_bottom = cot_first()
        if distance == 3:
            received(r_bottom)
            from_sib.append(cot_pass(left_part, bottom, sib))
            received(l_top)
            from_sib.append(cot_pass(right_part, top, sib))
        going_up, going_down = z_step(distance, going_up, going_down)
    received(far_top)
    from_sib.append(cot_pass(far_part, top, sib))
    received(far_bottom)
    from_sib.append(cot_pass(far_part, bottom, sib))
    keep_cot.wait()
    keep_hid.wait()
    received(*from_sib)
    wires.drain()


def gather(ny, nz, nx, cot, hid, proj, sk):
    any_spec = pl.BlockSpec(memory_space=pl.ANY)
    copies = 80
    return pl.pallas_call(
        functools.partial(gather_kernel, ny, nz, nx),
        in_specs=[any_spec] * 4,
        out_specs=[any_spec] * 4,
        out_shape=(
            jax.ShapeDtypeStruct((nx, 2) + cot.shape, cot.dtype),
            jax.ShapeDtypeStruct((2,) + hid.shape, hid.dtype),
            jax.ShapeDtypeStruct((nz, ny, 2) + proj.shape, proj.dtype),
            jax.ShapeDtypeStruct((nz, ny, 2, nx) + sk.shape, sk.dtype),
        ),
        scratch_shapes=[
            pltpu.VMEM(cot.shape, cot.dtype),
            pltpu.VMEM(hid.shape, hid.dtype),
            pltpu.VMEM(proj.shape, proj.dtype),
            pltpu.VMEM(sk.shape, sk.dtype),
            pltpu.SemaphoreType.DMA((copies,)),
            pltpu.SemaphoreType.DMA((copies,)),
            pltpu.SemaphoreType.DMA((8,)),
        ],
        compiler_params=pltpu.CompilerParams(collective_id=1, has_side_effects=True),
        cost_estimate=pl.CostEstimate(flops=0, bytes_accessed=60_000_000, transcendentals=0),
        name="gather",
    )(cot, hid, proj, sk)


def add_into(target, index, source, loop):
    at = index.index(None)

    @pl.loop(0, loop)
    def _(i):
        place = tuple(index[:at]) + (i,) + tuple(index[at + 1 :])
        target[place] = target[place] + source[i]


def reduce_kernel(
    ny, nz, nx, grad, comp, grad_o, comp_o, xg, xc, ya, za, zb, yb, cx, cy, cz, send_sems, recv_sems, local_sems
):
    here = Place(ny, nz, nx)
    x, y, z, c = (here.at[name] for name in "xyzc")
    wires = Wires(send_sems, recv_sems, local_sems)
    keep_comp = wires.keep(comp, xc)
    keep_grad = [wires.keep(grad.at[s], xg.at[s]) for s in (2, 3, 0, 1)]
    sib = here.device("c", 1)
    partners = [here.device("x", j) for j in range(1, nx)] + [here.device("y", j) for j in range(1, ny)]
    partners += [here.device("z", j) for j in range(1, nz)] + [sib]
    meet(partners)
    xp, xm = here.device("x", 1), here.device("x", -1)
    yp, ym = here.device("y", 1), here.device("y", -1)
    zp, zm = here.device("z", 1), here.device("z", -1)
    x1, x2, x3 = (here.shift("x", j) for j in (1, 2, 3))
    y1, y2, y3 = (here.shift("y", j) for j in (1, 2, 3))
    send = wires.send
    zlow, zhigh = pl.ds(0, nz // 2), pl.ds(nz // 2, nz // 2)

    chunk_rows = comp.shape[3] // CHUNKS
    from_sib = []

    class Chunk:
        def __init__(self, index):
            self.rows = pl.ds(index * chunk_rows, chunk_rows)

        def start(self):
            r = self.rows
            self.far = (
                send(xc.at[zlow, :, x2, r], cx.at[0, zlow, :, r], xp),
                send(xc.at[zhigh, :, x2, r], cx.at[1, zhigh, :, r], xm),
            )
            self.near = [
                send(xc.at[zhigh, :, x1, r], cx.at[2, zhigh, :, r], xp),
                send(xc.at[zlow, :, x3, r], cx.at[3, zlow, :, r], xm),
            ]

        def middle(self):
            r = self.rows
            received(self.far[0])

            @pl.loop(0, nz // 2)
            def _(i):
                xc[i, :, x1, r] = xc[i, :, x1, r] + cx[0, i, :, r]

            self.near.append(send(xc.at[zlow, :, x1, r], cx.at[2, zlow, :, r], xp))
            received(self.far[1])

            @pl.loop(nz // 2, nz)
            def _(i):
                xc[i, :, x3, r] = xc[i, :, x3, r] + cx[1, i, :, r]

            self.near.append(send(xc.at[zhigh, :, x3, r], cx.at[3, zhigh, :, r], xm))

        def along_y(self):
            r = self.rows
            received(*self.near)

            @pl.loop(0, nz)
            def _(i):
                xc[i, :, x, r] = xc[i, :, x, r] + cx[2, i, :, r] + cx[3, i, :, r]

            self.moved = [
                send(xc.at[:, here.shift("y", j), x, r], cy.at[j - 1, :, r], here.device("y", j)) for j in range(1, ny)
            ]

        def along_z(self):
            r = self.rows
            received(*self.moved)

            @pl.loop(0, nz)
            def _(i):
                xc[i, y, x, r] = xc[i, y, x, r] + (cy[0, i, r] + cy[1, i, r] + cy[2, i, r])

            self.moved = [
                send(xc.at[here.shift("z", j), y, x, r], cz.at[j - 1, r], here.device("z", j)) for j in range(1, nz)
            ]

        def total(self):
            r = self.rows
            received(*self.moved)
            total = xc[z, y, x, r]
            for j in range(nz - 1):
                total = total + cz[j, r]
            comp_o[z, y, c, x, r] = total
            mine = comp_o.at[z, y, c, x, r]
            self.moved = [send(mine, mine, here.device("z", j)) for j in range(1, nz)]

        def back_y(self):
            received(*self.moved)
            column = comp_o.at[:, y, c, x, self.rows]
            self.moved = [send(column, column, here.device("y", j)) for j in range(1, ny)]

        def copy_to(self, layers, at, device):
            part = comp_o.at[layers, :, c, at, self.rows]
            return send(part, part, device)

        def back_x(self):
            received(*self.moved)
            every = slice(None)
            self.moved = [self.copy_to(every, x, xp), self.copy_to(every, x, xm)]
            from_sib.append(self.copy_to(every, x, sib))

        def back_far(self):
            every = slice(None)
            received(self.moved[0])
            far = [self.copy_to(zlow, x3, xp)]
            received(self.moved[1])
            far.append(self.copy_to(zhigh, x1, xm))
            self.moved = far
            for at in (x3, x1):
                from_sib.append(self.copy_to(every, at, sib))

        def finish(self):
            for copy, layers in zip(self.moved, (zlow, zhigh)):
                received(copy)
                from_sib.append(self.copy_to(layers, x2, sib))

    keep_comp.wait()
    first, second = Chunk(0), Chunk(1)
    first.start()
    class Ring:
        def __init__(self, source, arrived, side, index, add, dist):
            self.source, self.arrived, self.side, self.index, self.add = source, arrived, side, index, add
            self.send(dist)

        def layer(self, dist):
            return here.shift("z", dist if self.side == 0 else -dist)

        def send(self, dist):
            self.dist = dist
            target = self.arrived.at[self.side, dist - 1, self.index]
            self.copy = send(self.source(self.index, self.layer(dist)), target, (zp, zm)[self.side])

        def step(self):
            if self.dist == 0:
                return
            received(self.copy)
            self.add(self.index, self.layer(self.dist - 1), self.side, self.dist - 1)
            if self.dist > 1:
                self.send(self.dist - 1)
            else:
                self.dist = 0

    far_z = nz // 2

    def b_add(index, layer, side, slot_at):
        add_into(xg, [2 + index, layer, None], zb.at[side, slot_at, index], ny)

    def a_add(index, layer, side, slot_at):
        xg[index, layer, y] = xg[index, layer, y] + za[side, slot_at, index]

    def b_ring(side, index, dist):
        return Ring(lambda s, layer: xg.at[2 + s, layer], zb, side, index, b_add, dist)

    def a_ring(side, index, dist):
        return Ring(lambda s, layer: xg.at[s, layer, y], za, side, index, a_add, dist)

    keep_grad[0].wait()
    keep_grad[1].wait()
    b_rings = [b_ring(0, 0, far_z), b_ring(1, 1, far_z), b_ring(0, 1, far_z - 1), b_ring(1, 0, far_z - 1)]
    keep_grad[2].wait()
    keep_grad[3].wait()
    a_far = (send(xg.at[0, :, y2], ya.at[0], yp), send(xg.at[1, :, y2], ya.at[1], ym))
    a_near = [send(xg.at[1, :, y1], ya.at[2], yp), send(xg.at[0, :, y3], ya.at[3], ym)]

    def advance(rings):
        for ring in rings:
            ring.step()

    first.middle()
    second.start()
    advance(b_rings[:2])
    second.middle()
    received(a_far[0])
    add_into(xg, [0, None, y1], ya.at[0], nz)
    a_near.append(send(xg.at[0, :, y1], ya.at[4], yp))
    received(a_far[1])
    add_into(xg, [1, None, y3], ya.at[1], nz)
    a_near.append(send(xg.at[1, :, y3], ya.at[5], ym))
    advance(b_rings[2:])
    first.along_y()
    advance(b_rings[:2])
    first.along_z()
    second.along_y()
    advance(b_rings[2:])
    first.total()
    second.along_z()
    advance(b_rings[:2])
    first.back_y()
    second.total()
    advance(b_rings[2:])
    first.back_x()
    second.back_y()
    received(a_near[2], a_near[1])

    @pl.loop(0, nz)
    def _(i):
        xg[0, i, y] = xg[0, i, y] + ya[4, i] + ya[3, i]

    a_rings = [a_ring(0, 0, far_z), None, None, a_ring(1, 0, far_z - 1)]
    received(a_near[0], a_near[3])

    @pl.loop(0, nz)
    def _(i):
        xg[1, i, y] = xg[1, i, y] + ya[2, i] + ya[5, i]

    a_rings[1:3] = [a_ring(1, 1, far_z), a_ring(0, 1, far_z - 1)]
    second.back_x()
    advance(b_rings[:2])
    b2_far = (send(xg.at[2, z, y2], yb.at[0], yp), send(xg.at[3, z, y2], yb.at[1], ym))
    b2_near = [send(xg.at[3, z, y1], yb.at[2], yp), send(xg.at[2, z, y3], yb.at[3], ym)]
    first.back_far()
    advance(a_rings)
    received(b2_far[0])
    xg[2, z, y1] = xg[2, z, y1] + yb[0]
    b2_near.append(send(xg.at[2, z, y1], yb.at[4], yp))
    received(b2_far[1])
    xg[3, z, y3] = xg[3, z, y3] + yb[1]
    b2_near.append(send(xg.at[3, z, y3], yb.at[5], ym))
    advance(a_rings)
    second.back_far()
    advance(a_rings)
    first.finish()
    received(*b2_near)
    xg[2, z, y] = xg[2, z, y] + yb[4] + yb[3]
    xg[3, z, y] = xg[3, z, y] + yb[2] + yb[5]
    advance(a_rings)
    units = grad_o.shape[1]
    theirs = pl.ds(pl.multiple_of((1 - c) * units, 8), units)
    swap = send(xg.at[:, z, y, theirs], grad_o.at[pl.ds(c * 4, 4)], sib)
    for s in range(4):
        grad_o[c * 4 + s] = xg[s, z, y, pl.ds(pl.multiple_of(c * units, 8), units)]
    second.finish()
    received(swap, *from_sib)
    wires.drain()


def reduce_all(ny, nz, nx, grad, comp):
    slots, _, _, units, blk = grad.shape
    piece = comp.shape[3:]
    any_spec = pl.BlockSpec(memory_space=pl.ANY)
    vmem = pl.BlockSpec(memory_space=pltpu.VMEM)
    copies = 128
    return pl.pallas_call(
        functools.partial(reduce_kernel, ny, nz, nx),
        in_specs=[any_spec] * 2,
        out_specs=[vmem, vmem],
        out_shape=(
            jax.ShapeDtypeStruct((2 * slots, units // 2, blk), F32),
            jax.ShapeDtypeStruct((nz, ny, 2, nx) + piece, F32),
        ),
        scratch_shapes=[
            pltpu.VMEM(grad.shape, F32),
            pltpu.VMEM(comp.shape, F32),
            pltpu.VMEM((6, nz, units, blk), F32),
            pltpu.VMEM((2, nz // 2, 2, units, blk), F32),
            pltpu.VMEM((2, nz // 2, 2, ny, units, blk), F32),
            pltpu.VMEM((6, units, blk), F32),
            pltpu.VMEM((4, nz, ny) + piece, F32),
            pltpu.VMEM((ny - 1, nz) + piece, F32),
            pltpu.VMEM((nz - 1,) + piece, F32),
            pltpu.SemaphoreType.DMA((copies,)),
            pltpu.SemaphoreType.DMA((copies,)),
            pltpu.SemaphoreType.DMA((5,)),
        ],
        compiler_params=pltpu.CompilerParams(
            collective_id=2, has_side_effects=True, vmem_limit_bytes=48 * MIB
        ),
        cost_estimate=pl.CostEstimate(flops=0, bytes_accessed=100_000_000, transcendentals=0),
        name="reduce",
    )(grad, comp)


def identity(n):
    rows = lax.broadcasted_iota(jnp.int32, (n, n), 0)
    cols = lax.broadcasted_iota(jnp.int32, (n, n), 1)
    return jnp.where(rows == cols, 1.0, 0.0).astype(F32)


def mul(left, right):
    return exact_dot(left, right, ((1,), (0,)))


def spd_inverse(mat, eye):
    n = mat.shape[0]
    bound = jnp.max(jnp.sum(jnp.abs(mat), axis=1, keepdims=True))
    start = eye * (2.0 / (bound + math.sqrt(EPS)))

    def unfinished(state):
        count, previous, residual, _ = state
        return (count < 100) & (residual > 2e-6) & ((residual < 0.5 * previous) | (residual > 0.1))

    def body(state):
        count, _, residual, guess = state
        gap = eye - mul(mat, guess)
        guess = guess + mul(guess, gap)
        return count + 1, residual, jnp.max(jnp.abs(gap)), guess

    state = lax.while_loop(unfinished, body, (0, jnp.float32(4.0), jnp.float32(2.0), start))
    return state[3]


def mixing_of(gram):
    n = gram.shape[0]
    eye = identity(n)
    shifted = gram + EPS * eye
    total = jnp.sum(jnp.sum(shifted * shifted, axis=1, keepdims=True), axis=0, keepdims=True)
    frob = jnp.sqrt(total)
    root = shifted / frob
    middle = 1.5 * eye - 0.5 * root
    root = mul(root, middle)
    inverse = middle
    for _ in range(NS_STEPS - 1):
        middle = 1.5 * eye - 0.5 * mul(inverse, root)
        root = mul(root, middle)
        inverse = mul(middle, inverse)
    half = 0.5 * jnp.sqrt(frob) * (root + root.T) + math.sqrt(EPS) * eye
    half_inv = spd_inverse(half, eye)
    return -mul(inverse, half_inv) / (math.sqrt(EPS) * jnp.sqrt(frob))


def finish_kernel(row_ref, pat_ref, grad_ref, sketch_ref, comp_ref, out_ref, gram_ref, sel_ref):
    slots, rows, blk = grad_ref.shape
    rank = comp_ref.shape[1]
    width = comp_ref.shape[0]
    chunk = 1024
    gram_ref[...] = jnp.zeros_like(gram_ref)

    @pl.loop(0, width // chunk)
    def _(i):
        at = pl.ds(pl.multiple_of(i * chunk, chunk), chunk)
        st = jnp.concatenate([sketch_ref[at, :], comp_ref[at, :]], axis=1)
        high, low = split_bf16(st)
        dims = (((0,), (0,)), ((), ()))
        gram_ref[0] += lax.dot_general(high, high, dims, preferred_element_type=F32)
        gram_ref[1] += lax.dot_general(high, low, dims, preferred_element_type=F32)

    cross = gram_ref[1]
    mixing = mixing_of(gram_ref[0] + (cross + cross.T))
    start = row_ref[0]
    first = lax.div(start, blk)
    last = pat_ref.shape[0] - 1
    grad = jnp.concatenate([grad_ref[k] for k in range(slots)], axis=1)
    block_of = lax.div(start + lax.broadcasted_iota(jnp.int32, (rows, 1), 0), blk)
    projected = None
    for g in range(2):
        brow = jnp.minimum(first + g, last)
        for k in range(slots):
            col = pl.multiple_of(pat_ref[brow, k] * blk, blk)
            here = pl.ds(k * blk, blk)
            sel_ref[g, here, :rank] = sketch_ref[pl.ds(col, blk), :]
            sel_ref[g, here, rank:] = comp_ref[pl.ds(col, blk), :]
        part = mul(grad, sel_ref[g])
        projected = part if projected is None else jnp.where(block_of == first + g, part, projected)
    mixed = mul(projected, mixing)
    corr = exact_dot(mixed, sel_ref[0], ((1,), (1,)))
    corr1 = exact_dot(mixed, sel_ref[1], ((1,), (1,)))
    corr = jnp.where(block_of == first + 1, corr1, corr)
    result = grad * (1.0 / math.sqrt(EPS)) + corr
    for k in range(slots):
        out_ref[:, k, :] = result[:, k * blk : (k + 1) * blk]


def finish(start_row, pattern, grad, sketch_t, comp_t):
    slots, rows, blk = grad.shape
    rank = comp_t.shape[1]
    smem = pl.BlockSpec(memory_space=pltpu.SMEM)
    vmem = pl.BlockSpec(memory_space=pltpu.VMEM)
    return pl.pallas_call(
        finish_kernel,
        in_specs=[smem, smem, vmem, vmem, vmem],
        out_specs=vmem,
        out_shape=jax.ShapeDtypeStruct((rows, slots, blk), F32),
        scratch_shapes=[
            pltpu.VMEM((2, 2 * rank, 2 * rank), F32),
            pltpu.VMEM((2, slots * blk, 2 * rank), F32),
        ],
        compiler_params=pltpu.CompilerParams(vmem_limit_bytes=40 * MIB),
        cost_estimate=pl.CostEstimate(flops=5_000_000_000, bytes_accessed=9_000_000, transcendentals=0),
        name="finish",
    )(start_row, pattern, grad, sketch_t, comp_t)


def per_device(weights, hidden, cotangent, sketch, projection, pattern):
    rank = sketch.shape[0]
    slots, blk = weights.shape[1:]
    dp_size = lax.axis_size("dp")
    nx = lax.axis_size("mp")
    ny = 4
    nz = dp_size // (2 * ny)
    dev_rows = weights.shape[0] // dp_size
    all_tokens = hidden.shape[0] * dp_size
    dp = lax.axis_index("dp")
    core = lax.rem(dp, 2).reshape(1).astype(jnp.int32)
    cot, hid, proj, sketch_t = gather(
        ny, nz, nx, cotangent, hidden, projection.reshape(rank, dev_rows).T, sketch.T
    )
    cot = cot.reshape(nx, -1, cotangent.shape[1])
    hid = hid.reshape(-1, hidden.shape[1])
    input_grad, grad, comp = local_step(
        core, pattern, cot, hid, weights, proj.reshape(-1, rank), all_tokens
    )
    grad, comp = reduce_all(
        ny, nz, nx, grad.reshape(slots // 2, nz, ny, 2 * dev_rows, blk), comp.reshape(nz, ny, nx, -1, rank)
    )
    start_row = (dp * dev_rows).reshape(1).astype(jnp.int32)
    direction = finish(start_row, pattern, grad, sketch_t.reshape(-1, rank), comp.reshape(-1, rank))
    return input_grad, direction[None]


def solution(mesh):
    return jax.shard_map(
        per_device,
        mesh=mesh,
        in_specs=(
            P("mp", None, None),
            P("dp", "mp"),
            P("dp", "mp"),
            P(None, ("dp", "mp")),
            P(None, "mp", "dp"),
            P("mp", None),
        ),
        out_specs=(P("dp", "mp"), P("mp", "dp", None, None)),
        check_vma=False,
    )
```

```python
import functools
import math

import jax
import jax.numpy as jnp
from jax import lax
from jax.experimental import pallas as pl
from jax.experimental.pallas import tpu as pltpu
from jax.sharding import PartitionSpec as P

NS_STEPS = 5
EPS = 0.0001
F32 = jnp.float32
BF16 = jnp.bfloat16
MIB = 1 << 20
TOGETHER = 4
UNROLL = 8
CHUNKS = 2


def split_bf16(value):
    high = value.astype(BF16)
    low = (value - high.astype(F32)).astype(BF16)
    return high, low


def exact_dot(left, right, dims):
    return lax.dot_general(
        left, right, (dims, ((), ())), precision=lax.Precision.HIGHEST, preferred_element_type=F32
    )


def local_kernel(inv_tokens, core_ref, pat_ref, cot_ref, hid_ref, wgt_ref, proj_ref, back_ref, grad_ref, comp_ref, z_ref, w_ref):
    step = pl.program_id(0)
    core = core_ref[0]
    _, slots, blk = wgt_ref.shape
    mine = slots // 2
    together = hid_ref.shape[1] // blk
    rank = proj_ref.shape[1]
    tokens = back_ref.shape[0]
    per_part = cot_ref.shape[2] // blk
    half_blocks = z_ref.shape[0]
    own = pl.ds(pl.multiple_of(core * tokens, tokens), tokens)

    def cot_block(col, rows=slice(None)):
        lane = pl.multiple_of(lax.rem(col, per_part) * blk, blk)
        return cot_ref[lax.div(col, per_part), rows, pl.ds(lane, blk)]

    @pl.when(step == 0)
    def _():
        @pl.loop(0, half_blocks)
        def _(i):
            z_ref[i] = jnp.zeros(z_ref.shape[1:], F32)

    for b in range(together):
        row = step * together + b
        units = slice(b * blk, (b + 1) * blk)
        cols = [pat_ref[row, k] for k in range(slots)]
        chosen = jnp.concatenate([cot_block(col, own) for col in cols], axis=1)
        w_ref[...] = wgt_ref[units].astype(F32).reshape(blk * slots, blk)
        weight = jnp.concatenate(
            [w_ref[pl.ds(k, blk, stride=slots), :].astype(BF16) for k in range(slots)], axis=1
        )
        back = lax.dot_general(chosen, weight, (((1,), (1,)), ((), ())), preferred_element_type=F32)
        back_ref[:, units] = back.astype(BF16)
        hid = hid_ref[:, units]
        wide = jnp.concatenate([cot_block(pat_ref[row, mine * core + j]) for j in range(mine)], axis=1)
        grad = lax.dot_general(hid, wide, (((0,), (0,)), ((), ())), preferred_element_type=F32)
        grad = grad * inv_tokens
        for j in range(mine):
            grad_ref[j, units, :] = grad[:, j * blk : (j + 1) * blk]
        high, low = split_bf16(proj_ref[units, :])
        both = jnp.dot(hid, jnp.concatenate([high, low], axis=1), preferred_element_type=F32)
        y = both[:, :rank] + both[:, rank:]
        for col in cols:

            @pl.when(lax.rem(col, 2) == core)
            def _(col=col, y=y):
                z_ref[lax.div(col, 2)] += y

    @pl.when(step == pl.num_programs(0) - 1)
    def _():
        @pl.loop(0, half_blocks, unroll=UNROLL)
        def _(i):
            zh, zl = split_bf16(z_ref[i])
            out = lax.dot_general(
                cot_block(2 * i + core),
                jnp.concatenate([zh, zl], axis=1),
                (((0,), (0,)), ((), ())),
                preferred_element_type=F32,
            )
            comp_ref[i] = (out[:, :rank] + out[:, rank:]) * inv_tokens


def local_step(core, pattern, cot, hidden, weights, proj, all_tokens):
    parts, wide_tokens, part_cols = cot.shape
    tokens = wide_tokens // 2
    block_rows, slots = pattern.shape
    blk = weights.shape[2]
    rows = hidden.shape[1]
    rank = proj.shape[1]
    half_blocks = parts * part_cols // blk // 2
    wide = TOGETHER * blk
    grid_spec = pltpu.PrefetchScalarGridSpec(
        num_scalar_prefetch=2,
        grid=(block_rows // TOGETHER,),
        in_specs=[
            pl.BlockSpec((parts, wide_tokens, part_cols), lambda r, *_: (0, 0, 0), pipeline_mode=pl.Buffered(1)),
            pl.BlockSpec((wide_tokens, wide), lambda r, *_: (0, r)),
            pl.BlockSpec((wide, slots, blk), lambda r, *_: (r, 0, 0)),
            pl.BlockSpec((wide, rank), lambda r, *_: (r, 0)),
        ],
        out_specs=[
            pl.BlockSpec((tokens, wide), lambda r, *_: (0, r)),
            pl.BlockSpec((slots // 2, wide, blk), lambda r, *_: (0, r, 0)),
            pl.BlockSpec((half_blocks, blk, rank), lambda r, *_: (0, 0, 0), pipeline_mode=pl.Buffered(1)),
        ],
        scratch_shapes=[pltpu.VMEM((half_blocks, wide_tokens, rank), F32), pltpu.VMEM((blk * slots, blk), F32)],
    )
    return pl.pallas_call(
        functools.partial(local_kernel, 1.0 / all_tokens),
        grid_spec=grid_spec,
        out_shape=(
            jax.ShapeDtypeStruct((tokens, rows), BF16),
            jax.ShapeDtypeStruct((slots // 2, rows, blk), F32),
            jax.ShapeDtypeStruct((half_blocks, blk, rank), F32),
        ),
        compiler_params=pltpu.CompilerParams(vmem_limit_bytes=56 * MIB),
        cost_estimate=pl.CostEstimate(flops=6_000_000_000, bytes_accessed=36_000_000, transcendentals=0),
        name="local_step",
    )(core, pattern, cot, hidden, weights, proj)


class Wires:
    def __init__(self, send_sems, recv_sems, local_sems):
        self.send_sems, self.recv_sems, self.local_sems = send_sems, recv_sems, local_sems
        self.used = 0
        self.locals = 0
        self.sent = []

    def send(self, source, target, device):
        copy = pltpu.make_async_remote_copy(
            src_ref=source,
            dst_ref=target,
            send_sem=self.send_sems.at[self.used],
            recv_sem=self.recv_sems.at[self.used],
            device_id=device,
            device_id_type=pl.DeviceIdType.MESH,
        )
        self.used += 1
        copy.start()
        self.sent.append(copy)
        return copy

    def keep(self, source, target):
        copy = pltpu.make_async_copy(source, target, self.local_sems.at[self.locals])
        self.locals += 1
        copy.start()
        return copy

    def drain(self):
        for copy in self.sent:
            copy.wait_send()


def received(*copies):
    for copy in copies:
        copy.wait_recv()


class Place:
    def __init__(self, ny, nz, nx):
        self.n = {"x": nx, "y": ny, "z": nz, "c": 2}
        d = lax.axis_index("dp")
        self.at = {
            "x": lax.axis_index("mp"),
            "c": lax.rem(d, 2),
            "y": lax.rem(lax.div(d, 2), ny),
            "z": lax.div(d, 2 * ny),
        }

    def shift(self, axis, by):
        n = self.n[axis]
        return lax.rem(self.at[axis] + (by % n), n)

    def device(self, axis, by):
        at = dict(self.at)
        at[axis] = self.shift(axis, by)
        return ((at["z"] * self.n["y"] + at["y"]) * 2 + at["c"], at["x"])


def meet(devices):
    barrier = pltpu.get_barrier_semaphore()
    for device in devices:
        pl.semaphore_signal(barrier, inc=1, device_id=device, device_id_type=pl.DeviceIdType.MESH)
    pl.semaphore_wait(barrier, len(devices))


def gather_kernel(ny, nz, nx, cot, hid, proj, sk, cot_o, hid_o, proj_o, sk_o, cot_v, hid_v, proj_v, sk_v, send_sems, recv_sems, local_sems):
    here = Place(ny, nz, nx)
    x, y, z, c = (here.at[name] for name in "xyzc")
    wires = Wires(send_sems, recv_sems, local_sems)
    partners = [here.device("x", j) for j in range(1, nx)] + [here.device("y", j) for j in range(1, ny)]
    partners += [here.device("z", 1), here.device("z", -1), here.device("c", 1)]
    sib = here.device("c", 1)
    loads = [wires.keep(a, b) for a, b in ((sk, sk_v), (proj, proj_v), (cot, cot_v), (hid, hid_v))]
    meet(partners)
    targets = (sk_o.at[z, y, c, x], proj_o.at[z, y, c], cot_o.at[x, c], hid_o.at[c])
    rows = cot.shape[0] // 2
    top, bottom = pl.ds(0, rows), pl.ds(rows, rows)
    sk_x = [wires.send(sk, sk_o.at[z, y, c, x], here.device("x", j)) for j in range(1, nx)]
    proj_y = [wires.send(proj, proj_o.at[z, y, c], here.device("y", j)) for j in range(1, ny)]
    right, left = here.device("x", 1), here.device("x", -1)

    def cot_send(rows_at, device):
        return wires.send(cot.at[rows_at], cot_o.at[x, c, rows_at], device)

    def cot_pass(part, rows_at, device):
        return wires.send(cot_o.at[part, c, rows_at], cot_o.at[part, c, rows_at], device)

    r_top, l_bottom = cot_send(top, right), cot_send(bottom, left)
    r_bottom, l_top = cot_send(bottom, right), cot_send(top, left)
    from_sib = [wires.send(hid, hid_o.at[c], sib), wires.send(cot, cot_o.at[x, c], sib)]

    keeps = []
    for load, value, target in zip(loads, (sk_v, proj_v, cot_v, hid_v), targets):
        load.wait()
        keeps.append(wires.keep(value, target))
    keep_sk, keep_proj, keep_cot, keep_hid = keeps
    keep_sk.wait()
    received(*sk_x)
    sk_y = [
        wires.send(sk_o.at[z, y, c], sk_o.at[z, y, c], here.device("y", j)) for j in range(1, ny)
    ]
    keep_proj.wait()
    received(*proj_y)

    up, down = here.device("z", 1), here.device("z", -1)

    def z_pass(ref, layer, device, ys=slice(None)):
        view = ref.at[layer, ys, c]
        return wires.send(view, view, device)

    arrays = (proj_o, sk_o)
    low, high = pl.ds(0, ny // 2), pl.ds(ny // 2, ny // 2)
    going_up, going_down = [z_pass(proj_o, z, up)], [z_pass(proj_o, z, down)]
    from_sib.append(z_pass(proj_o, z, sib))
    received(*sk_y)
    going_up.append(z_pass(sk_o, z, up))
    going_down.append(z_pass(sk_o, z, down))
    from_sib.append(z_pass(sk_o, z, sib))

    def z_step(distance, going_up, going_down):
        below, above = here.shift("z", -distance), here.shift("z", distance)
        next_up, next_down = [], []
        last = distance == nz // 2
        for moved, layer, device, part, nexts in (
            (going_up, below, up, low, next_up),
            (going_down, above, down, high, next_down),
        ):
            for copy, ref in zip(moved, arrays):
                received(copy)
                if not last:
                    ys = part if distance + 1 == nz // 2 else slice(None)
                    nexts.append(z_pass(ref, layer, device, ys))
                from_sib.append(z_pass(ref, layer, sib, part if last else slice(None)))
        return next_up, next_down

    left_part, right_part, far_part = here.shift("x", -1), here.shift("x", 1), here.shift("x", 2)

    def cot_first():
        received(r_top)
        far_top = cot_pass(left_part, top, right)
        from_sib.append(cot_pass(left_part, top, sib))
        received(l_bottom)
        far_bottom = cot_pass(right_part, bottom, left)
        from_sib.append(cot_pass(right_part, bottom, sib))
        return far_top, far_bottom

    for distance in range(1, nz // 2 + 1):
        if distance == 2:
            far_top, far_bottom = cot_first()
        if distance == 3:
            received(r_bottom)
            from_sib.append(cot_pass(left_part, bottom, sib))
            received(l_top)
            from_sib.append(cot_pass(right_part, top, sib))
        going_up, going_down = z_step(distance, going_up, going_down)
    received(far_top)
    from_sib.append(cot_pass(far_part, top, sib))
    received(far_bottom)
    from_sib.append(cot_pass(far_part, bottom, sib))
    keep_cot.wait()
    keep_hid.wait()
    received(*from_sib)
    wires.drain()


def gather(ny, nz, nx, cot, hid, proj, sk):
    any_spec = pl.BlockSpec(memory_space=pl.ANY)
    copies = 80
    return pl.pallas_call(
        functools.partial(gather_kernel, ny, nz, nx),
        in_specs=[any_spec] * 4,
        out_specs=[any_spec] * 4,
        out_shape=(
            jax.ShapeDtypeStruct((nx, 2) + cot.shape, cot.dtype),
            jax.ShapeDtypeStruct((2,) + hid.shape, hid.dtype),
            jax.ShapeDtypeStruct((nz, ny, 2) + proj.shape, proj.dtype),
            jax.ShapeDtypeStruct((nz, ny, 2, nx) + sk.shape, sk.dtype),
        ),
        scratch_shapes=[
            pltpu.VMEM(cot.shape, cot.dtype),
            pltpu.VMEM(hid.shape, hid.dtype),
            pltpu.VMEM(proj.shape, proj.dtype),
            pltpu.VMEM(sk.shape, sk.dtype),
            pltpu.SemaphoreType.DMA((copies,)),
            pltpu.SemaphoreType.DMA((copies,)),
            pltpu.SemaphoreType.DMA((8,)),
        ],
        compiler_params=pltpu.CompilerParams(collective_id=1, has_side_effects=True),
        cost_estimate=pl.CostEstimate(flops=0, bytes_accessed=60_000_000, transcendentals=0),
        name="gather",
    )(cot, hid, proj, sk)


def add_into(target, index, source, loop):
    at = index.index(None)

    @pl.loop(0, loop)
    def _(i):
        place = tuple(index[:at]) + (i,) + tuple(index[at + 1 :])
        target[place] = target[place] + source[i]


def reduce_kernel(
    ny, nz, nx, grad, comp, grad_o, comp_o, xg, xc, ya, za, zb, yb, cx, cy, cz, send_sems, recv_sems, local_sems
):
    here = Place(ny, nz, nx)
    x, y, z, c = (here.at[name] for name in "xyzc")
    wires = Wires(send_sems, recv_sems, local_sems)
    keep_comp = wires.keep(comp, xc)
    keep_grad = [wires.keep(grad.at[s], xg.at[s]) for s in (2, 3, 0, 1)]
    sib = here.device("c", 1)
    partners = [here.device("x", j) for j in range(1, nx)] + [here.device("y", j) for j in range(1, ny)]
    partners += [here.device("z", j) for j in range(1, nz)] + [sib]
    meet(partners)
    xp, xm = here.device("x", 1), here.device("x", -1)
    yp, ym = here.device("y", 1), here.device("y", -1)
    zp, zm = here.device("z", 1), here.device("z", -1)
    x1, x2, x3 = (here.shift("x", j) for j in (1, 2, 3))
    y1, y2, y3 = (here.shift("y", j) for j in (1, 2, 3))
    send = wires.send
    zlow, zhigh = pl.ds(0, nz // 2), pl.ds(nz // 2, nz // 2)

    chunk_rows = comp.shape[3] // CHUNKS
    from_sib = []

    class Chunk:
        def __init__(self, index):
            self.rows = pl.ds(index * chunk_rows, chunk_rows)

        def start(self):
            r = self.rows
            self.far = (
                send(xc.at[zlow, :, x2, r], cx.at[0, zlow, :, r], xp),
                send(xc.at[zhigh, :, x2, r], cx.at[1, zhigh, :, r], xm),
            )
            self.near = [
                send(xc.at[zhigh, :, x1, r], cx.at[2, zhigh, :, r], xp),
                send(xc.at[zlow, :, x3, r], cx.at[3, zlow, :, r], xm),
            ]

        def middle(self):
            r = self.rows
            received(self.far[0])

            @pl.loop(0, nz // 2)
            def _(i):
                xc[i, :, x1, r] = xc[i, :, x1, r] + cx[0, i, :, r]

            self.near.append(send(xc.at[zlow, :, x1, r], cx.at[2, zlow, :, r], xp))
            received(self.far[1])

            @pl.loop(nz // 2, nz)
            def _(i):
                xc[i, :, x3, r] = xc[i, :, x3, r] + cx[1, i, :, r]

            self.near.append(send(xc.at[zhigh, :, x3, r], cx.at[3, zhigh, :, r], xm))

        def along_y(self):
            r = self.rows
            received(*self.near)

            @pl.loop(0, nz)
            def _(i):
                xc[i, :, x, r] = xc[i, :, x, r] + cx[2, i, :, r] + cx[3, i, :, r]

            self.moved = [
                send(xc.at[:, here.shift("y", j), x, r], cy.at[j - 1, :, r], here.device("y", j)) for j in range(1, ny)
            ]

        def along_z(self):
            r = self.rows
            received(*self.moved)

            @pl.loop(0, nz)
            def _(i):
                xc[i, y, x, r] = xc[i, y, x, r] + (cy[0, i, r] + cy[1, i, r] + cy[2, i, r])

            self.moved = [
                send(xc.at[here.shift("z", j), y, x, r], cz.at[j - 1, r], here.device("z", j)) for j in range(1, nz)
            ]

        def total(self):
            r = self.rows
            received(*self.moved)
            total = xc[z, y, x, r]
            for j in range(nz - 1):
                total = total + cz[j, r]
            comp_o[z, y, c, x, r] = total
            mine = comp_o.at[z, y, c, x, r]
            self.moved = [send(mine, mine, here.device("z", j)) for j in range(1, nz)]

        def back_y(self):
            received(*self.moved)
            column = comp_o.at[:, y, c, x, self.rows]
            self.moved = [send(column, column, here.device("y", j)) for j in range(1, ny)]

        def copy_to(self, layers, at, device):
            part = comp_o.at[layers, :, c, at, self.rows]
            return send(part, part, device)

        def back_x(self):
            received(*self.moved)
            every = slice(None)
            self.moved = [self.copy_to(every, x, xp), self.copy_to(every, x, xm)]
            from_sib.append(self.copy_to(every, x, sib))

        def back_far(self):
            every = slice(None)
            received(self.moved[0])
            far = [self.copy_to(zlow, x3, xp)]
            received(self.moved[1])
            far.append(self.copy_to(zhigh, x1, xm))
            self.moved = far
            for at in (x3, x1):
                from_sib.append(self.copy_to(every, at, sib))

        def finish(self):
            for copy, layers in zip(self.moved, (zlow, zhigh)):
                received(copy)
                from_sib.append(self.copy_to(layers, x2, sib))

    keep_comp.wait()
    first, second = Chunk(0), Chunk(1)
    first.start()
    class Ring:
        def __init__(self, source, arrived, side, index, add, dist):
            self.source, self.arrived, self.side, self.index, self.add = source, arrived, side, index, add
            self.send(dist)

        def layer(self, dist):
            return here.shift("z", dist if self.side == 0 else -dist)

        def send(self, dist):
            self.dist = dist
            target = self.arrived.at[self.side, dist - 1, self.index]
            self.copy = send(self.source(self.index, self.layer(dist)), target, (zp, zm)[self.side])

        def step(self):
            if self.dist == 0:
                return
            received(self.copy)
            self.add(self.index, self.layer(self.dist - 1), self.side, self.dist - 1)
            if self.dist > 1:
                self.send(self.dist - 1)
            else:
                self.dist = 0

    far_z = nz // 2

    def b_add(index, layer, side, slot_at):
        add_into(xg, [2 + index, layer, None], zb.at[side, slot_at, index], ny)

    def a_add(index, layer, side, slot_at):
        xg[index, layer, y] = xg[index, layer, y] + za[side, slot_at, index]

    def b_ring(side, index, dist):
        return Ring(lambda s, layer: xg.at[2 + s, layer], zb, side, index, b_add, dist)

    def a_ring(side, index, dist):
        return Ring(lambda s, layer: xg.at[s, layer, y], za, side, index, a_add, dist)

    keep_grad[0].wait()
    keep_grad[1].wait()
    b_rings = [b_ring(0, 0, far_z), b_ring(1, 1, far_z), b_ring(0, 1, far_z - 1), b_ring(1, 0, far_z - 1)]
    keep_grad[2].wait()
    keep_grad[3].wait()
    a_far = (send(xg.at[0, :, y2], ya.at[0], yp), send(xg.at[1, :, y2], ya.at[1], ym))
    a_near = [send(xg.at[1, :, y1], ya.at[2], yp), send(xg.at[0, :, y3], ya.at[3], ym)]

    def advance(rings):
        for ring in rings:
            ring.step()

    first.middle()
    second.start()
    advance(b_rings[:2])
    second.middle()
    received(a_far[0])
    add_into(xg, [0, None, y1], ya.at[0], nz)
    a_near.append(send(xg.at[0, :, y1], ya.at[4], yp))
    received(a_far[1])
    add_into(xg, [1, None, y3], ya.at[1], nz)
    a_near.append(send(xg.at[1, :, y3], ya.at[5], ym))
    advance(b_rings[2:])
    first.along_y()
    advance(b_rings[:2])
    first.along_z()
    second.along_y()
    advance(b_rings[2:])
    first.total()
    second.along_z()
    advance(b_rings[:2])
    first.back_y()
    second.total()
    advance(b_rings[2:])
    first.back_x()
    second.back_y()
    received(a_near[2], a_near[1])

    @pl.loop(0, nz)
    def _(i):
        xg[0, i, y] = xg[0, i, y] + ya[4, i] + ya[3, i]

    a_rings = [a_ring(0, 0, far_z), None, None, a_ring(1, 0, far_z - 1)]
    received(a_near[0], a_near[3])

    @pl.loop(0, nz)
    def _(i):
        xg[1, i, y] = xg[1, i, y] + ya[2, i] + ya[5, i]

    a_rings[1:3] = [a_ring(1, 1, far_z), a_ring(0, 1, far_z - 1)]
    second.back_x()
    advance(b_rings[:2])
    b2_far = (send(xg.at[2, z, y2], yb.at[0], yp), send(xg.at[3, z, y2], yb.at[1], ym))
    b2_near = [send(xg.at[3, z, y1], yb.at[2], yp), send(xg.at[2, z, y3], yb.at[3], ym)]
    first.back_far()
    advance(a_rings)
    received(b2_far[0])
    xg[2, z, y1] = xg[2, z, y1] + yb[0]
    b2_near.append(send(xg.at[2, z, y1], yb.at[4], yp))
    received(b2_far[1])
    xg[3, z, y3] = xg[3, z, y3] + yb[1]
    b2_near.append(send(xg.at[3, z, y3], yb.at[5], ym))
    advance(a_rings)
    second.back_far()
    advance(a_rings)
    first.finish()
    received(*b2_near)
    xg[2, z, y] = xg[2, z, y] + yb[4] + yb[3]
    xg[3, z, y] = xg[3, z, y] + yb[2] + yb[5]
    advance(a_rings)
    units = grad_o.shape[1]
    theirs = pl.ds(pl.multiple_of((1 - c) * units, 8), units)
    swap = send(xg.at[:, z, y, theirs], grad_o.at[pl.ds(c * 4, 4)], sib)
    for s in range(4):
        grad_o[c * 4 + s] = xg[s, z, y, pl.ds(pl.multiple_of(c * units, 8), units)]
    second.finish()
    received(swap, *from_sib)
    wires.drain()


def reduce_all(ny, nz, nx, grad, comp):
    slots, _, _, units, blk = grad.shape
    piece = comp.shape[3:]
    any_spec = pl.BlockSpec(memory_space=pl.ANY)
    vmem = pl.BlockSpec(memory_space=pltpu.VMEM)
    copies = 128
    return pl.pallas_call(
        functools.partial(reduce_kernel, ny, nz, nx),
        in_specs=[any_spec] * 2,
        out_specs=[vmem, vmem],
        out_shape=(
            jax.ShapeDtypeStruct((2 * slots, units // 2, blk), F32),
            jax.ShapeDtypeStruct((nz, ny, 2, nx) + piece, F32),
        ),
        scratch_shapes=[
            pltpu.VMEM(grad.shape, F32),
            pltpu.VMEM(comp.shape, F32),
            pltpu.VMEM((6, nz, units, blk), F32),
            pltpu.VMEM((2, nz // 2, 2, units, blk), F32),
            pltpu.VMEM((2, nz // 2, 2, ny, units, blk), F32),
            pltpu.VMEM((6, units, blk), F32),
            pltpu.VMEM((4, nz, ny) + piece, F32),
            pltpu.VMEM((ny - 1, nz) + piece, F32),
            pltpu.VMEM((nz - 1,) + piece, F32),
            pltpu.SemaphoreType.DMA((copies,)),
            pltpu.SemaphoreType.DMA((copies,)),
            pltpu.SemaphoreType.DMA((5,)),
        ],
        compiler_params=pltpu.CompilerParams(
            collective_id=2, has_side_effects=True, vmem_limit_bytes=48 * MIB
        ),
        cost_estimate=pl.CostEstimate(flops=0, bytes_accessed=100_000_000, transcendentals=0),
        name="reduce",
    )(grad, comp)


def identity(n):
    rows = lax.broadcasted_iota(jnp.int32, (n, n), 0)
    cols = lax.broadcasted_iota(jnp.int32, (n, n), 1)
    return jnp.where(rows == cols, 1.0, 0.0).astype(F32)


def mul(left, right):
    return exact_dot(left, right, ((1,), (0,)))


def spd_inverse(mat, start, eye):
    def unfinished(state):
        count, previous, residual, _ = state
        return (count < 100) & (residual > 1e-5) & ((residual < 0.5 * previous) | (residual > 0.1))

    def body(state):
        count, _, residual, guess = state
        gap = eye - mul(mat, guess)
        guess = guess + mul(guess, gap)
        return count + 1, residual, jnp.sqrt(jnp.sum(gap * gap)), guess

    state = lax.while_loop(unfinished, body, (0, jnp.float32(64.0), jnp.float32(32.0), start))
    return state[3]


def mixing_of(gram):
    n = gram.shape[0]
    eye = identity(n)
    shifted = gram + EPS * eye
    total = jnp.sum(jnp.sum(shifted * shifted, axis=1, keepdims=True), axis=0, keepdims=True)
    frob = jnp.sqrt(total)
    root = shifted / frob
    middle = 1.5 * eye - 0.5 * root
    root = mul(root, middle)
    inverse = middle
    for _ in range(NS_STEPS - 1):
        middle = 1.5 * eye - 0.5 * mul(inverse, root)
        root = mul(root, middle)
        inverse = mul(middle, inverse)
    half = 0.5 * jnp.sqrt(frob) * (root + root.T) + math.sqrt(EPS) * eye
    near = inverse / jnp.sqrt(frob)
    norm = jnp.max(jnp.sum(jnp.abs(near), axis=1, keepdims=True))
    shift = math.sqrt(EPS)
    start = near * (1.0 / (1.0 + 0.5 * jnp.minimum(shift * norm, 1.0)))
    half_inv = spd_inverse(half, start, eye)
    return -mul(inverse, half_inv) / (math.sqrt(EPS) * jnp.sqrt(frob))


def finish_kernel(row_ref, pat_ref, grad_ref, sketch_ref, comp_ref, out_ref, gram_ref, sel_ref):
    slots, rows, blk = grad_ref.shape
    rank = comp_ref.shape[1]
    width = comp_ref.shape[0]
    chunk = 1024
    gram_ref[...] = jnp.zeros_like(gram_ref)

    @pl.loop(0, width // chunk)
    def _(i):
        at = pl.ds(pl.multiple_of(i * chunk, chunk), chunk)
        st = jnp.concatenate([sketch_ref[at, :], comp_ref[at, :]], axis=1)
        high, low = split_bf16(st)
        dims = (((0,), (0,)), ((), ()))
        gram_ref[0] += lax.dot_general(high, high, dims, preferred_element_type=F32)
        gram_ref[1] += lax.dot_general(high, low, dims, preferred_element_type=F32)

    cross = gram_ref[1]
    mixing = mixing_of(gram_ref[0] + (cross + cross.T))
    start = row_ref[0]
    first = lax.div(start, blk)
    last = pat_ref.shape[0] - 1
    grad = jnp.concatenate([grad_ref[k] for k in range(slots)], axis=1)
    block_of = lax.div(start + lax.broadcasted_iota(jnp.int32, (rows, 1), 0), blk)
    projected = None
    for g in range(2):
        brow = jnp.minimum(first + g, last)
        for k in range(slots):
            col = pl.multiple_of(pat_ref[brow, k] * blk, blk)
            here = pl.ds(k * blk, blk)
            sel_ref[g, here, :rank] = sketch_ref[pl.ds(col, blk), :]
            sel_ref[g, here, rank:] = comp_ref[pl.ds(col, blk), :]
        part = mul(grad, sel_ref[g])
        projected = part if projected is None else jnp.where(block_of == first + g, part, projected)
    mixed = mul(projected, mixing)
    corr = exact_dot(mixed, sel_ref[0], ((1,), (1,)))
    corr1 = exact_dot(mixed, sel_ref[1], ((1,), (1,)))
    corr = jnp.where(block_of == first + 1, corr1, corr)
    result = grad * (1.0 / math.sqrt(EPS)) + corr
    for k in range(slots):
        out_ref[:, k, :] = result[:, k * blk : (k + 1) * blk]


def finish(start_row, pattern, grad, sketch_t, comp_t):
    slots, rows, blk = grad.shape
    rank = comp_t.shape[1]
    smem = pl.BlockSpec(memory_space=pltpu.SMEM)
    vmem = pl.BlockSpec(memory_space=pltpu.VMEM)
    return pl.pallas_call(
        finish_kernel,
        in_specs=[smem, smem, vmem, vmem, vmem],
        out_specs=vmem,
        out_shape=jax.ShapeDtypeStruct((rows, slots, blk), F32),
        scratch_shapes=[
            pltpu.VMEM((2, 2 * rank, 2 * rank), F32),
            pltpu.VMEM((2, slots * blk, 2 * rank), F32),
        ],
        compiler_params=pltpu.CompilerParams(vmem_limit_bytes=40 * MIB),
        cost_estimate=pl.CostEstimate(flops=5_000_000_000, bytes_accessed=9_000_000, transcendentals=0),
        name="finish",
    )(start_row, pattern, grad, sketch_t, comp_t)


def per_device(weights, hidden, cotangent, sketch, projection, pattern):
    rank = sketch.shape[0]
    slots, blk = weights.shape[1:]
    dp_size = lax.axis_size("dp")
    nx = lax.axis_size("mp")
    ny = 4
    nz = dp_size // (2 * ny)
    dev_rows = weights.shape[0] // dp_size
    all_tokens = hidden.shape[0] * dp_size
    dp = lax.axis_index("dp")
    core = lax.rem(dp, 2).reshape(1).astype(jnp.int32)
    cot, hid, proj, sketch_t = gather(
        ny, nz, nx, cotangent, hidden, projection.reshape(rank, dev_rows).T, sketch.T
    )
    cot = cot.reshape(nx, -1, cotangent.shape[1])
    hid = hid.reshape(-1, hidden.shape[1])
    input_grad, grad, comp = local_step(
        core, pattern, cot, hid, weights, proj.reshape(-1, rank), all_tokens
    )
    grad, comp = reduce_all(
        ny, nz, nx, grad.reshape(slots // 2, nz, ny, 2 * dev_rows, blk), comp.reshape(nz, ny, nx, -1, rank)
    )
    start_row = (dp * dev_rows).reshape(1).astype(jnp.int32)
    direction = finish(start_row, pattern, grad, sketch_t.reshape(-1, rank), comp.reshape(-1, rank))
    return input_grad, direction[None]


def solution(mesh):
    return jax.shard_map(
        per_device,
        mesh=mesh,
        in_specs=(
            P("mp", None, None),
            P("dp", "mp"),
            P("dp", "mp"),
            P(None, ("dp", "mp")),
            P(None, "mp", "dp"),
            P("mp", None),
        ),
        out_specs=(P("dp", "mp"), P("mp", "dp", None, None)),
        check_vma=False,
    )
```

```python
import functools
import math

import jax
import jax.numpy as jnp
from jax import lax
from jax.experimental import pallas as pl
from jax.experimental.pallas import tpu as pltpu
from jax.sharding import PartitionSpec as P

NS_STEPS = 5
EPS = 0.0001
F32 = jnp.float32
BF16 = jnp.bfloat16
MIB = 1 << 20
TOGETHER = 4
UNROLL = 8
CHUNKS = 2


def split_bf16(value):
    high = value.astype(BF16)
    low = (value - high.astype(F32)).astype(BF16)
    return high, low


def exact_dot(left, right, dims):
    return lax.dot_general(
        left, right, (dims, ((), ())), precision=lax.Precision.HIGHEST, preferred_element_type=F32
    )


def local_kernel(inv_tokens, core_ref, pat_ref, cot_ref, hid_ref, wgt_ref, proj_ref, back_ref, grad_ref, comp_ref, z_ref, w_ref):
    step = pl.program_id(0)
    core = core_ref[0]
    _, slots, blk = wgt_ref.shape
    mine = slots // 2
    together = hid_ref.shape[1] // blk
    rank = proj_ref.shape[1]
    tokens = back_ref.shape[0]
    per_part = cot_ref.shape[2] // blk
    half_blocks = z_ref.shape[0]
    own = pl.ds(pl.multiple_of(core * tokens, tokens), tokens)

    def cot_block(col, rows=slice(None)):
        lane = pl.multiple_of(lax.rem(col, per_part) * blk, blk)
        return cot_ref[lax.div(col, per_part), rows, pl.ds(lane, blk)]

    @pl.when(step == 0)
    def _():
        @pl.loop(0, half_blocks)
        def _(i):
            z_ref[i] = jnp.zeros(z_ref.shape[1:], F32)

    for b in range(together):
        row = step * together + b
        units = slice(b * blk, (b + 1) * blk)
        cols = [pat_ref[row, k] for k in range(slots)]
        chosen = jnp.concatenate([cot_block(col, own) for col in cols], axis=1)
        w_ref[...] = wgt_ref[units].astype(F32).reshape(blk * slots, blk)
        weight = jnp.concatenate(
            [w_ref[pl.ds(k, blk, stride=slots), :].astype(BF16) for k in range(slots)], axis=1
        )
        back = lax.dot_general(chosen, weight, (((1,), (1,)), ((), ())), preferred_element_type=F32)
        back_ref[:, units] = back.astype(BF16)
        hid = hid_ref[:, units]
        wide = jnp.concatenate([cot_block(pat_ref[row, mine * core + j]) for j in range(mine)], axis=1)
        grad = lax.dot_general(hid, wide, (((0,), (0,)), ((), ())), preferred_element_type=F32)
        grad = grad * inv_tokens
        for j in range(mine):
            grad_ref[j, units, :] = grad[:, j * blk : (j + 1) * blk]
        high, low = split_bf16(proj_ref[units, :])
        both = jnp.dot(hid, jnp.concatenate([high, low], axis=1), preferred_element_type=F32)
        y = both[:, :rank] + both[:, rank:]
        for col in cols:

            @pl.when(lax.rem(col, 2) == core)
            def _(col=col, y=y):
                z_ref[lax.div(col, 2)] += y

    @pl.when(step == pl.num_programs(0) - 1)
    def _():
        @pl.loop(0, half_blocks, unroll=UNROLL)
        def _(i):
            zh, zl = split_bf16(z_ref[i])
            out = lax.dot_general(
                cot_block(2 * i + core),
                jnp.concatenate([zh, zl], axis=1),
                (((0,), (0,)), ((), ())),
                preferred_element_type=F32,
            )
            comp_ref[i] = (out[:, :rank] + out[:, rank:]) * inv_tokens


def local_step(core, pattern, cot, hidden, weights, proj, all_tokens):
    parts, wide_tokens, part_cols = cot.shape
    tokens = wide_tokens // 2
    block_rows, slots = pattern.shape
    blk = weights.shape[2]
    rows = hidden.shape[1]
    rank = proj.shape[1]
    half_blocks = parts * part_cols // blk // 2
    wide = TOGETHER * blk
    grid_spec = pltpu.PrefetchScalarGridSpec(
        num_scalar_prefetch=2,
        grid=(block_rows // TOGETHER,),
        in_specs=[
            pl.BlockSpec((parts, wide_tokens, part_cols), lambda r, *_: (0, 0, 0), pipeline_mode=pl.Buffered(1)),
            pl.BlockSpec((wide_tokens, wide), lambda r, *_: (0, r)),
            pl.BlockSpec((wide, slots, blk), lambda r, *_: (r, 0, 0)),
            pl.BlockSpec((wide, rank), lambda r, *_: (r, 0)),
        ],
        out_specs=[
            pl.BlockSpec((tokens, wide), lambda r, *_: (0, r)),
            pl.BlockSpec((slots // 2, wide, blk), lambda r, *_: (0, r, 0)),
            pl.BlockSpec((half_blocks, blk, rank), lambda r, *_: (0, 0, 0), pipeline_mode=pl.Buffered(1)),
        ],
        scratch_shapes=[pltpu.VMEM((half_blocks, wide_tokens, rank), F32), pltpu.VMEM((blk * slots, blk), F32)],
    )
    return pl.pallas_call(
        functools.partial(local_kernel, 1.0 / all_tokens),
        grid_spec=grid_spec,
        out_shape=(
            jax.ShapeDtypeStruct((tokens, rows), BF16),
            jax.ShapeDtypeStruct((slots // 2, rows, blk), F32),
            jax.ShapeDtypeStruct((half_blocks, blk, rank), F32),
        ),
        compiler_params=pltpu.CompilerParams(vmem_limit_bytes=56 * MIB),
        cost_estimate=pl.CostEstimate(flops=6_000_000_000, bytes_accessed=36_000_000, transcendentals=0),
        name="local_step",
    )(core, pattern, cot, hidden, weights, proj)


class Wires:
    def __init__(self, send_sems, recv_sems, local_sems):
        self.send_sems, self.recv_sems, self.local_sems = send_sems, recv_sems, local_sems
        self.used = 0
        self.locals = 0
        self.sent = []

    def send(self, source, target, device):
        copy = pltpu.make_async_remote_copy(
            src_ref=source,
            dst_ref=target,
            send_sem=self.send_sems.at[self.used],
            recv_sem=self.recv_sems.at[self.used],
            device_id=device,
            device_id_type=pl.DeviceIdType.MESH,
        )
        self.used += 1
        copy.start()
        self.sent.append(copy)
        return copy

    def keep(self, source, target):
        copy = pltpu.make_async_copy(source, target, self.local_sems.at[self.locals])
        self.locals += 1
        copy.start()
        return copy

    def drain(self):
        for copy in self.sent:
            copy.wait_send()


def received(*copies):
    for copy in copies:
        copy.wait_recv()


class Place:
    def __init__(self, ny, nz, nx):
        self.n = {"x": nx, "y": ny, "z": nz, "c": 2}
        d = lax.axis_index("dp")
        self.at = {
            "x": lax.axis_index("mp"),
            "c": lax.rem(d, 2),
            "y": lax.rem(lax.div(d, 2), ny),
            "z": lax.div(d, 2 * ny),
        }

    def shift(self, axis, by):
        n = self.n[axis]
        return lax.rem(self.at[axis] + (by % n), n)

    def device(self, axis, by):
        at = dict(self.at)
        at[axis] = self.shift(axis, by)
        return ((at["z"] * self.n["y"] + at["y"]) * 2 + at["c"], at["x"])


def meet(devices):
    barrier = pltpu.get_barrier_semaphore()
    for device in devices:
        pl.semaphore_signal(barrier, inc=1, device_id=device, device_id_type=pl.DeviceIdType.MESH)
    pl.semaphore_wait(barrier, len(devices))


def gather_kernel(ny, nz, nx, cot, hid, proj, sk, cot_o, hid_o, proj_o, sk_o, cot_v, hid_v, proj_v, sk_v, send_sems, recv_sems, local_sems):
    here = Place(ny, nz, nx)
    x, y, z, c = (here.at[name] for name in "xyzc")
    wires = Wires(send_sems, recv_sems, local_sems)
    partners = [here.device("x", j) for j in range(1, nx)] + [here.device("y", j) for j in range(1, ny)]
    partners += [here.device("z", 1), here.device("z", -1), here.device("c", 1)]
    sib = here.device("c", 1)
    loads = [wires.keep(a, b) for a, b in ((sk, sk_v), (proj, proj_v), (cot, cot_v), (hid, hid_v))]
    meet(partners)
    targets = (sk_o.at[z, y, c, x], proj_o.at[z, y, c], cot_o.at[x, c], hid_o.at[c])
    rows = cot.shape[0] // 2
    top, bottom = pl.ds(0, rows), pl.ds(rows, rows)
    sk_x = [wires.send(sk, sk_o.at[z, y, c, x], here.device("x", j)) for j in range(1, nx)]
    proj_y = [wires.send(proj, proj_o.at[z, y, c], here.device("y", j)) for j in range(1, ny)]
    right, left = here.device("x", 1), here.device("x", -1)

    def cot_send(rows_at, device):
        return wires.send(cot.at[rows_at], cot_o.at[x, c, rows_at], device)

    def cot_pass(part, rows_at, device):
        return wires.send(cot_o.at[part, c, rows_at], cot_o.at[part, c, rows_at], device)

    r_top, l_bottom = cot_send(top, right), cot_send(bottom, left)
    r_bottom, l_top = cot_send(bottom, right), cot_send(top, left)
    from_sib = [wires.send(hid, hid_o.at[c], sib), wires.send(cot, cot_o.at[x, c], sib)]

    keeps = []
    for load, value, target in zip(loads, (sk_v, proj_v, cot_v, hid_v), targets):
        load.wait()
        keeps.append(wires.keep(value, target))
    keep_sk, keep_proj, keep_cot, keep_hid = keeps
    keep_sk.wait()
    received(*sk_x)
    sk_y = [
        wires.send(sk_o.at[z, y, c], sk_o.at[z, y, c], here.device("y", j)) for j in range(1, ny)
    ]
    keep_proj.wait()
    received(*proj_y)

    up, down = here.device("z", 1), here.device("z", -1)

    def z_pass(ref, layer, device, ys=slice(None)):
        view = ref.at[layer, ys, c]
        return wires.send(view, view, device)

    arrays = (proj_o, sk_o)
    low, high = pl.ds(0, ny // 2), pl.ds(ny // 2, ny // 2)
    going_up, going_down = [z_pass(proj_o, z, up)], [z_pass(proj_o, z, down)]
    from_sib.append(z_pass(proj_o, z, sib))
    received(*sk_y)
    going_up.append(z_pass(sk_o, z, up))
    going_down.append(z_pass(sk_o, z, down))
    from_sib.append(z_pass(sk_o, z, sib))

    def z_step(distance, going_up, going_down):
        below, above = here.shift("z", -distance), here.shift("z", distance)
        next_up, next_down = [], []
        last = distance == nz // 2
        for moved, layer, device, part, nexts in (
            (going_up, below, up, low, next_up),
            (going_down, above, down, high, next_down),
        ):
            for copy, ref in zip(moved, arrays):
                received(copy)
                if not last:
                    ys = part if distance + 1 == nz // 2 else slice(None)
                    nexts.append(z_pass(ref, layer, device, ys))
                from_sib.append(z_pass(ref, layer, sib, part if last else slice(None)))
        return next_up, next_down

    left_part, right_part, far_part = here.shift("x", -1), here.shift("x", 1), here.shift("x", 2)

    def cot_first():
        received(r_top)
        far_top = cot_pass(left_part, top, right)
        from_sib.append(cot_pass(left_part, top, sib))
        received(l_bottom)
        far_bottom = cot_pass(right_part, bottom, left)
        from_sib.append(cot_pass(right_part, bottom, sib))
        return far_top, far_bottom

    for distance in range(1, nz // 2 + 1):
        if distance == 2:
            far_top, far_bottom = cot_first()
        if distance == 3:
            received(r_bottom)
            from_sib.append(cot_pass(left_part, bottom, sib))
            received(l_top)
            from_sib.append(cot_pass(right_part, top, sib))
        going_up, going_down = z_step(distance, going_up, going_down)
    received(far_top)
    from_sib.append(cot_pass(far_part, top, sib))
    received(far_bottom)
    from_sib.append(cot_pass(far_part, bottom, sib))
    keep_cot.wait()
    keep_hid.wait()
    received(*from_sib)
    wires.drain()


def gather(ny, nz, nx, cot, hid, proj, sk):
    any_spec = pl.BlockSpec(memory_space=pl.ANY)
    copies = 80
    return pl.pallas_call(
        functools.partial(gather_kernel, ny, nz, nx),
        in_specs=[any_spec] * 4,
        out_specs=[any_spec] * 4,
        out_shape=(
            jax.ShapeDtypeStruct((nx, 2) + cot.shape, cot.dtype),
            jax.ShapeDtypeStruct((2,) + hid.shape, hid.dtype),
            jax.ShapeDtypeStruct((nz, ny, 2) + proj.shape, proj.dtype),
            jax.ShapeDtypeStruct((nz, ny, 2, nx) + sk.shape, sk.dtype),
        ),
        scratch_shapes=[
            pltpu.VMEM(cot.shape, cot.dtype),
            pltpu.VMEM(hid.shape, hid.dtype),
            pltpu.VMEM(proj.shape, proj.dtype),
            pltpu.VMEM(sk.shape, sk.dtype),
            pltpu.SemaphoreType.DMA((copies,)),
            pltpu.SemaphoreType.DMA((copies,)),
            pltpu.SemaphoreType.DMA((8,)),
        ],
        compiler_params=pltpu.CompilerParams(collective_id=1, has_side_effects=True),
        cost_estimate=pl.CostEstimate(flops=0, bytes_accessed=60_000_000, transcendentals=0),
        name="gather",
    )(cot, hid, proj, sk)


def add_into(target, index, source, loop):
    at = index.index(None)

    @pl.loop(0, loop)
    def _(i):
        place = tuple(index[:at]) + (i,) + tuple(index[at + 1 :])
        target[place] = target[place] + source[i]


def reduce_kernel(
    ny, nz, nx, grad, comp, grad_o, comp_o, xg, xc, ya, za, zb, yb, cx, cy, cz, send_sems, recv_sems, local_sems
):
    here = Place(ny, nz, nx)
    x, y, z, c = (here.at[name] for name in "xyzc")
    wires = Wires(send_sems, recv_sems, local_sems)
    keep_comp = wires.keep(comp, xc)
    keep_grad = [wires.keep(grad.at[s], xg.at[s]) for s in (2, 3, 0, 1)]
    sib = here.device("c", 1)
    partners = [here.device("x", j) for j in range(1, nx)] + [here.device("y", j) for j in range(1, ny)]
    partners += [here.device("z", j) for j in range(1, nz)] + [sib]
    meet(partners)
    xp, xm = here.device("x", 1), here.device("x", -1)
    yp, ym = here.device("y", 1), here.device("y", -1)
    zp, zm = here.device("z", 1), here.device("z", -1)
    x1, x2, x3 = (here.shift("x", j) for j in (1, 2, 3))
    y1, y2, y3 = (here.shift("y", j) for j in (1, 2, 3))
    send = wires.send
    zlow, zhigh = pl.ds(0, nz // 2), pl.ds(nz // 2, nz // 2)

    chunk_rows = comp.shape[3] // CHUNKS
    from_sib = []

    class Chunk:
        def __init__(self, index):
            self.rows = pl.ds(index * chunk_rows, chunk_rows)

        def start(self):
            r = self.rows
            self.far = (
                send(xc.at[zlow, :, x2, r], cx.at[0, zlow, :, r], xp),
                send(xc.at[zhigh, :, x2, r], cx.at[1, zhigh, :, r], xm),
            )
            self.near = [
                send(xc.at[zhigh, :, x1, r], cx.at[2, zhigh, :, r], xp),
                send(xc.at[zlow, :, x3, r], cx.at[3, zlow, :, r], xm),
            ]

        def middle(self):
            r = self.rows
            received(self.far[0])

            @pl.loop(0, nz // 2)
            def _(i):
                xc[i, :, x1, r] = xc[i, :, x1, r] + cx[0, i, :, r]

            self.near.append(send(xc.at[zlow, :, x1, r], cx.at[2, zlow, :, r], xp))
            received(self.far[1])

            @pl.loop(nz // 2, nz)
            def _(i):
                xc[i, :, x3, r] = xc[i, :, x3, r] + cx[1, i, :, r]

            self.near.append(send(xc.at[zhigh, :, x3, r], cx.at[3, zhigh, :, r], xm))

        def along_y(self):
            r = self.rows
            received(*self.near)

            @pl.loop(0, nz)
            def _(i):
                xc[i, :, x, r] = xc[i, :, x, r] + cx[2, i, :, r] + cx[3, i, :, r]

            self.moved = [
                send(xc.at[:, here.shift("y", j), x, r], cy.at[j - 1, :, r], here.device("y", j)) for j in range(1, ny)
            ]

        def along_z(self):
            r = self.rows
            received(*self.moved)

            @pl.loop(0, nz)
            def _(i):
                xc[i, y, x, r] = xc[i, y, x, r] + (cy[0, i, r] + cy[1, i, r] + cy[2, i, r])

            self.moved = [
                send(xc.at[here.shift("z", j), y, x, r], cz.at[j - 1, r], here.device("z", j)) for j in range(1, nz)
            ]

        def total(self):
            r = self.rows
            received(*self.moved)
            total = xc[z, y, x, r]
            for j in range(nz - 1):
                total = total + cz[j, r]
            comp_o[z, y, c, x, r] = total
            mine = comp_o.at[z, y, c, x, r]
            self.moved = [send(mine, mine, here.device("z", j)) for j in range(1, nz)]

        def back_y(self):
            received(*self.moved)
            column = comp_o.at[:, y, c, x, self.rows]
            self.moved = [send(column, column, here.device("y", j)) for j in range(1, ny)]

        def copy_to(self, layers, at, device):
            part = comp_o.at[layers, :, c, at, self.rows]
            return send(part, part, device)

        def back_x(self):
            received(*self.moved)
            every = slice(None)
            self.moved = [self.copy_to(every, x, xp), self.copy_to(every, x, xm)]
            from_sib.append(self.copy_to(every, x, sib))

        def back_far(self):
            every = slice(None)
            received(self.moved[0])
            far = [self.copy_to(zlow, x3, xp)]
            received(self.moved[1])
            far.append(self.copy_to(zhigh, x1, xm))
            self.moved = far
            for at in (x3, x1):
                from_sib.append(self.copy_to(every, at, sib))

        def finish(self):
            for copy, layers in zip(self.moved, (zlow, zhigh)):
                received(copy)
                from_sib.append(self.copy_to(layers, x2, sib))

    keep_comp.wait()
    first, second = Chunk(0), Chunk(1)
    first.start()
    class Ring:
        def __init__(self, source, arrived, side, index, add, dist):
            self.source, self.arrived, self.side, self.index, self.add = source, arrived, side, index, add
            self.send(dist)

        def layer(self, dist):
            return here.shift("z", dist if self.side == 0 else -dist)

        def send(self, dist):
            self.dist = dist
            target = self.arrived.at[self.side, dist - 1, self.index]
            self.copy = send(self.source(self.index, self.layer(dist)), target, (zp, zm)[self.side])

        def step(self):
            if self.dist == 0:
                return
            received(self.copy)
            self.add(self.index, self.layer(self.dist - 1), self.side, self.dist - 1)
            if self.dist > 1:
                self.send(self.dist - 1)
            else:
                self.dist = 0

    far_z = nz // 2

    def b_add(index, layer, side, slot_at):
        add_into(xg, [2 + index, layer, None], zb.at[side, slot_at, index], ny)

    def a_add(index, layer, side, slot_at):
        xg[index, layer, y] = xg[index, layer, y] + za[side, slot_at, index]

    def b_ring(side, index, dist):
        return Ring(lambda s, layer: xg.at[2 + s, layer], zb, side, index, b_add, dist)

    def a_ring(side, index, dist):
        return Ring(lambda s, layer: xg.at[s, layer, y], za, side, index, a_add, dist)

    keep_grad[0].wait()
    keep_grad[1].wait()
    b_rings = [b_ring(0, 0, far_z), b_ring(1, 1, far_z), b_ring(0, 1, far_z - 1), b_ring(1, 0, far_z - 1)]
    keep_grad[2].wait()
    keep_grad[3].wait()
    a_far = (send(xg.at[0, :, y2], ya.at[0], yp), send(xg.at[1, :, y2], ya.at[1], ym))
    a_near = [send(xg.at[1, :, y1], ya.at[2], yp), send(xg.at[0, :, y3], ya.at[3], ym)]

    def advance(rings):
        for ring in rings:
            ring.step()

    first.middle()
    second.start()
    advance(b_rings[:2])
    second.middle()
    first.along_y()
    received(a_far[0])
    add_into(xg, [0, None, y1], ya.at[0], nz)
    a_near.append(send(xg.at[0, :, y1], ya.at[4], yp))
    received(a_far[1])
    add_into(xg, [1, None, y3], ya.at[1], nz)
    a_near.append(send(xg.at[1, :, y3], ya.at[5], ym))
    advance(b_rings[2:])
    first.along_z()
    advance(b_rings[:2])
    second.along_y()
    first.total()
    advance(b_rings[2:])
    second.along_z()
    first.back_y()
    advance(b_rings[:2])
    second.total()
    first.back_x()
    advance(b_rings[2:])
    second.back_y()
    received(a_near[2], a_near[1])

    @pl.loop(0, nz)
    def _(i):
        xg[0, i, y] = xg[0, i, y] + ya[4, i] + ya[3, i]

    a_rings = [a_ring(0, 0, far_z), None, None, a_ring(1, 0, far_z - 1)]
    received(a_near[0], a_near[3])

    @pl.loop(0, nz)
    def _(i):
        xg[1, i, y] = xg[1, i, y] + ya[2, i] + ya[5, i]

    a_rings[1:3] = [a_ring(1, 1, far_z), a_ring(0, 1, far_z - 1)]
    second.back_x()
    advance(b_rings[:2])
    b2_far = (send(xg.at[2, z, y2], yb.at[0], yp), send(xg.at[3, z, y2], yb.at[1], ym))
    b2_near = [send(xg.at[3, z, y1], yb.at[2], yp), send(xg.at[2, z, y3], yb.at[3], ym)]
    first.back_far()
    advance(a_rings)
    received(b2_far[0])
    xg[2, z, y1] = xg[2, z, y1] + yb[0]
    b2_near.append(send(xg.at[2, z, y1], yb.at[4], yp))
    received(b2_far[1])
    xg[3, z, y3] = xg[3, z, y3] + yb[1]
    b2_near.append(send(xg.at[3, z, y3], yb.at[5], ym))
    advance(a_rings)
    second.back_far()
    advance(a_rings)
    first.finish()
    received(*b2_near)
    xg[2, z, y] = xg[2, z, y] + yb[4] + yb[3]
    xg[3, z, y] = xg[3, z, y] + yb[2] + yb[5]
    advance(a_rings)
    units = grad_o.shape[1]
    theirs = pl.ds(pl.multiple_of((1 - c) * units, 8), units)
    swap = send(xg.at[:, z, y, theirs], grad_o.at[pl.ds(c * 4, 4)], sib)
    for s in range(4):
        grad_o[c * 4 + s] = xg[s, z, y, pl.ds(pl.multiple_of(c * units, 8), units)]
    second.finish()
    received(swap, *from_sib)
    wires.drain()


def reduce_all(ny, nz, nx, grad, comp):
    slots, _, _, units, blk = grad.shape
    piece = comp.shape[3:]
    any_spec = pl.BlockSpec(memory_space=pl.ANY)
    vmem = pl.BlockSpec(memory_space=pltpu.VMEM)
    copies = 128
    return pl.pallas_call(
        functools.partial(reduce_kernel, ny, nz, nx),
        in_specs=[any_spec] * 2,
        out_specs=[vmem, vmem],
        out_shape=(
            jax.ShapeDtypeStruct((2 * slots, units // 2, blk), F32),
            jax.ShapeDtypeStruct((nz, ny, 2, nx) + piece, F32),
        ),
        scratch_shapes=[
            pltpu.VMEM(grad.shape, F32),
            pltpu.VMEM(comp.shape, F32),
            pltpu.VMEM((6, nz, units, blk), F32),
            pltpu.VMEM((2, nz // 2, 2, units, blk), F32),
            pltpu.VMEM((2, nz // 2, 2, ny, units, blk), F32),
            pltpu.VMEM((6, units, blk), F32),
            pltpu.VMEM((4, nz, ny) + piece, F32),
            pltpu.VMEM((ny - 1, nz) + piece, F32),
            pltpu.VMEM((nz - 1,) + piece, F32),
            pltpu.SemaphoreType.DMA((copies,)),
            pltpu.SemaphoreType.DMA((copies,)),
            pltpu.SemaphoreType.DMA((5,)),
        ],
        compiler_params=pltpu.CompilerParams(
            collective_id=2, has_side_effects=True, vmem_limit_bytes=48 * MIB
        ),
        cost_estimate=pl.CostEstimate(flops=0, bytes_accessed=100_000_000, transcendentals=0),
        name="reduce",
    )(grad, comp)


def identity(n):
    rows = lax.broadcasted_iota(jnp.int32, (n, n), 0)
    cols = lax.broadcasted_iota(jnp.int32, (n, n), 1)
    return jnp.where(rows == cols, 1.0, 0.0).astype(F32)


def mul(left, right):
    return exact_dot(left, right, ((1,), (0,)))


def spd_inverse(mat, start, eye):
    def unfinished(state):
        count, previous, residual, _ = state
        return (count < 100) & (residual > 1e-5) & ((residual < 0.5 * previous) | (residual > 0.1))

    def body(state):
        count, _, residual, guess = state
        gap = eye - mul(mat, guess)
        guess = guess + mul(guess, gap)
        return count + 1, residual, jnp.sqrt(jnp.sum(gap * gap)), guess

    state = lax.while_loop(unfinished, body, (0, jnp.float32(64.0), jnp.float32(32.0), start))
    return state[3]


def mixing_of(gram):
    n = gram.shape[0]
    eye = identity(n)
    shifted = gram + EPS * eye
    total = jnp.sum(jnp.sum(shifted * shifted, axis=1, keepdims=True), axis=0, keepdims=True)
    frob = jnp.sqrt(total)
    root = shifted / frob
    middle = 1.5 * eye - 0.5 * root
    root = mul(root, middle)
    inverse = middle
    for _ in range(NS_STEPS - 1):
        middle = 1.5 * eye - 0.5 * mul(inverse, root)
        root = mul(root, middle)
        inverse = mul(middle, inverse)
    half = 0.5 * jnp.sqrt(frob) * (root + root.T) + math.sqrt(EPS) * eye
    near = inverse / jnp.sqrt(frob)
    norm = jnp.max(jnp.sum(jnp.abs(near), axis=1, keepdims=True))
    shift = math.sqrt(EPS)
    start = near * (1.0 / (1.0 + 0.5 * jnp.minimum(shift * norm, 1.0)))
    half_inv = spd_inverse(half, start, eye)
    return -mul(inverse, half_inv) / (math.sqrt(EPS) * jnp.sqrt(frob))


def finish_kernel(row_ref, pat_ref, grad_ref, sketch_ref, comp_ref, out_ref, gram_ref, sel_ref):
    slots, rows, blk = grad_ref.shape
    rank = comp_ref.shape[1]
    width = comp_ref.shape[0]
    chunk = 1024
    gram_ref[...] = jnp.zeros_like(gram_ref)

    @pl.loop(0, width // chunk)
    def _(i):
        at = pl.ds(pl.multiple_of(i * chunk, chunk), chunk)
        st = jnp.concatenate([sketch_ref[at, :], comp_ref[at, :]], axis=1)
        high, low = split_bf16(st)
        dims = (((0,), (0,)), ((), ()))
        gram_ref[0] += lax.dot_general(high, high, dims, preferred_element_type=F32)
        gram_ref[1] += lax.dot_general(high, low, dims, preferred_element_type=F32)

    cross = gram_ref[1]
    mixing = mixing_of(gram_ref[0] + (cross + cross.T))
    start = row_ref[0]
    first = lax.div(start, blk)
    last = pat_ref.shape[0] - 1
    grad = jnp.concatenate([grad_ref[k] for k in range(slots)], axis=1)
    block_of = lax.div(start + lax.broadcasted_iota(jnp.int32, (rows, 1), 0), blk)
    projected = None
    for g in range(2):
        brow = jnp.minimum(first + g, last)
        for k in range(slots):
            col = pl.multiple_of(pat_ref[brow, k] * blk, blk)
            here = pl.ds(k * blk, blk)
            sel_ref[g, here, :rank] = sketch_ref[pl.ds(col, blk), :]
            sel_ref[g, here, rank:] = comp_ref[pl.ds(col, blk), :]
        part = mul(grad, sel_ref[g])
        projected = part if projected is None else jnp.where(block_of == first + g, part, projected)
    mixed = mul(projected, mixing)
    corr = exact_dot(mixed, sel_ref[0], ((1,), (1,)))
    corr1 = exact_dot(mixed, sel_ref[1], ((1,), (1,)))
    corr = jnp.where(block_of == first + 1, corr1, corr)
    result = grad * (1.0 / math.sqrt(EPS)) + corr
    for k in range(slots):
        out_ref[:, k, :] = result[:, k * blk : (k + 1) * blk]


def finish(start_row, pattern, grad, sketch_t, comp_t):
    slots, rows, blk = grad.shape
    rank = comp_t.shape[1]
    smem = pl.BlockSpec(memory_space=pltpu.SMEM)
    vmem = pl.BlockSpec(memory_space=pltpu.VMEM)
    return pl.pallas_call(
        finish_kernel,
        in_specs=[smem, smem, vmem, vmem, vmem],
        out_specs=vmem,
        out_shape=jax.ShapeDtypeStruct((rows, slots, blk), F32),
        scratch_shapes=[
            pltpu.VMEM((2, 2 * rank, 2 * rank), F32),
            pltpu.VMEM((2, slots * blk, 2 * rank), F32),
        ],
        compiler_params=pltpu.CompilerParams(vmem_limit_bytes=40 * MIB),
        cost_estimate=pl.CostEstimate(flops=5_000_000_000, bytes_accessed=9_000_000, transcendentals=0),
        name="finish",
    )(start_row, pattern, grad, sketch_t, comp_t)


def per_device(weights, hidden, cotangent, sketch, projection, pattern):
    rank = sketch.shape[0]
    slots, blk = weights.shape[1:]
    dp_size = lax.axis_size("dp")
    nx = lax.axis_size("mp")
    ny = 4
    nz = dp_size // (2 * ny)
    dev_rows = weights.shape[0] // dp_size
    all_tokens = hidden.shape[0] * dp_size
    dp = lax.axis_index("dp")
    core = lax.rem(dp, 2).reshape(1).astype(jnp.int32)
    cot, hid, proj, sketch_t = gather(
        ny, nz, nx, cotangent, hidden, projection.reshape(rank, dev_rows).T, sketch.T
    )
    cot = cot.reshape(nx, -1, cotangent.shape[1])
    hid = hid.reshape(-1, hidden.shape[1])
    input_grad, grad, comp = local_step(
        core, pattern, cot, hid, weights, proj.reshape(-1, rank), all_tokens
    )
    grad, comp = reduce_all(
        ny, nz, nx, grad.reshape(slots // 2, nz, ny, 2 * dev_rows, blk), comp.reshape(nz, ny, nx, -1, rank)
    )
    start_row = (dp * dev_rows).reshape(1).astype(jnp.int32)
    direction = finish(start_row, pattern, grad, sketch_t.reshape(-1, rank), comp.reshape(-1, rank))
    return input_grad, direction[None]


def solution(mesh):
    return jax.shard_map(
        per_device,
        mesh=mesh,
        in_specs=(
            P("mp", None, None),
            P("dp", "mp"),
            P("dp", "mp"),
            P(None, ("dp", "mp")),
            P(None, "mp", "dp"),
            P("mp", None),
        ),
        out_specs=(P("dp", "mp"), P("mp", "dp", None, None)),
        check_vma=False,
    )
```

```python
import functools
import math

import jax
import jax.numpy as jnp
from jax import lax
from jax.experimental import pallas as pl
from jax.experimental.pallas import tpu as pltpu
from jax.sharding import PartitionSpec as P

NS_STEPS = 5
EPS = 0.0001
F32 = jnp.float32
BF16 = jnp.bfloat16
MIB = 1 << 20
TOGETHER = 4
UNROLL = 8
CHUNKS = 2


def split_bf16(value):
    high = value.astype(BF16)
    low = (value - high.astype(F32)).astype(BF16)
    return high, low


def exact_dot(left, right, dims):
    return lax.dot_general(
        left, right, (dims, ((), ())), precision=lax.Precision.HIGHEST, preferred_element_type=F32
    )


def local_kernel(inv_tokens, core_ref, pat_ref, cot_ref, hid_ref, wgt_ref, proj_ref, back_ref, grad_ref, comp_ref, z_ref, w_ref):
    step = pl.program_id(0)
    core = core_ref[0]
    _, slots, blk = wgt_ref.shape
    mine = slots // 2
    together = hid_ref.shape[1] // blk
    rank = proj_ref.shape[1]
    tokens = back_ref.shape[0]
    per_part = cot_ref.shape[2] // blk
    half_blocks = z_ref.shape[0]
    own = pl.ds(pl.multiple_of(core * tokens, tokens), tokens)

    def cot_block(col, rows=slice(None)):
        lane = pl.multiple_of(lax.rem(col, per_part) * blk, blk)
        return cot_ref[lax.div(col, per_part), rows, pl.ds(lane, blk)]

    @pl.when(step == 0)
    def _():
        @pl.loop(0, half_blocks)
        def _(i):
            z_ref[i] = jnp.zeros(z_ref.shape[1:], F32)

    for b in range(together):
        row = step * together + b
        units = slice(b * blk, (b + 1) * blk)
        cols = [pat_ref[row, k] for k in range(slots)]
        chosen = jnp.concatenate([cot_block(col, own) for col in cols], axis=1)
        w_ref[...] = wgt_ref[units].astype(F32).reshape(blk * slots, blk)
        weight = jnp.concatenate(
            [w_ref[pl.ds(k, blk, stride=slots), :].astype(BF16) for k in range(slots)], axis=1
        )
        back = lax.dot_general(chosen, weight, (((1,), (1,)), ((), ())), preferred_element_type=F32)
        back_ref[:, units] = back.astype(BF16)
        hid = hid_ref[:, units]
        wide = jnp.concatenate([cot_block(pat_ref[row, mine * core + j]) for j in range(mine)], axis=1)
        grad = lax.dot_general(hid, wide, (((0,), (0,)), ((), ())), preferred_element_type=F32)
        grad = grad * inv_tokens
        for j in range(mine):
            grad_ref[j, units, :] = grad[:, j * blk : (j + 1) * blk]
        high, low = split_bf16(proj_ref[units, :])
        both = jnp.dot(hid, jnp.concatenate([high, low], axis=1), preferred_element_type=F32)
        y = both[:, :rank] + both[:, rank:]
        for col in cols:

            @pl.when(lax.rem(col, 2) == core)
            def _(col=col, y=y):
                z_ref[lax.div(col, 2)] += y

    @pl.when(step == pl.num_programs(0) - 1)
    def _():
        @pl.loop(0, half_blocks, unroll=UNROLL)
        def _(i):
            zh, zl = split_bf16(z_ref[i])
            out = lax.dot_general(
                cot_block(2 * i + core),
                jnp.concatenate([zh, zl], axis=1),
                (((0,), (0,)), ((), ())),
                preferred_element_type=F32,
            )
            comp_ref[i] = (out[:, :rank] + out[:, rank:]) * inv_tokens


def local_step(core, pattern, cot, hidden, weights, proj, all_tokens):
    parts, wide_tokens, part_cols = cot.shape
    tokens = wide_tokens // 2
    block_rows, slots = pattern.shape
    blk = weights.shape[2]
    rows = hidden.shape[1]
    rank = proj.shape[1]
    half_blocks = parts * part_cols // blk // 2
    wide = TOGETHER * blk
    grid_spec = pltpu.PrefetchScalarGridSpec(
        num_scalar_prefetch=2,
        grid=(block_rows // TOGETHER,),
        in_specs=[
            pl.BlockSpec((parts, wide_tokens, part_cols), lambda r, *_: (0, 0, 0), pipeline_mode=pl.Buffered(1)),
            pl.BlockSpec((wide_tokens, wide), lambda r, *_: (0, r)),
            pl.BlockSpec((wide, slots, blk), lambda r, *_: (r, 0, 0)),
            pl.BlockSpec((wide, rank), lambda r, *_: (r, 0)),
        ],
        out_specs=[
            pl.BlockSpec((tokens, wide), lambda r, *_: (0, r)),
            pl.BlockSpec((slots // 2, wide, blk), lambda r, *_: (0, r, 0)),
            pl.BlockSpec((half_blocks, blk, rank), lambda r, *_: (0, 0, 0), pipeline_mode=pl.Buffered(1)),
        ],
        scratch_shapes=[pltpu.VMEM((half_blocks, wide_tokens, rank), F32), pltpu.VMEM((blk * slots, blk), F32)],
    )
    return pl.pallas_call(
        functools.partial(local_kernel, 1.0 / all_tokens),
        grid_spec=grid_spec,
        out_shape=(
            jax.ShapeDtypeStruct((tokens, rows), BF16),
            jax.ShapeDtypeStruct((slots // 2, rows, blk), F32),
            jax.ShapeDtypeStruct((half_blocks, blk, rank), F32),
        ),
        compiler_params=pltpu.CompilerParams(vmem_limit_bytes=56 * MIB),
        cost_estimate=pl.CostEstimate(flops=6_000_000_000, bytes_accessed=36_000_000, transcendentals=0),
        name="local_step",
    )(core, pattern, cot, hidden, weights, proj)


class Wires:
    def __init__(self, send_sems, recv_sems, local_sems):
        self.send_sems, self.recv_sems, self.local_sems = send_sems, recv_sems, local_sems
        self.used = 0
        self.locals = 0
        self.sent = []

    def send(self, source, target, device):
        copy = pltpu.make_async_remote_copy(
            src_ref=source,
            dst_ref=target,
            send_sem=self.send_sems.at[self.used],
            recv_sem=self.recv_sems.at[self.used],
            device_id=device,
            device_id_type=pl.DeviceIdType.MESH,
        )
        self.used += 1
        copy.start()
        self.sent.append(copy)
        return copy

    def keep(self, source, target):
        copy = pltpu.make_async_copy(source, target, self.local_sems.at[self.locals])
        self.locals += 1
        copy.start()
        return copy

    def drain(self):
        for copy in self.sent:
            copy.wait_send()


def received(*copies):
    for copy in copies:
        copy.wait_recv()


class Place:
    def __init__(self, ny, nz, nx):
        self.n = {"x": nx, "y": ny, "z": nz, "c": 2}
        d = lax.axis_index("dp")
        self.at = {
            "x": lax.axis_index("mp"),
            "c": lax.rem(d, 2),
            "y": lax.rem(lax.div(d, 2), ny),
            "z": lax.div(d, 2 * ny),
        }

    def shift(self, axis, by):
        n = self.n[axis]
        return lax.rem(self.at[axis] + (by % n), n)

    def device(self, axis, by):
        at = dict(self.at)
        at[axis] = self.shift(axis, by)
        return ((at["z"] * self.n["y"] + at["y"]) * 2 + at["c"], at["x"])


def meet(devices):
    barrier = pltpu.get_barrier_semaphore()
    for device in devices:
        pl.semaphore_signal(barrier, inc=1, device_id=device, device_id_type=pl.DeviceIdType.MESH)
    pl.semaphore_wait(barrier, len(devices))


def gather_kernel(ny, nz, nx, cot, hid, proj, sk, cot_o, hid_o, proj_o, sk_o, cot_v, hid_v, proj_v, sk_v, send_sems, recv_sems, local_sems):
    here = Place(ny, nz, nx)
    x, y, z, c = (here.at[name] for name in "xyzc")
    wires = Wires(send_sems, recv_sems, local_sems)
    partners = [here.device("x", j) for j in range(1, nx)] + [here.device("y", j) for j in range(1, ny)]
    partners += [here.device("z", 1), here.device("z", -1), here.device("c", 1)]
    sib = here.device("c", 1)
    loads = [wires.keep(a, b) for a, b in ((sk, sk_v), (proj, proj_v), (cot, cot_v), (hid, hid_v))]
    meet(partners)
    targets = (sk_o.at[z, y, c, x], proj_o.at[z, y, c], cot_o.at[x, c], hid_o.at[c])
    rows = cot.shape[0] // 2
    top, bottom = pl.ds(0, rows), pl.ds(rows, rows)
    sk_x = [wires.send(sk, sk_o.at[z, y, c, x], here.device("x", j)) for j in range(1, nx)]
    proj_y = [wires.send(proj, proj_o.at[z, y, c], here.device("y", j)) for j in range(1, ny)]
    right, left = here.device("x", 1), here.device("x", -1)

    def cot_send(rows_at, device):
        return wires.send(cot.at[rows_at], cot_o.at[x, c, rows_at], device)

    def cot_pass(part, rows_at, device):
        return wires.send(cot_o.at[part, c, rows_at], cot_o.at[part, c, rows_at], device)

    r_top, l_bottom = cot_send(top, right), cot_send(bottom, left)
    r_bottom, l_top = cot_send(bottom, right), cot_send(top, left)
    from_sib = [wires.send(hid, hid_o.at[c], sib), wires.send(cot, cot_o.at[x, c], sib)]

    keeps = []
    for load, value, target in zip(loads, (sk_v, proj_v, cot_v, hid_v), targets):
        load.wait()
        keeps.append(wires.keep(value, target))
    keep_sk, keep_proj, keep_cot, keep_hid = keeps
    keep_sk.wait()
    received(*sk_x)
    sk_y = [
        wires.send(sk_o.at[z, y, c], sk_o.at[z, y, c], here.device("y", j)) for j in range(1, ny)
    ]
    keep_proj.wait()
    received(*proj_y)

    up, down = here.device("z", 1), here.device("z", -1)

    def z_pass(ref, layer, device, ys=slice(None)):
        view = ref.at[layer, ys, c]
        return wires.send(view, view, device)

    arrays = (proj_o, sk_o)
    low, high = pl.ds(0, ny // 2), pl.ds(ny // 2, ny // 2)
    going_up, going_down = [z_pass(proj_o, z, up)], [z_pass(proj_o, z, down)]
    from_sib.append(z_pass(proj_o, z, sib))
    received(*sk_y)
    going_up.append(z_pass(sk_o, z, up))
    going_down.append(z_pass(sk_o, z, down))
    from_sib.append(z_pass(sk_o, z, sib))

    def z_step(distance, going_up, going_down):
        below, above = here.shift("z", -distance), here.shift("z", distance)
        next_up, next_down = [], []
        last = distance == nz // 2
        for moved, layer, device, part, nexts in (
            (going_up, below, up, low, next_up),
            (going_down, above, down, high, next_down),
        ):
            for copy, ref in zip(moved, arrays):
                received(copy)
                if not last:
                    ys = part if distance + 1 == nz // 2 else slice(None)
                    nexts.append(z_pass(ref, layer, device, ys))
                from_sib.append(z_pass(ref, layer, sib, part if last else slice(None)))
        return next_up, next_down

    left_part, right_part, far_part = here.shift("x", -1), here.shift("x", 1), here.shift("x", 2)

    def cot_first():
        received(r_top)
        far_top = cot_pass(left_part, top, right)
        from_sib.append(cot_pass(left_part, top, sib))
        received(l_bottom)
        far_bottom = cot_pass(right_part, bottom, left)
        from_sib.append(cot_pass(right_part, bottom, sib))
        return far_top, far_bottom

    for distance in range(1, nz // 2 + 1):
        if distance == 2:
            far_top, far_bottom = cot_first()
        if distance == 3:
            received(r_bottom)
            from_sib.append(cot_pass(left_part, bottom, sib))
            received(l_top)
            from_sib.append(cot_pass(right_part, top, sib))
        going_up, going_down = z_step(distance, going_up, going_down)
    received(far_top)
    from_sib.append(cot_pass(far_part, top, sib))
    received(far_bottom)
    from_sib.append(cot_pass(far_part, bottom, sib))
    keep_cot.wait()
    keep_hid.wait()
    received(*from_sib)
    wires.drain()


def gather(ny, nz, nx, cot, hid, proj, sk):
    any_spec = pl.BlockSpec(memory_space=pl.ANY)
    copies = 80
    return pl.pallas_call(
        functools.partial(gather_kernel, ny, nz, nx),
        in_specs=[any_spec] * 4,
        out_specs=[any_spec] * 4,
        out_shape=(
            jax.ShapeDtypeStruct((nx, 2) + cot.shape, cot.dtype),
            jax.ShapeDtypeStruct((2,) + hid.shape, hid.dtype),
            jax.ShapeDtypeStruct((nz, ny, 2) + proj.shape, proj.dtype),
            jax.ShapeDtypeStruct((nz, ny, 2, nx) + sk.shape, sk.dtype),
        ),
        scratch_shapes=[
            pltpu.VMEM(cot.shape, cot.dtype),
            pltpu.VMEM(hid.shape, hid.dtype),
            pltpu.VMEM(proj.shape, proj.dtype),
            pltpu.VMEM(sk.shape, sk.dtype),
            pltpu.SemaphoreType.DMA((copies,)),
            pltpu.SemaphoreType.DMA((copies,)),
            pltpu.SemaphoreType.DMA((8,)),
        ],
        compiler_params=pltpu.CompilerParams(collective_id=1, has_side_effects=True),
        cost_estimate=pl.CostEstimate(flops=0, bytes_accessed=60_000_000, transcendentals=0),
        name="gather",
    )(cot, hid, proj, sk)


def add_into(target, index, source, loop):
    at = index.index(None)

    @pl.loop(0, loop)
    def _(i):
        place = tuple(index[:at]) + (i,) + tuple(index[at + 1 :])
        target[place] = target[place] + source[i]


def reduce_kernel(
    ny, nz, nx, grad, comp, grad_o, comp_o, xg, xc, ya, za, zb, yb, cx, cy, cz, send_sems, recv_sems, local_sems
):
    here = Place(ny, nz, nx)
    x, y, z, c = (here.at[name] for name in "xyzc")
    wires = Wires(send_sems, recv_sems, local_sems)
    keep_comp = wires.keep(comp, xc)
    keep_grad = [wires.keep(grad.at[s], xg.at[s]) for s in (2, 3, 0, 1)]
    sib = here.device("c", 1)
    partners = [here.device("x", j) for j in range(1, nx)] + [here.device("y", j) for j in range(1, ny)]
    partners += [here.device("z", j) for j in range(1, nz)] + [sib]
    meet(partners)
    xp, xm = here.device("x", 1), here.device("x", -1)
    yp, ym = here.device("y", 1), here.device("y", -1)
    zp, zm = here.device("z", 1), here.device("z", -1)
    x1, x2, x3 = (here.shift("x", j) for j in (1, 2, 3))
    y1, y2, y3 = (here.shift("y", j) for j in (1, 2, 3))
    send = wires.send
    zlow, zhigh = pl.ds(0, nz // 2), pl.ds(nz // 2, nz // 2)

    chunk_rows = comp.shape[3] // CHUNKS
    from_sib = []

    class Chunk:
        def __init__(self, index):
            self.rows = pl.ds(index * chunk_rows, chunk_rows)

        def start(self):
            r = self.rows
            self.far = (
                send(xc.at[zlow, :, x2, r], cx.at[0, zlow, :, r], xp),
                send(xc.at[zhigh, :, x2, r], cx.at[1, zhigh, :, r], xm),
            )
            self.near = [
                send(xc.at[zhigh, :, x1, r], cx.at[2, zhigh, :, r], xp),
                send(xc.at[zlow, :, x3, r], cx.at[3, zlow, :, r], xm),
            ]

        def middle(self):
            r = self.rows
            received(self.far[0])

            @pl.loop(0, nz // 2)
            def _(i):
                xc[i, :, x1, r] = xc[i, :, x1, r] + cx[0, i, :, r]

            self.near.append(send(xc.at[zlow, :, x1, r], cx.at[2, zlow, :, r], xp))
            received(self.far[1])

            @pl.loop(nz // 2, nz)
            def _(i):
                xc[i, :, x3, r] = xc[i, :, x3, r] + cx[1, i, :, r]

            self.near.append(send(xc.at[zhigh, :, x3, r], cx.at[3, zhigh, :, r], xm))

        def along_y(self):
            r = self.rows
            received(*self.near)

            @pl.loop(0, nz)
            def _(i):
                xc[i, :, x, r] = xc[i, :, x, r] + cx[2, i, :, r] + cx[3, i, :, r]

            self.moved = [
                send(xc.at[:, here.shift("y", j), x, r], cy.at[j - 1, :, r], here.device("y", j)) for j in range(1, ny)
            ]

        def along_z(self):
            r = self.rows
            received(*self.moved)

            @pl.loop(0, nz)
            def _(i):
                xc[i, y, x, r] = xc[i, y, x, r] + (cy[0, i, r] + cy[1, i, r] + cy[2, i, r])

            self.moved = [
                send(xc.at[here.shift("z", j), y, x, r], cz.at[j - 1, r], here.device("z", j)) for j in range(1, nz)
            ]

        def total(self):
            r = self.rows
            received(*self.moved)
            total = xc[z, y, x, r]
            for j in range(nz - 1):
                total = total + cz[j, r]
            comp_o[z, y, c, x, r] = total
            mine = comp_o.at[z, y, c, x, r]
            self.moved = [send(mine, mine, here.device("z", j)) for j in range(1, nz)]

        def back_y(self):
            received(*self.moved)
            column = comp_o.at[:, y, c, x, self.rows]
            self.moved = [send(column, column, here.device("y", j)) for j in range(1, ny)]

        def copy_to(self, layers, at, device):
            part = comp_o.at[layers, :, c, at, self.rows]
            return send(part, part, device)

        def back_x(self):
            received(*self.moved)
            every = slice(None)
            self.moved = [self.copy_to(every, x, xp), self.copy_to(every, x, xm)]
            from_sib.append(self.copy_to(every, x, sib))

        def back_far(self):
            every = slice(None)
            received(self.moved[0])
            far = [self.copy_to(zlow, x3, xp)]
            received(self.moved[1])
            far.append(self.copy_to(zhigh, x1, xm))
            self.moved = far
            for at in (x3, x1):
                from_sib.append(self.copy_to(every, at, sib))

        def finish(self):
            for copy, layers in zip(self.moved, (zlow, zhigh)):
                received(copy)
                from_sib.append(self.copy_to(layers, x2, sib))

    keep_comp.wait()
    first, second = Chunk(0), Chunk(1)
    first.start()
    class Ring:
        def __init__(self, source, arrived, side, index, add, dist):
            self.source, self.arrived, self.side, self.index, self.add = source, arrived, side, index, add
            self.send(dist)

        def layer(self, dist):
            return here.shift("z", dist if self.side == 0 else -dist)

        def send(self, dist):
            self.dist = dist
            target = self.arrived.at[self.side, dist - 1, self.index]
            self.copy = send(self.source(self.index, self.layer(dist)), target, (zp, zm)[self.side])

        def step(self):
            if self.dist == 0:
                return
            received(self.copy)
            self.add(self.index, self.layer(self.dist - 1), self.side, self.dist - 1)
            if self.dist > 1:
                self.send(self.dist - 1)
            else:
                self.dist = 0

    far_z = nz // 2

    def b_add(index, layer, side, slot_at):
        add_into(xg, [2 + index, layer, None], zb.at[side, slot_at, index], ny)

    def a_add(index, layer, side, slot_at):
        xg[index, layer, y] = xg[index, layer, y] + za[side, slot_at, index]

    def b_ring(side, index, dist):
        return Ring(lambda s, layer: xg.at[2 + s, layer], zb, side, index, b_add, dist)

    def a_ring(side, index, dist):
        return Ring(lambda s, layer: xg.at[s, layer, y], za, side, index, a_add, dist)

    keep_grad[0].wait()
    keep_grad[1].wait()
    b_rings = [b_ring(0, 0, far_z), b_ring(1, 1, far_z), b_ring(0, 1, far_z - 1), b_ring(1, 0, far_z - 1)]
    keep_grad[2].wait()
    keep_grad[3].wait()
    a_far = (send(xg.at[0, :, y2], ya.at[0], yp), send(xg.at[1, :, y2], ya.at[1], ym))
    a_near = [send(xg.at[1, :, y1], ya.at[2], yp), send(xg.at[0, :, y3], ya.at[3], ym)]

    def advance(rings):
        for ring in rings:
            ring.step()

    first.middle()
    second.start()
    advance(b_rings[:2])
    second.middle()
    first.along_y()
    received(a_far[0])
    add_into(xg, [0, None, y1], ya.at[0], nz)
    a_near.append(send(xg.at[0, :, y1], ya.at[4], yp))
    received(a_far[1])
    add_into(xg, [1, None, y3], ya.at[1], nz)
    a_near.append(send(xg.at[1, :, y3], ya.at[5], ym))
    advance(b_rings[2:])
    first.along_z()
    advance(b_rings[:2])
    second.along_y()
    first.total()
    advance(b_rings[2:])
    second.along_z()
    first.back_y()
    advance(b_rings[:2])
    second.total()
    first.back_x()
    advance(b_rings[2:])
    second.back_y()
    received(a_near[2], a_near[1])

    @pl.loop(0, nz)
    def _(i):
        xg[0, i, y] = xg[0, i, y] + ya[4, i] + ya[3, i]

    a_rings = [a_ring(0, 0, far_z), None, None, a_ring(1, 0, far_z - 1)]
    received(a_near[0], a_near[3])

    @pl.loop(0, nz)
    def _(i):
        xg[1, i, y] = xg[1, i, y] + ya[2, i] + ya[5, i]

    a_rings[1:3] = [a_ring(1, 1, far_z), a_ring(0, 1, far_z - 1)]
    second.back_x()
    advance(b_rings[:2])
    b2_far = (send(xg.at[2, z, y2], yb.at[0], yp), send(xg.at[3, z, y2], yb.at[1], ym))
    b2_near = [send(xg.at[3, z, y1], yb.at[2], yp), send(xg.at[2, z, y3], yb.at[3], ym)]
    first.back_far()
    advance(a_rings)
    received(b2_far[0])
    xg[2, z, y1] = xg[2, z, y1] + yb[0]
    b2_near.append(send(xg.at[2, z, y1], yb.at[4], yp))
    received(b2_far[1])
    xg[3, z, y3] = xg[3, z, y3] + yb[1]
    b2_near.append(send(xg.at[3, z, y3], yb.at[5], ym))
    advance(a_rings)
    second.back_far()
    advance(a_rings)
    first.finish()
    received(*b2_near)
    xg[2, z, y] = xg[2, z, y] + yb[4] + yb[3]
    xg[3, z, y] = xg[3, z, y] + yb[2] + yb[5]
    advance(a_rings)
    units = grad_o.shape[1]
    theirs = pl.ds(pl.multiple_of((1 - c) * units, 8), units)
    swap = send(xg.at[:, z, y, theirs], grad_o.at[pl.ds(c * 4, 4)], sib)
    for s in range(4):
        grad_o[c * 4 + s] = xg[s, z, y, pl.ds(pl.multiple_of(c * units, 8), units)]
    second.finish()
    received(swap, *from_sib)
    wires.drain()


def reduce_all(ny, nz, nx, grad, comp):
    slots, _, _, units, blk = grad.shape
    piece = comp.shape[3:]
    any_spec = pl.BlockSpec(memory_space=pl.ANY)
    vmem = pl.BlockSpec(memory_space=pltpu.VMEM)
    copies = 128
    return pl.pallas_call(
        functools.partial(reduce_kernel, ny, nz, nx),
        in_specs=[any_spec] * 2,
        out_specs=[vmem, vmem],
        out_shape=(
            jax.ShapeDtypeStruct((2 * slots, units // 2, blk), F32),
            jax.ShapeDtypeStruct((nz, ny, 2, nx) + piece, F32),
        ),
        scratch_shapes=[
            pltpu.VMEM(grad.shape, F32),
            pltpu.VMEM(comp.shape, F32),
            pltpu.VMEM((6, nz, units, blk), F32),
            pltpu.VMEM((2, nz // 2, 2, units, blk), F32),
            pltpu.VMEM((2, nz // 2, 2, ny, units, blk), F32),
            pltpu.VMEM((6, units, blk), F32),
            pltpu.VMEM((4, nz, ny) + piece, F32),
            pltpu.VMEM((ny - 1, nz) + piece, F32),
            pltpu.VMEM((nz - 1,) + piece, F32),
            pltpu.SemaphoreType.DMA((copies,)),
            pltpu.SemaphoreType.DMA((copies,)),
            pltpu.SemaphoreType.DMA((5,)),
        ],
        compiler_params=pltpu.CompilerParams(
            collective_id=2, has_side_effects=True, vmem_limit_bytes=48 * MIB
        ),
        cost_estimate=pl.CostEstimate(flops=0, bytes_accessed=100_000_000, transcendentals=0),
        name="reduce",
    )(grad, comp)


def identity(n):
    rows = lax.broadcasted_iota(jnp.int32, (n, n), 0)
    cols = lax.broadcasted_iota(jnp.int32, (n, n), 1)
    return jnp.where(rows == cols, 1.0, 0.0).astype(F32)


def mul(left, right):
    return exact_dot(left, right, ((1,), (0,)))


def spd_inverse(mat, start, eye):
    def unfinished(state):
        count, previous, residual, _ = state
        return (count < 100) & (residual > 1e-5) & ((residual < 0.5 * previous) | (residual > 0.1))

    def body(state):
        count, _, residual, guess = state
        gap = eye - mul(mat, guess)
        guess = guess + mul(guess, gap)
        return count + 1, residual, jnp.sqrt(jnp.sum(gap * gap)), guess

    state = lax.while_loop(unfinished, body, (0, jnp.float32(64.0), jnp.float32(32.0), start))
    return state[3]


def mixing_of(gram):
    n = gram.shape[0]
    eye = identity(n)
    shifted = gram + EPS * eye
    total = jnp.sum(jnp.sum(shifted * shifted, axis=1, keepdims=True), axis=0, keepdims=True)
    frob = jnp.sqrt(total)
    root = shifted / frob
    middle = 1.5 * eye - 0.5 * root
    root = mul(root, middle)
    inverse = middle
    for _ in range(NS_STEPS - 1):
        middle = 1.5 * eye - 0.5 * mul(inverse, root)
        root = mul(root, middle)
        inverse = mul(middle, inverse)
    half = 0.5 * jnp.sqrt(frob) * (root + root.T) + math.sqrt(EPS) * eye
    near = inverse / jnp.sqrt(frob)
    norm = jnp.max(jnp.sum(jnp.abs(near), axis=1, keepdims=True))
    shift = math.sqrt(EPS)
    start = near * (1.0 / (1.0 + 0.5 * jnp.minimum(shift * norm, 1.0)))
    half_inv = spd_inverse(half, start, eye)
    return -mul(inverse, half_inv) / (math.sqrt(EPS) * jnp.sqrt(frob))


def finish_kernel(
    row_ref, pat_ref, grad_ref, sketch_hbm, comp_hbm, out_ref, gram_ref, sel_ref, sketch_ref, comp_ref, sems
):
    slots, rows, blk = grad_ref.shape
    width, rank = comp_ref.shape
    parts = sems.shape[1]
    chunk = width // parts

    def load(i):
        at = pl.ds(i * chunk, chunk)
        return (
            pltpu.make_async_copy(sketch_hbm.at[at], sketch_ref.at[at], sems.at[0, i]),
            pltpu.make_async_copy(comp_hbm.at[at], comp_ref.at[at], sems.at[1, i]),
        )

    loads = [load(i) for i in range(parts)]
    for pair in loads:
        for copy in pair:
            copy.start()
    gram_ref[...] = jnp.zeros_like(gram_ref)
    for i in range(parts):
        for copy in loads[i]:
            copy.wait()
        at = pl.ds(i * chunk, chunk)
        st = jnp.concatenate([sketch_ref[at, :], comp_ref[at, :]], axis=1)
        high, low = split_bf16(st)
        dims = (((0,), (0,)), ((), ()))
        gram_ref[0] += lax.dot_general(high, high, dims, preferred_element_type=F32)
        gram_ref[1] += lax.dot_general(high, low, dims, preferred_element_type=F32)

    cross = gram_ref[1]
    mixing = mixing_of(gram_ref[0] + (cross + cross.T))
    start = row_ref[0]
    first = lax.div(start, blk)
    last = pat_ref.shape[0] - 1
    grad = jnp.concatenate([grad_ref[k] for k in range(slots)], axis=1)
    block_of = lax.div(start + lax.broadcasted_iota(jnp.int32, (rows, 1), 0), blk)
    projected = None
    for g in range(2):
        brow = jnp.minimum(first + g, last)
        for k in range(slots):
            col = pl.multiple_of(pat_ref[brow, k] * blk, blk)
            here = pl.ds(k * blk, blk)
            sel_ref[g, here, :rank] = sketch_ref[pl.ds(col, blk), :]
            sel_ref[g, here, rank:] = comp_ref[pl.ds(col, blk), :]
        part = mul(grad, sel_ref[g])
        projected = part if projected is None else jnp.where(block_of == first + g, part, projected)
    mixed = mul(projected, mixing)
    corr = exact_dot(mixed, sel_ref[0], ((1,), (1,)))
    corr1 = exact_dot(mixed, sel_ref[1], ((1,), (1,)))
    corr = jnp.where(block_of == first + 1, corr1, corr)
    result = grad * (1.0 / math.sqrt(EPS)) + corr
    for k in range(slots):
        out_ref[:, k, :] = result[:, k * blk : (k + 1) * blk]


def finish(start_row, pattern, grad, sketch_t, comp_t):
    slots, rows, blk = grad.shape
    rank = comp_t.shape[1]
    smem = pl.BlockSpec(memory_space=pltpu.SMEM)
    vmem = pl.BlockSpec(memory_space=pltpu.VMEM)
    return pl.pallas_call(
        finish_kernel,
        in_specs=[smem, smem, vmem] + [pl.BlockSpec(memory_space=pl.ANY)] * 2,
        out_specs=vmem,
        out_shape=jax.ShapeDtypeStruct((rows, slots, blk), F32),
        scratch_shapes=[
            pltpu.VMEM((2, 2 * rank, 2 * rank), F32),
            pltpu.VMEM((2, slots * blk, 2 * rank), F32),
            pltpu.VMEM(sketch_t.shape, F32),
            pltpu.VMEM(comp_t.shape, F32),
            pltpu.SemaphoreType.DMA((2, 8)),
        ],
        compiler_params=pltpu.CompilerParams(vmem_limit_bytes=60 * MIB),
        cost_estimate=pl.CostEstimate(flops=5_000_000_000, bytes_accessed=9_000_000, transcendentals=0),
        name="finish",
    )(start_row, pattern, grad, sketch_t, comp_t)


def per_device(weights, hidden, cotangent, sketch, projection, pattern):
    rank = sketch.shape[0]
    slots, blk = weights.shape[1:]
    dp_size = lax.axis_size("dp")
    nx = lax.axis_size("mp")
    ny = 4
    nz = dp_size // (2 * ny)
    dev_rows = weights.shape[0] // dp_size
    all_tokens = hidden.shape[0] * dp_size
    dp = lax.axis_index("dp")
    core = lax.rem(dp, 2).reshape(1).astype(jnp.int32)
    cot, hid, proj, sketch_t = gather(
        ny, nz, nx, cotangent, hidden, projection.reshape(rank, dev_rows).T, sketch.T
    )
    cot = cot.reshape(nx, -1, cotangent.shape[1])
    hid = hid.reshape(-1, hidden.shape[1])
    input_grad, grad, comp = local_step(
        core, pattern, cot, hid, weights, proj.reshape(-1, rank), all_tokens
    )
    grad, comp = reduce_all(
        ny, nz, nx, grad.reshape(slots // 2, nz, ny, 2 * dev_rows, blk), comp.reshape(nz, ny, nx, -1, rank)
    )
    start_row = (dp * dev_rows).reshape(1).astype(jnp.int32)
    direction = finish(start_row, pattern, grad, sketch_t.reshape(-1, rank), comp.reshape(-1, rank))
    return input_grad, direction[None]


def solution(mesh):
    return jax.shard_map(
        per_device,
        mesh=mesh,
        in_specs=(
            P("mp", None, None),
            P("dp", "mp"),
            P("dp", "mp"),
            P(None, ("dp", "mp")),
            P(None, "mp", "dp"),
            P("mp", None),
        ),
        out_specs=(P("dp", "mp"), P("mp", "dp", None, None)),
        check_vma=False,
    )
```
